32 devices in a mesh: tiles: 2 (over y), strip: 4 (over z), col: 2 (over x), expo: 2 (over core).
Axes of the slice: x: 2, y: 2, z: 4, core: 2. Of those that a mesh axis runs over, the one named last changes fastest.
Arguments:
- mask_params: float32 [2, 2048, 256], P('expo', ('tiles', 'strip'), 'col'), parts along dimension 1, may hold values from -3 to 3
- target: int32 [2048, 256], P(('tiles', 'strip'), 'col'), parts along dimension 0, may hold values from 0 to 1, as said below
- col_taps: bfloat16 [24, 2, 65], replicated, may hold values from -0.75 to 0.75
- row_taps: bfloat16 [24, 2, 65], replicated, may hold values from -0.75 to 0.75
- kernel_weights: float32 [24], replicated, may hold values from 0.05 to 0.5
Outputs:
- new_params: float32 [2, 2048, 256], P('expo', ('tiles', 'strip'), 'col'), parts along dimension 1
- resist: float32 [2048, 256], P(('tiles', 'strip'), 'col'), parts along dimension 0
- mean_loss: float32 [2], P('tiles'), parts along dimension 0
The draws below stay inside these ranges and needn't reach their ends.
There are 2 independent parts, one for each index of `tiles`. The reference program is written for one: setup_inputs(seed, part) draws one part's arguments, and reference() takes and returns one part's arrays. A program takes and returns all parts, laid end to end along the dimension named above; an argument that names none is the same for every part. Nothing has to cross between parts.
Inputs may be any that keep to these rules, and one draw needn't show every extreme that they name: `target`: 1 where the layout is printed, 0 elsewhere.
All inputs are finite; a program needn't handle non-finite values.
Results may differ from the reference program's by a relative error of at most 0.0078.
Values may be sent and summed in bfloat16 or wider, within the bound.
No kernel may reach another device: no remote copies, remote signals or barrier semaphores. Data moves between devices by JAX's collectives and lax.ppermute only.
A program may use at most 64 MiB of HBM per device.

```python
import math
import jax
import jax.numpy as jnp
from jax import lax

TAPS = 65
KERNELS = 24
EXPOSURES = 2
HALF = 32
HEIGHT = 1024
WIDTH = 256


def draw_target(key, part):
    row_ids = jnp.arange(HEIGHT, dtype=jnp.int32)[:, None]
    level = 150 + 600 * row_ids // HEIGHT
    votes = jax.random.randint(key, (HEIGHT, WIDTH), 0, 1000, dtype=jnp.int32)
    return jnp.where(votes < level, 1, 0).astype(jnp.int32)


def levels(own_key, dims, shards, low, largest):
    gain, own = 1.0, jax.random.fold_in(own_key, 6)
    for dim, blocks in shards:
        steps = jnp.exp(jax.random.uniform(jax.random.fold_in(own, dim), (blocks,), jnp.float32, low / len(shards), largest / len(shards)))
        gain = gain * jnp.repeat(steps, dims[dim] // blocks).reshape([-1 if axis == dim else 1 for axis in range(len(dims))])
    return gain


def noise(rng, shape, deviation, most, cuts=(), held_as=jnp.bfloat16):
    drawn = deviation * jax.random.normal(rng, shape, jnp.float32)
    if cuts:
        drawn = drawn * levels(rng, shape, cuts, -0.22, 0.18)
    return jnp.clip(drawn, -most, most).astype(held_as)


def setup_inputs(seed: int = 0, part: int = 0) -> dict:
    key_list = jax.random.split(jax.random.key(seed), 6)
    own_keys = jax.random.split(jax.random.fold_in(key_list[5], part), 6)
    return {
        "mask_params": noise(own_keys[0], (EXPOSURES, HEIGHT, WIDTH), 0.5, 3.0, ((0, 2), (1, 4), (2, 2)), jnp.float32),
        "target": draw_target(jax.random.fold_in(jax.random.fold_in(key_list[5], part), 71), part),
        "col_taps": noise(key_list[2], (KERNELS, 2, TAPS), TAPS ** -0.5, 0.75),
        "row_taps": noise(key_list[3], (KERNELS, 2, TAPS), TAPS ** -0.5, 0.75),
        "kernel_weights": jnp.clip(jnp.exp(jax.random.uniform(key_list[4], (KERNELS,), jnp.float32, math.log(0.05), math.log(0.5))), 0.05, 0.5),
    }


mask_slope = 4.0
resist_steep = 4.0
resist_level = 3.0
step_length = 0.5
norm_eps = 1e-06

def conv_plane(source, kernel, pad_rows, pad_cols):
    return lax.conv_general_dilated(source.astype(jnp.float32), kernel.astype(jnp.float32), (1, 1), ((pad_rows, pad_rows), (pad_cols, pad_cols)), dimension_numbers=('NCHW', 'OIHW', 'NCHW'), precision=lax.Precision.HIGHEST)

def kernel_fields(mask_half, col_pair, row_pair):
    columns = conv_plane(mask_half, col_pair[:, None, None, :], 0, HALF).astype(jnp.bfloat16)
    height, width = (columns.shape[2], columns.shape[3])
    stacked = columns.reshape(columns.shape[0] * 2, 1, height, width)
    pair_sums = conv_plane(stacked, row_pair[:, None, :, None], HALF, 0).reshape(columns.shape[0], 2, 2, height, width)
    real_part = pair_sums[:, 0, 0] - pair_sums[:, 1, 1]
    imag_part = pair_sums[:, 0, 1] + pair_sums[:, 1, 0]
    return (real_part, imag_part)

def reference(mask_params, target, col_taps, row_taps, kernel_weights):
    mask_field = jax.nn.sigmoid(mask_slope * mask_params)
    mask_half = mask_field.astype(jnp.bfloat16)[:, None]
    kernel_ids = jnp.arange(KERNELS, dtype=jnp.int32)

    def add_intensity(running, kernel):
        real_part, imag_part = kernel_fields(mask_half, col_taps[kernel], row_taps[kernel])
        return (running + kernel_weights[kernel] * (real_part * real_part + imag_part * imag_part), None)
    intensity, unused = lax.scan(add_intensity, jnp.zeros(mask_params.shape, jnp.float32), kernel_ids)
    summed = intensity[0] + intensity[1]
    resist = jax.nn.sigmoid(resist_steep * (summed - resist_level))
    mismatch = resist - target.astype(jnp.float32)
    mean_loss = jnp.mean(mismatch * mismatch).reshape(1)
    slope_field = 2.0 * mismatch * resist_steep * resist * (1.0 - resist)
    height, width = target.shape

    def add_gradient(running, kernel):
        col_pair = col_taps[kernel]
        row_pair = row_taps[kernel]
        real_part, imag_part = kernel_fields(mask_half, col_pair, row_pair)
        weighting = 2.0 * kernel_weights[kernel] * slope_field
        products = jnp.stack([weighting * real_part, weighting * imag_part], axis=1).astype(jnp.bfloat16)
        returned = conv_plane(products.reshape(-1, 1, height, width), row_pair[:, ::-1][:, None, :, None], HALF, 0)
        returned = returned.reshape(products.shape[0], 2, 2, height, width)
        unrolled = jnp.stack([returned[:, 0, 0] + returned[:, 1, 1], returned[:, 1, 0] - returned[:, 0, 1]], axis=1).astype(jnp.bfloat16)
        term = conv_plane(unrolled, col_pair[:, ::-1][None, :, None, :], 0, HALF)[:, 0]
        return (running + term, None)
    descent, unused = lax.scan(add_gradient, jnp.zeros(mask_params.shape, jnp.float32), kernel_ids)
    gradient = descent * mask_slope * mask_field * (1.0 - mask_field)
    root_mean = jnp.sqrt(jnp.mean(gradient * gradient) + norm_eps)
    new_params = mask_params - step_length * gradient / root_mean
    return (new_params, resist, mean_loss)
```

```python
import functools
import jax
import jax.numpy as jnp
from jax import lax
from jax.experimental import pallas as pl
from jax.experimental.pallas import tpu as pltpu
from jax.sharding import PartitionSpec as P

HALF = 32
LANES = 128
UNROLL = 4

mask_slope = 4.0
resist_steep = 4.0
resist_level = 3.0
step_length = 0.5
norm_eps = 1e-06

BF16 = jnp.bfloat16
F32 = jnp.float32


def neighbours(axis, to_next, to_previous):
    peers = lax.axis_size(axis)
    if peers == 1:
        return jnp.zeros_like(to_next), jnp.zeros_like(to_previous)
    if peers == 2:
        first = lax.axis_index(axis) == 0
        got = lax.ppermute(jnp.where(first, to_next, to_previous), axis, [(0, 1), (1, 0)])
        nothing = jnp.zeros_like(got)
        return jnp.where(first, nothing, got), jnp.where(first, got, nothing)
    up = [(i, i + 1) for i in range(peers - 1)]
    down = [(j, i) for i, j in up]
    return lax.ppermute(to_next, axis, up), lax.ppermute(to_previous, axis, down)


def total_over(value, axis):
    peers = lax.axis_size(axis)
    if peers & (peers - 1):
        return lax.psum(value, axis)
    reach = 1
    while reach < peers:
        value = value + lax.ppermute(value, axis, [(i, i ^ reach) for i in range(peers)])
        reach *= 2
    return value


def circulant(row, shift):
    spread = jnp.broadcast_to(row, (LANES, LANES))
    return pltpu.roll(spread, shift, 1, stride=1, stride_axis=0)


def index_pair(shape):
    return lax.broadcasted_iota(jnp.int32, shape, 0), lax.broadcasted_iota(jnp.int32, shape, 1)


def assemble_kernel(mask_ref, up_ref, down_ref, code_ref, centre_ref, code_out_ref, right_ref, left_ref):
    rows, cols = mask_ref.shape
    wide = 2 * HALF
    tall = jnp.concatenate([up_ref[0:wide, :], mask_ref[...], down_ref[0:wide, :]], axis=0)
    turned = tall.astype(F32).T.astype(BF16)
    code = jnp.concatenate(
        [up_ref[wide:, :], code_ref[...], down_ref[wide:, :], jnp.zeros((wide, cols), BF16)], axis=0
    )
    code = code.astype(F32).T.astype(BF16)
    centre_ref[...] = turned
    code_out_ref[...] = code
    right_ref[0:wide, :] = turned[cols - wide :, :]
    right_ref[wide:, :] = code[cols - HALF :, :]
    left_ref[0:wide, :] = turned[0:wide, :]
    left_ref[wide:, :] = code[0:HALF, :]


def forward_kernel(
    weights_ref, centre_ref, before_ref, after_ref, taps_ref, field_ref, intensity_ref, mask_ref, total_ref
):
    step = pl.program_id(0)
    cols = centre_ref.shape[0]
    wide = 2 * HALF
    tiles = centre_ref.shape[1] // LANES
    span = cols + wide

    @pl.when(step == 0)
    def _():
        mask_ref[0:wide, :] = before_ref[0:wide, :]
        mask_ref[wide : wide + cols, :] = centre_ref[...]
        mask_ref[wide + cols :, :] = after_ref[0:wide, :]
        total_ref[...] = jnp.zeros_like(total_ref)

    a, b = index_pair((LANES, LANES))
    upper, lower = b >= a, a >= b
    zero = jnp.zeros((LANES, LANES), F32)
    for unit in range(UNROLL):
        weight = weights_ref[step * UNROLL + unit]
        stack = []
        for part in range(2):
            base = circulant(taps_ref[unit, part : part + 1, :], 0)
            near = jnp.where(upper, base, zero).astype(BF16)
            far = jnp.where(upper, zero, base).astype(BF16)
            stack.append(jnp.concatenate([near, far], axis=1))
            stack.append(jnp.concatenate([jnp.zeros((wide, LANES), BF16), near[0:wide]], axis=1))
        table = jnp.concatenate(stack, axis=0)
        columns = jnp.dot(table, mask_ref[...], preferred_element_type=F32).astype(BF16)
        near, far = [], []
        for part in range(2):
            base = circulant(taps_ref[unit, 2 + part : 3 + part, :], LANES // 2)
            near.append(jnp.where(lower, base, zero).astype(BF16))
            far.append(jnp.where(lower, zero, base).astype(BF16))
        table = jnp.concatenate(
            [
                jnp.concatenate([near[0], near[1]], axis=1),
                jnp.concatenate([-near[1], near[0]], axis=1),
                jnp.concatenate([far[0], far[1]], axis=1),
                jnp.concatenate([-far[1], far[0]], axis=1),
            ],
            axis=0,
        )
        pieces = [
            jnp.concatenate(
                [columns[part * span : (part + 1) * span, t * LANES : (t + 1) * LANES] for part in range(2)],
                axis=1,
            )
            for t in range(tiles)
        ]
        for t in range(tiles):
            if t + 1 < tiles:
                window = jnp.concatenate([pieces[t], pieces[t + 1]], axis=1)
                field = jnp.dot(window, table, preferred_element_type=F32)
            else:
                field = jnp.dot(pieces[t], table[0 : 2 * LANES], preferred_element_type=F32)
            field_ref[unit, t] = field.astype(field_ref.dtype)
            total_ref[t] += weight * (field * field)

    @pl.when(step == pl.num_programs(0) - 1)
    def _():
        for t in range(tiles):
            intensity_ref[t] = total_ref[t, :, 0:LANES] + total_ref[t, :, LANES:]


def backward_kernel(
    weights_ref,
    own_ref,
    other_ref,
    code_ref,
    code_before_ref,
    code_after_ref,
    params_ref,
    field_ref,
    taps_ref,
    gradient_ref,
    resist_ref,
    sums_ref,
    slope_ref,
    descent_ref,
    resist_all_ref,
    mismatch_ref,
):
    step = pl.program_id(0)
    cols = code_ref.shape[0]
    wide = 2 * HALF
    tiles = own_ref.shape[0]
    rows = (tiles - 1) * LANES

    @pl.when(step == 0)
    def _():
        for t in range(tiles):
            lanes = slice(t * LANES, (t + 1) * LANES)
            code = jnp.concatenate(
                [code_before_ref[wide:, lanes], code_ref[:, lanes], code_after_ref[wide:, lanes]], axis=0
            ).astype(F32)
            summed = own_ref[t] + other_ref[t]
            resist = jax.nn.sigmoid(resist_steep * (summed - resist_level))
            mismatch = resist - (code - 1.0)
            slope = 2.0 * mismatch * resist_steep * resist * (1.0 - resist)
            slope = jnp.where(code > 0.5, slope, 0.0)
            slope_ref[t, :, 0:LANES] = slope
            slope_ref[t, :, LANES:] = slope
            resist_all_ref[:, lanes] = resist[HALF : HALF + cols]
            mismatch_ref[:, lanes] = mismatch[HALF : HALF + cols]
        descent_ref[...] = jnp.zeros_like(descent_ref)

    a, b = index_pair((LANES, LANES))
    upper, lower = b >= a, a >= b
    zero = jnp.zeros((LANES, LANES), F32)
    for unit in range(UNROLL):
        weight = 2.0 * weights_ref[step * UNROLL + unit]
        near, far = [], []
        for part in range(2):
            base = circulant(taps_ref[unit, 2 + part : 3 + part, :], LANES // 2)
            near.append(jnp.where(lower, base, zero).astype(BF16))
            far.append(jnp.where(lower, zero, base).astype(BF16))
        table = jnp.concatenate(
            [
                jnp.concatenate([near[0], -near[1]], axis=1),
                jnp.concatenate([near[1], near[0]], axis=1),
                jnp.concatenate([far[0], -far[1]], axis=1),
                jnp.concatenate([far[1], far[0]], axis=1),
            ],
            axis=0,
        )
        products = [
            ((weight * slope_ref[t]) * field_ref[unit, t].astype(F32)).astype(BF16) for t in range(tiles)
        ]
        returned = []
        for t in range(tiles - 1):
            window = jnp.concatenate([products[t], products[t + 1]], axis=1)
            returned.append(jnp.dot(window, table, preferred_element_type=F32).astype(BF16))
        split = [
            jnp.concatenate([r[:, part * LANES : (part + 1) * LANES] for r in returned], axis=1)
            for part in range(2)
        ]
        near, far = [], []
        for part in range(2):
            base = circulant(taps_ref[unit, part : part + 1, :], 0)
            near.append(jnp.where(upper, base, zero).astype(BF16))
            far.append(jnp.where(upper, zero, base))
        joined = jnp.where(b < wide, far[0], pltpu.roll(far[1], wide, 1)).astype(BF16)
        table = jnp.concatenate([near[0], near[1], joined], axis=1)
        source = jnp.concatenate([split[0][0:cols], split[1][0:cols], split[0][cols:], split[1][cols:]], axis=0)
        descent_ref[...] += jnp.dot(table, source, preferred_element_type=F32)

    @pl.when(step == pl.num_programs(0) - 1)
    def _():
        mask = jax.nn.sigmoid(mask_slope * params_ref[...])
        gradient = descent_ref[...].T * mask_slope * mask * (1.0 - mask)
        gradient_ref[...] = gradient
        resist_ref[...] = resist_all_ref[...].T[HALF : HALF + rows]
        a, b = index_pair(mismatch_ref.shape)
        mismatch = jnp.where((b >= HALF) & (b < HALF + rows), mismatch_ref[...], 0.0)
        squares = jnp.sum(gradient * gradient, axis=0, keepdims=True)
        loss = jnp.sum(mismatch * mismatch)
        sums_ref[0:1, :] = jnp.broadcast_to(jnp.sum(squares), (1, LANES))
        sums_ref[1:2, :] = jnp.broadcast_to(loss, (1, LANES))


def whole(shape):
    return pl.BlockSpec(shape, lambda *_: (0,) * len(shape))


def shards(mask_params, target, col_taps, row_taps, kernel_weights):
    rows, cols = target.shape
    kernels, _, taps = col_taps.shape
    wide = 2 * HALF
    tiles = rows // LANES + 1
    long, span = tiles * LANES, cols + wide
    if cols != LANES or rows % LANES or taps != wide + 1 or kernels % UNROLL:
        raise ValueError("block shape")
    params = mask_params[0]
    mask_half = jax.nn.sigmoid(mask_slope * params).astype(BF16)
    code = (target + 1).astype(BF16)
    strip_up, strip_down = neighbours(
        "strip",
        jnp.concatenate([mask_half[rows - wide :], code[rows - HALF :]], axis=0),
        jnp.concatenate([mask_half[:wide], code[:HALF]], axis=0),
    )
    side = jax.ShapeDtypeStruct((wide + HALF, long), BF16)
    turned = jax.ShapeDtypeStruct((cols, long), BF16)
    centre, code_turned, to_right, to_left = pl.pallas_call(
        assemble_kernel, out_shape=(turned, turned, side, side), name="assemble"
    )(mask_half, strip_up, strip_down, code)
    before, after = neighbours("col", to_right, to_left)

    pad = ((0, 0), (0, 0), (0, LANES - taps))
    col_plain, row_plain = jnp.pad(col_taps, pad), jnp.pad(row_taps, pad)
    col_turned, row_turned = jnp.pad(col_taps[..., ::-1], pad), jnp.pad(row_taps[..., ::-1], pad)
    forward_taps = jnp.concatenate([col_plain, row_turned], axis=1).astype(F32)
    backward_taps = jnp.concatenate([col_turned, row_plain], axis=1).astype(F32)

    smem = pl.BlockSpec(memory_space=pltpu.SMEM)
    taps_spec = pl.BlockSpec((UNROLL, 4, LANES), lambda k: (k, 0, 0))
    field_spec = pl.BlockSpec((UNROLL, tiles, span, 2 * LANES), lambda k: (k, 0, 0, 0))
    plane = (tiles, span, LANES)
    field, intensity = pl.pallas_call(
        forward_kernel,
        grid=(kernels // UNROLL,),
        in_specs=[smem, whole((cols, long)), whole((wide + HALF, long)), whole((wide + HALF, long)), taps_spec],
        out_specs=[field_spec, whole(plane)],
        out_shape=(
            jax.ShapeDtypeStruct((kernels, tiles, span, 2 * LANES), BF16),
            jax.ShapeDtypeStruct(plane, F32),
        ),
        scratch_shapes=[
            pltpu.VMEM((cols + 2 * wide, long), BF16),
            pltpu.VMEM((tiles, span, 2 * LANES), F32),
        ],
        name="forward",
    )(kernel_weights, centre, before, after, forward_taps)

    exposures = lax.axis_size("expo")
    other = lax.ppermute(intensity, "expo", [(i, (i + 1) % exposures) for i in range(exposures)])

    gradient, resist, sums = pl.pallas_call(
        backward_kernel,
        grid=(kernels // UNROLL,),
        in_specs=[
            smem,
            whole(plane),
            whole(plane),
            whole((cols, long)),
            whole((wide + HALF, long)),
            whole((wide + HALF, long)),
            whole((rows, cols)),
            field_spec,
            taps_spec,
        ],
        out_specs=[whole((rows, cols)), whole((rows, cols)), whole((2, LANES))],
        out_shape=(
            jax.ShapeDtypeStruct((rows, cols), F32),
            jax.ShapeDtypeStruct((rows, cols), F32),
            jax.ShapeDtypeStruct((2, LANES), F32),
        ),
        scratch_shapes=[
            pltpu.VMEM((tiles, span, 2 * LANES), F32),
            pltpu.VMEM((cols, rows), F32),
            pltpu.VMEM((cols, long), F32),
            pltpu.VMEM((cols, long), F32),
        ],
        name="backward",
    )(kernel_weights, intensity, other, code_turned, before, after, params, field, backward_taps)

    for axis in ("expo", "col", "strip"):
        sums = total_over(sums, axis)
    pixels = rows * cols * lax.axis_size("strip") * lax.axis_size("col")
    count = exposures * pixels
    root_mean = jnp.sqrt(sums[0, 0] / count + norm_eps)
    new_params = mask_params - step_length * gradient[None] / root_mean
    mean_loss = sums[1, 0:1] / count
    return (new_params, resist, mean_loss)


def solution(mesh):
    if mesh.shape["expo"] != 2:
        raise ValueError("two exposures")
    return jax.shard_map(
        shards,
        mesh=mesh,
        in_specs=(
            P("expo", ("tiles", "strip"), "col"),
            P(("tiles", "strip"), "col"),
            P(),
            P(),
            P(),
        ),
        out_specs=(P("expo", ("tiles", "strip"), "col"), P(("tiles", "strip"), "col"), P("tiles")),
        check_vma=False,
    )
```

```python
import functools
import jax
import jax.numpy as jnp
from jax import lax
from jax.experimental import pallas as pl
from jax.experimental.pallas import tpu as pltpu
from jax.sharding import PartitionSpec as P

HALF = 32
LANES = 128
FORWARD_UNROLL = 8
BACKWARD_UNROLL = 8
VMEM = 26 * 2**20

mask_slope = 4.0
resist_steep = 4.0
resist_level = 3.0
step_length = 0.5
norm_eps = 1e-06

BF16 = jnp.bfloat16
F32 = jnp.float32


def total_over(value, axis):
    peers = lax.axis_size(axis)
    if peers & (peers - 1):
        return lax.psum(value, axis)
    reach = 1
    while reach < peers:
        value = value + lax.ppermute(value, axis, [(i, i ^ reach) for i in range(peers)])
        reach *= 2
    return value


def circulant(row, shift):
    spread = jnp.broadcast_to(row, (LANES, LANES))
    return pltpu.roll(spread, shift, 1, stride=1, stride_axis=0).astype(BF16)


def index_pair(shape):
    return lax.broadcasted_iota(jnp.int32, shape, 0), lax.broadcasted_iota(jnp.int32, shape, 1)


def write_masks(masks_ref):
    a, b = index_pair((LANES, LANES))
    one, zero = jnp.ones((LANES, LANES), F32), jnp.zeros((LANES, LANES), F32)
    for slot, keep in enumerate((b >= a, b < a, a >= b, a < b)):
        masks_ref[slot] = jnp.where(keep, one, zero).astype(BF16)


def taps_kernel(col_ref, row_ref, out_ref):
    kernels, _, taps = col_ref.shape
    t, l = index_pair((taps, 2 * LANES))
    pick = jnp.where((l == t) | (l == LANES + taps - 1 - t), 1.0, 0.0).astype(BF16)
    for k in range(kernels):
        both = jnp.concatenate([col_ref[k].astype(F32), row_ref[k].astype(F32)], axis=0).astype(BF16)
        out_ref[k] = jnp.dot(both, pick, preferred_element_type=F32)


def prepare_kernel(params_ref, target_ref, mask_ref, code_ref, down_ref, up_ref):
    rows = params_ref.shape[0]
    wide = 2 * HALF
    mask = jax.nn.sigmoid(mask_slope * params_ref[...]).astype(BF16)
    code = (target_ref[...] + 1).astype(F32).astype(BF16)
    mask_ref[...] = mask
    code_ref[...] = code
    down_ref[0:wide, :] = mask[rows - wide :]
    down_ref[wide:, :] = code[rows - HALF :]
    up_ref[0:wide, :] = mask[0:wide]
    up_ref[wide:, :] = code[0:HALF]


def assemble_kernel(first_ref, mask_ref, code_ref, up_ref, down_ref, centre_ref, code_out_ref, *side_refs):
    rows, cols = mask_ref.shape
    wide = 2 * HALF
    tall = jnp.concatenate([up_ref[0:wide, :], mask_ref[...], down_ref[0:wide, :]], axis=0)
    turned = tall.astype(F32).T.astype(BF16)
    code = jnp.concatenate(
        [up_ref[wide:, :], code_ref[...], down_ref[wide:, :], jnp.zeros((wide, cols), BF16)], axis=0
    )
    code = code.astype(F32).T.astype(BF16)
    centre_ref[...] = turned
    code_out_ref[...] = code

    def right(ref):
        ref[0:wide, :] = turned[cols - wide :, :]
        ref[wide:, :] = code[cols - HALF :, :]

    def left(ref):
        ref[0:wide, :] = turned[0:wide, :]
        ref[wide:, :] = code[0:HALF, :]

    if len(side_refs) == 2:
        right(side_refs[0])
        left(side_refs[1])
    else:
        pl.when(first_ref[0] == 1)(lambda: right(side_refs[0]))
        pl.when(first_ref[0] == 0)(lambda: left(side_refs[0]))


def forward_kernel(
    weights_ref,
    ends_ref,
    centre_ref,
    before_ref,
    after_ref,
    taps_ref,
    field_ref,
    intensity_ref,
    mask_ref,
    total_ref,
    masks_ref,
    table_ref,
    columns_ref,
):
    step = pl.program_id(0)
    units = taps_ref.shape[0]
    cols = centre_ref.shape[0]
    wide = 2 * HALF
    tiles = centre_ref.shape[1] // LANES
    span = cols + wide

    @pl.when(step == 0)
    def _():
        mask_ref[0:wide, :] = jnp.where(ends_ref[0] == 1, 0.0, before_ref[0:wide, :].astype(F32)).astype(BF16)
        mask_ref[wide : wide + cols, :] = centre_ref[...]
        mask_ref[wide + cols :, :] = jnp.where(ends_ref[1] == 1, 0.0, after_ref[0:wide, :].astype(F32)).astype(BF16)
        total_ref[...] = jnp.zeros_like(total_ref)
        write_masks(masks_ref)
        table_ref[...] = jnp.zeros_like(table_ref)

    for unit in range(units):
        for part in range(2):
            base = circulant(taps_ref[unit, part : part + 1, 0:LANES], 0)
            near, far = base * masks_ref[0], base * masks_ref[1]
            table_ref[unit, part, 0:LANES, 0:LANES] = near
            table_ref[unit, part, 0:LANES, LANES:] = far
            table_ref[unit, part, LANES:, LANES:] = near[0:wide]
    table = table_ref[...].reshape(units * 2 * span, cols + 2 * wide)
    columns = jnp.dot(table, mask_ref[...], preferred_element_type=F32).astype(BF16)
    for unit in range(units):
        for part in range(2):
            at = (unit * 2 + part) * span
            for t in range(tiles):
                columns_ref[unit, t * span : (t + 1) * span, part * LANES : (part + 1) * LANES] = columns[
                    at : at + span, t * LANES : (t + 1) * LANES
                ]
    for unit in range(units):
        weight = weights_ref[step * units + unit]
        near, far = [], []
        for part in range(2):
            base = circulant(taps_ref[unit, 2 + part : 3 + part, LANES:], LANES // 2)
            near.append(base * masks_ref[2])
            far.append(base * masks_ref[3])

        def joined(half):
            return jnp.concatenate(
                [jnp.concatenate([half[0], half[1]], axis=1), jnp.concatenate([-half[1], half[0]], axis=1)], axis=0
            )

        field = jnp.dot(columns_ref[unit], joined(near), preferred_element_type=F32)
        rest = jnp.dot(columns_ref[unit, span:, :], joined(far), preferred_element_type=F32)
        for t in range(tiles):
            part = field[t * span : (t + 1) * span]
            if t + 1 < tiles:
                part = part + rest[t * span : (t + 1) * span]
            scaled = weight * part
            field_ref[unit, t] = scaled.astype(field_ref.dtype)
            total_ref[t] += scaled * part

    @pl.when(step == pl.num_programs(0) - 1)
    def _():
        for t in range(tiles):
            intensity_ref[t] = total_ref[t, :, 0:LANES] + total_ref[t, :, LANES:]


def backward_kernel(
    ends_ref,
    own_ref,
    other_ref,
    code_ref,
    code_before_ref,
    code_after_ref,
    params_ref,
    field_ref,
    taps_ref,
    gradient_ref,
    resist_ref,
    sums_ref,
    slope_ref,
    descent_ref,
    resist_all_ref,
    mismatch_ref,
    masks_ref,
    table_ref,
    source_ref,
):
    step = pl.program_id(0)
    units = taps_ref.shape[0]
    cols = code_ref.shape[0]
    wide = 2 * HALF
    tiles = own_ref.shape[0]
    span = cols + wide
    rows = (tiles - 1) * LANES

    @pl.when(step == 0)
    def _():
        for t in range(tiles):
            lanes = slice(t * LANES, (t + 1) * LANES)
            code = jnp.concatenate(
                [
                    jnp.where(ends_ref[0] == 1, 0.0, code_before_ref[wide:, lanes].astype(F32)),
                    code_ref[:, lanes].astype(F32),
                    jnp.where(ends_ref[1] == 1, 0.0, code_after_ref[wide:, lanes].astype(F32)),
                ],
                axis=0,
            )
            summed = own_ref[t] + other_ref[t]
            resist = jax.nn.sigmoid(resist_steep * (summed - resist_level))
            mismatch = resist - (code - 1.0)
            slope = 4.0 * mismatch * resist_steep * resist * (1.0 - resist)
            slope_ref[t] = jnp.where(code > 0.5, slope, 0.0)
            resist_all_ref[:, lanes] = resist[HALF : HALF + cols]
            mismatch_ref[:, lanes] = mismatch[HALF : HALF + cols]
        descent_ref[...] = jnp.zeros_like(descent_ref)
        write_masks(masks_ref)

    _, b = index_pair((LANES, LANES))
    for unit in range(units):
        near, far = [], []
        for part in range(2):
            base = circulant(taps_ref[unit, 2 + part : 3 + part, 0:LANES], LANES // 2)
            near.append(base * masks_ref[2])
            far.append(base * masks_ref[3])
        table = jnp.concatenate(
            [
                jnp.concatenate([near[0], -near[1]], axis=1),
                jnp.concatenate([near[1], near[0]], axis=1),
                jnp.concatenate([far[0], -far[1]], axis=1),
                jnp.concatenate([far[1], far[0]], axis=1),
            ],
            axis=0,
        )
        products = []
        for t in range(tiles):
            slope = jnp.concatenate([slope_ref[t], slope_ref[t]], axis=1)
            products.append((slope * field_ref[unit, t].astype(F32)).astype(BF16))
        window = jnp.concatenate(
            [
                jnp.concatenate(products[:-1], axis=0),
                jnp.concatenate(products[1:], axis=0),
            ],
            axis=1,
        )
        returned = jnp.dot(window, table, preferred_element_type=F32).astype(BF16)
        at = unit * 2 * span
        for t in range(tiles - 1):
            to = slice(t * LANES, (t + 1) * LANES)
            for part in range(2):
                piece = returned[t * span : (t + 1) * span, part * LANES : (part + 1) * LANES]
                source_ref[at + part * cols : at + (part + 1) * cols, to] = piece[0:cols]
                tail = at + 2 * cols + part * wide
                source_ref[tail : tail + wide, to] = piece[cols:]
        for part in range(2):
            base = circulant(taps_ref[unit, part : part + 1, LANES:], 0)
            table_ref[:, at + part * LANES : at + (part + 1) * LANES] = base * masks_ref[0]
        spread = [
            jnp.broadcast_to(taps_ref[unit, part : part + 1, LANES:], (LANES, LANES)) for part in range(2)
        ]
        turned = [pltpu.roll(spread[part], part * wide, 1, stride=1, stride_axis=0) for part in range(2)]
        a, _ = index_pair((LANES, LANES))
        both = jnp.where(b < wide, turned[0], turned[1])
        inside = jnp.where(b < wide, b, b - wide) < a
        table_ref[:, at + 2 * LANES : at + 3 * LANES] = jnp.where(inside, both, 0.0).astype(BF16)
    descent_ref[...] += jnp.dot(table_ref[...], source_ref[...], preferred_element_type=F32)

    @pl.when(step == pl.num_programs(0) - 1)
    def _():
        mask = jax.nn.sigmoid(mask_slope * params_ref[...])
        gradient = descent_ref[...].T * mask_slope * mask * (1.0 - mask)
        gradient_ref[...] = gradient
        resist_ref[...] = resist_all_ref[...].T[HALF : HALF + rows]
        _, b = index_pair(mismatch_ref.shape)
        mismatch = jnp.where((b >= HALF) & (b < HALF + rows), mismatch_ref[...], 0.0)
        sums_ref[0:1, :] = jnp.broadcast_to(jnp.sum(gradient * gradient), (1, LANES))
        sums_ref[1:2, :] = jnp.broadcast_to(jnp.sum(mismatch * mismatch), (1, LANES))


def finish_kernel(params_ref, gradient_ref, sums_ref, new_ref, loss_ref, *, count):
    mean = sums_ref[...] * (1.0 / count)
    scale = step_length / jnp.sqrt(mean[0:1] + norm_eps)
    new_ref[...] = params_ref[...] - gradient_ref[...] * scale
    loss_ref[...] = mean[1:2]


def whole(shape):
    return pl.BlockSpec(shape, lambda *_: (0,) * len(shape))


def limit(size):
    return pltpu.CompilerParams(vmem_limit_bytes=size)


def shards(mask_params, target, col_taps, row_taps, kernel_weights):
    rows, cols = target.shape
    kernels, _, taps = col_taps.shape
    wide = 2 * HALF
    tiles = rows // LANES + 1
    long, span = tiles * LANES, cols + wide
    units, back_units = FORWARD_UNROLL, BACKWARD_UNROLL
    if cols != LANES or rows % LANES or taps != wide + 1 or kernels % units or kernels % back_units:
        raise ValueError("block shape")
    params = mask_params[0]
    smem = pl.BlockSpec(memory_space=pltpu.SMEM)
    small = limit(4 * 2**20)

    plain = jax.ShapeDtypeStruct((rows, cols), BF16)
    edge = jax.ShapeDtypeStruct((wide + HALF, cols), BF16)
    mask_half, code, to_down, to_up = pl.pallas_call(
        prepare_kernel, out_shape=(plain, plain, edge, edge), compiler_params=small, name="prepare"
    )(params, target)
    strips = lax.axis_size("strip")
    onward = [(i, i + 1) for i in range(strips - 1)]
    back = [(i + 1, i) for i in range(strips - 1)]
    from_up = lax.ppermute(to_down, "strip", onward)
    from_down = lax.ppermute(to_up, "strip", back)
    tap_rows = pl.pallas_call(
        taps_kernel,
        out_shape=jax.ShapeDtypeStruct((kernels, 4, 2 * LANES), F32),
        compiler_params=small,
        cost_estimate=pl.CostEstimate(flops=10**8, bytes_accessed=10**6, transcendentals=0),
        name="taps",
    )(col_taps, row_taps)

    sides = lax.axis_size("col")
    place = lax.axis_index("col")
    ends = jnp.stack([place == 0, place == sides - 1]).astype(jnp.int32)
    side = jax.ShapeDtypeStruct((wide + HALF, long), BF16)
    turned = jax.ShapeDtypeStruct((cols, long), BF16)
    vmem = pl.BlockSpec(memory_space=pltpu.VMEM)
    centre, code_turned, *messages = pl.pallas_call(
        assemble_kernel,
        in_specs=[smem, vmem, vmem, vmem, vmem],
        out_shape=(turned, turned) + (side,) * (1 if sides == 2 else 2),
        compiler_params=small,
        name="assemble",
    )(ends, mask_half, code, from_up, from_down)
    if sides == 2:
        before = after = lax.ppermute(messages[0], "col", [(0, 1), (1, 0)])
    else:
        before = lax.ppermute(messages[0], "col", [(i, i + 1) for i in range(sides - 1)])
        after = lax.ppermute(messages[1], "col", [(i + 1, i) for i in range(sides - 1)])

    def taps_spec(n):
        return pl.BlockSpec((n, 4, 2 * LANES), lambda k: (k, 0, 0))

    def field_spec(n):
        return pl.BlockSpec((n, tiles, span, 2 * LANES), lambda k: (k, 0, 0, 0))

    plane = (tiles, span, LANES)
    masks = pltpu.VMEM((4, LANES, LANES), BF16)
    field, intensity = pl.pallas_call(
        forward_kernel,
        grid=(kernels // units,),
        in_specs=[smem, smem, whole((cols, long)), whole(side.shape), whole(side.shape), taps_spec(units)],
        out_specs=[field_spec(units), whole(plane)],
        out_shape=(
            jax.ShapeDtypeStruct((kernels, tiles, span, 2 * LANES), BF16),
            jax.ShapeDtypeStruct(plane, F32),
        ),
        scratch_shapes=[
            pltpu.VMEM((cols + 2 * wide, long), BF16),
            pltpu.VMEM((tiles, span, 2 * LANES), F32),
            masks,
            pltpu.VMEM((units, 2, span, cols + 2 * wide), BF16),
            pltpu.VMEM((units, tiles * span, 2 * LANES), BF16),
        ],
        compiler_params=limit(VMEM),
        name="forward",
    )(kernel_weights, ends, centre, before, after, tap_rows)

    other = lax.ppermute(intensity, "expo", [(0, 1), (1, 0)])

    gradient, resist, sums = pl.pallas_call(
        backward_kernel,
        grid=(kernels // back_units,),
        in_specs=[
            smem,
            whole(plane),
            whole(plane),
            whole((cols, long)),
            whole(side.shape),
            whole(side.shape),
            whole((rows, cols)),
            field_spec(back_units),
            taps_spec(back_units),
        ],
        out_specs=[whole((rows, cols)), whole((rows, cols)), whole((2, LANES))],
        out_shape=(
            jax.ShapeDtypeStruct((rows, cols), F32),
            jax.ShapeDtypeStruct((rows, cols), F32),
            jax.ShapeDtypeStruct((2, LANES), F32),
        ),
        scratch_shapes=[
            pltpu.VMEM(plane, F32),
            pltpu.VMEM((cols, rows), F32),
            pltpu.VMEM((cols, long), F32),
            pltpu.VMEM((cols, long), F32),
            masks,
            pltpu.VMEM((cols, back_units * 2 * span), BF16),
            pltpu.VMEM((back_units * 2 * span, rows), BF16),
        ],
        compiler_params=limit(VMEM),
        name="backward",
    )(ends, intensity, other, code_turned, before, after, params, field, tap_rows)

    for axis in ("expo", "col", "strip"):
        sums = total_over(sums, axis)
    count = 2 * rows * cols * lax.axis_size("strip") * lax.axis_size("col")
    new_params, loss = pl.pallas_call(
        functools.partial(finish_kernel, count=count),
        out_shape=(jax.ShapeDtypeStruct((rows, cols), F32), jax.ShapeDtypeStruct((1, LANES), F32)),
        compiler_params=small,
        name="finish",
    )(params, gradient, sums)
    return (new_params[None], resist, loss[0, 0:1])


def solution(mesh):
    if mesh.shape["expo"] != 2:
        raise ValueError("two exposures")
    return jax.shard_map(
        shards,
        mesh=mesh,
        in_specs=(
            P("expo", ("tiles", "strip"), "col"),
            P(("tiles", "strip"), "col"),
            P(),
            P(),
            P(),
        ),
        out_specs=(P("expo", ("tiles", "strip"), "col"), P(("tiles", "strip"), "col"), P("tiles")),
        check_vma=False,
    )
```

```python
import functools
import jax
import jax.numpy as jnp
from jax import lax
from jax.experimental import pallas as pl
from jax.experimental.pallas import tpu as pltpu
from jax.sharding import PartitionSpec as P

HALF = 32
LANES = 128
FORWARD_UNROLL = 8
BACKWARD_UNROLL = 8
VMEM = 16 * 2**20

mask_slope = 4.0
resist_steep = 4.0
resist_level = 3.0
step_length = 0.5
norm_eps = 1e-06

BF16 = jnp.bfloat16
F32 = jnp.float32


def ring(axis, step):
    peers = lax.axis_size(axis)
    return [(i, (i + step) % peers) for i in range(peers)]


def partners(peers, other):
    return [(2 * i + core, 2 * other(i) + 1 - core) for i in range(peers) for core in range(2)]


def total_over(value, axis):
    peers = lax.axis_size(axis)
    if peers & (peers - 1):
        return lax.psum(value, axis)
    both = (axis, "expo")
    if peers == 4:
        one, two, three = (
            lax.ppermute(value, both, partners(peers, lambda i, d=d: (i + d) % peers)) for d in (1, 2, 3)
        )
        return (value + two) + (one + three)
    reach = 1
    while reach < peers:
        value = value + lax.ppermute(value, both, partners(peers, lambda i, r=reach: i ^ r))
        reach *= 2
    return value


def circulant(row, shift):
    spread = jnp.broadcast_to(row, (LANES, LANES))
    return pltpu.roll(spread, shift, 1, stride=1, stride_axis=0).astype(BF16)


def index_pair(shape):
    return lax.broadcasted_iota(jnp.int32, shape, 0), lax.broadcasted_iota(jnp.int32, shape, 1)


def write_masks(masks_ref):
    a, b = index_pair((LANES, LANES))
    one, zero = jnp.ones((LANES, LANES), F32), jnp.zeros((LANES, LANES), F32)
    for slot, keep in enumerate((b >= a, b < a, a >= b, a < b)):
        masks_ref[slot] = jnp.where(keep, one, zero).astype(BF16)


def taps_kernel(weights_ref, col_ref, row_ref, out_ref):
    kernels, _, taps = col_ref.shape
    t, l = index_pair((taps, 2 * LANES))
    pick = jnp.where((l == t) | (l == LANES + taps - 1 - t), 1.0, 0.0).astype(BF16)
    for k in range(kernels):
        both = jnp.concatenate([col_ref[k].astype(F32), row_ref[k].astype(F32)], axis=0).astype(BF16)
        out_ref[k, 0:4] = jnp.dot(both, pick, preferred_element_type=F32)
        out_ref[k, 4:8] = jnp.full((4, 2 * LANES), weights_ref[k], F32)


def prepare_kernel(
    params_hbm, target_hbm, params_ref, mask_ref, code_ref, down_ref, up_ref, target_ref, sems
):
    rows = params_ref.shape[0]
    wide = 2 * HALF
    copies = [
        pltpu.make_async_copy(params_hbm, params_ref, sems.at[0]),
        pltpu.make_async_copy(target_hbm, target_ref, sems.at[1]),
    ]
    for copy in copies:
        copy.start()
    for copy in copies:
        copy.wait()
    mask = jax.nn.sigmoid(mask_slope * params_ref[...]).astype(BF16)
    code = (target_ref[...] + 1).astype(F32).astype(BF16)
    mask_ref[...] = mask
    code_ref[...] = code
    down_ref[0:wide, :] = mask[rows - wide :]
    down_ref[wide:, :] = code[rows - HALF :]
    up_ref[0:wide, :] = mask[0:wide]
    up_ref[wide:, :] = code[0:HALF]


def unless(end, values):
    return jnp.where(end == 1, 0.0, values.astype(F32))


def assemble_kernel(
    ends_ref, mask_ref, code_ref, up_ref, down_ref, _, centre_ref, code_out_ref, *side_refs
):
    rows, cols = mask_ref.shape
    wide = 2 * HALF
    above, below = unless(ends_ref[2], up_ref[...]), unless(ends_ref[3], down_ref[...])
    tall = jnp.concatenate([above[0:wide], mask_ref[...].astype(F32), below[0:wide]], axis=0)
    turned = tall.T.astype(BF16)
    code = jnp.concatenate(
        [above[wide:], code_ref[...].astype(F32), below[wide:], jnp.zeros((wide, cols), F32)], axis=0
    )
    code = code.T.astype(BF16)
    centre_ref[...] = turned
    code_out_ref[...] = code

    def right(ref):
        ref[0:wide, :] = turned[cols - wide :, :]
        ref[wide:, :] = code[cols - HALF :, :]

    def left(ref):
        ref[0:wide, :] = turned[0:wide, :]
        ref[wide:, :] = code[0:HALF, :]

    if len(side_refs) == 2:
        right(side_refs[0])
        left(side_refs[1])
    else:
        pl.when(ends_ref[0] == 1)(lambda: right(side_refs[0]))
        pl.when(ends_ref[0] == 0)(lambda: left(side_refs[0]))


def forward_kernel(
    ends_ref,
    centre_ref,
    before_ref,
    after_ref,
    taps_ref,
    field_ref,
    intensity_ref,
    mask_ref,
    total_ref,
    masks_ref,
    table_ref,
    columns_ref,
):
    kernels = taps_ref.shape[0]
    units = columns_ref.shape[0]
    cols = centre_ref.shape[0]
    wide = 2 * HALF
    long = centre_ref.shape[1]
    tiles = long // LANES
    blocks = cols // wide + 1
    span = cols + wide

    mask = jnp.concatenate(
        [
            unless(ends_ref[0], before_ref[0:wide, :]).astype(BF16),
            centre_ref[...],
            unless(ends_ref[1], after_ref[0:wide, :]).astype(BF16),
        ],
        axis=0,
    )
    for block in range(blocks):
        mask_ref[:, block * long : (block + 1) * long] = mask[block * wide : block * wide + LANES]
    total_ref[...] = jnp.zeros_like(total_ref)
    write_masks(masks_ref)

    def group(step, carry):
        for unit in range(units):
            for part in range(2):
                row = taps_ref[step * units + unit, part : part + 1, 0:LANES]
                base = circulant(row, 0)[0:wide]
                at = (unit * 2 + part) * wide
                table_ref[at : at + wide, :] = base * masks_ref[0, 0:wide]
        columns = jnp.dot(table_ref[...], mask_ref[...], preferred_element_type=F32).astype(BF16)
        for unit in range(units):
            for part in range(2):
                at = (unit * 2 + part) * wide
                for block in range(blocks):
                    for t in range(tiles):
                        lane = block * long + t * LANES
                        to = t * span + block * wide
                        columns_ref[unit, to : to + wide, part * LANES : (part + 1) * LANES] = columns[
                            at : at + wide, lane : lane + LANES
                        ]
        for unit in range(units):
            kernel = step * units + unit
            near, far = [], []
            for part in range(2):
                base = circulant(taps_ref[kernel, 2 + part : 3 + part, LANES:], LANES // 2)
                near.append(base * masks_ref[2])
                far.append(base * masks_ref[3])
            near = [
                jnp.concatenate([near[0], near[1]], axis=1),
                jnp.concatenate([-near[1], near[0]], axis=1),
            ]
            far = [
                jnp.concatenate([far[0], far[1]], axis=1),
                jnp.concatenate([-far[1], far[0]], axis=1),
            ]
            weight = taps_ref[kernel, 4:5, :]
            edge = (tiles - 1) * span
            window = jnp.concatenate([columns_ref[unit, 0:edge], columns_ref[unit, span:]], axis=1)
            inner = jnp.dot(window, jnp.concatenate(near + far, axis=0), preferred_element_type=F32)
            outer = jnp.dot(
                columns_ref[unit, edge:], jnp.concatenate(near, axis=0), preferred_element_type=F32
            )
            for t in range(tiles):
                part = inner[t * span : (t + 1) * span] if t + 1 < tiles else outer
                scaled = weight * part
                field_ref[kernel, t] = scaled.astype(field_ref.dtype)
                total_ref[t] += scaled * part
        return carry

    lax.fori_loop(0, kernels // units, group, 0)
    for t in range(tiles):
        intensity_ref[t] = total_ref[t, :, 0:LANES] + total_ref[t, :, LANES:]


def backward_kernel(
    ends_ref,
    own_ref,
    other_ref,
    code_ref,
    code_before_ref,
    code_after_ref,
    params_ref,
    field_ref,
    taps_ref,
    gradient_ref,
    resist_hbm,
    sums_ref,
    slope_ref,
    descent_ref,
    resist_ref,
    masks_ref,
    table_ref,
    source_ref,
    sem,
):
    kernels = taps_ref.shape[0]
    cols = code_ref.shape[0]
    wide = 2 * HALF
    tiles = own_ref.shape[0]
    span = cols + wide
    rows = (tiles - 1) * LANES
    units = table_ref.shape[1] // (2 * span)

    resists, loss = [], 0.0
    for t in range(tiles):
        lanes = slice(t * LANES, (t + 1) * LANES)
        code = jnp.concatenate(
            [
                unless(ends_ref[0], code_before_ref[wide:, lanes]),
                code_ref[:, lanes].astype(F32),
                unless(ends_ref[1], code_after_ref[wide:, lanes]),
            ],
            axis=0,
        )
        summed = own_ref[t] + other_ref[t]
        resist = jax.nn.sigmoid(resist_steep * (summed - resist_level))
        mismatch = resist - (code - 1.0)
        slope = 4.0 * mismatch * resist_steep * resist * (1.0 - resist)
        slope = jnp.where(code > 0.5, slope, 0.0).astype(BF16)
        slope_ref[t] = jnp.concatenate([slope, slope], axis=1)
        resists.append(resist[HALF : HALF + cols])
        mine = mismatch[HALF : HALF + cols]
        _, lane = index_pair(mine.shape)
        lane = lane + t * LANES
        mine = jnp.where((lane >= HALF) & (lane < HALF + rows), mine, 0.0)
        loss = loss + mine * mine
    resist_ref[...] = jnp.concatenate(resists, axis=1).T[HALF : HALF + rows]
    copy = pltpu.make_async_copy(resist_ref, resist_hbm, sem)
    copy.start()
    descent_ref[...] = jnp.zeros_like(descent_ref)
    write_masks(masks_ref)

    def group(step, carry):
        a, b = index_pair((LANES, LANES))
        inside = jnp.where(b < wide, b, b - wide) < a
        for unit in range(units):
            kernel = step * units + unit
            near, far = [], []
            for part in range(2):
                base = circulant(taps_ref[kernel, 2 + part : 3 + part, 0:LANES], LANES // 2)
                near.append(base * masks_ref[2])
                far.append(base * masks_ref[3])
            table = jnp.concatenate(
                [
                    jnp.concatenate([near[0], -near[1]], axis=1),
                    jnp.concatenate([near[1], near[0]], axis=1),
                    jnp.concatenate([far[0], -far[1]], axis=1),
                    jnp.concatenate([far[1], far[0]], axis=1),
                ],
                axis=0,
            )
            products = [slope_ref[t] * field_ref[kernel, t] for t in range(tiles)]
            window = jnp.concatenate(
                [jnp.concatenate(products[:-1], axis=0), jnp.concatenate(products[1:], axis=0)], axis=1
            )
            returned = jnp.dot(window, table, preferred_element_type=F32).astype(BF16)
            at = unit * 2 * span
            for t in range(tiles - 1):
                to = slice(t * LANES, (t + 1) * LANES)
                for part in range(2):
                    piece = returned[t * span : (t + 1) * span, part * LANES : (part + 1) * LANES]
                    source_ref[at + part * cols : at + (part + 1) * cols, to] = piece[0:cols]
                    tail = at + 2 * cols + part * wide
                    source_ref[tail : tail + wide, to] = piece[cols:]
            turned = []
            for part in range(2):
                row = taps_ref[kernel, part : part + 1, LANES:]
                table_ref[:, at + part * LANES : at + (part + 1) * LANES] = circulant(row, 0) * masks_ref[0]
                spread = jnp.broadcast_to(row, (LANES, LANES))
                turned.append(pltpu.roll(spread, part * wide, 1, stride=1, stride_axis=0))
            both = jnp.where(b < wide, turned[0], turned[1])
            table_ref[:, at + 2 * LANES : at + 3 * LANES] = jnp.where(inside, both, 0.0).astype(BF16)
        descent_ref[...] += jnp.dot(table_ref[...], source_ref[...], preferred_element_type=F32)
        return carry

    lax.fori_loop(0, kernels // units, group, 0)
    mask = jax.nn.sigmoid(mask_slope * params_ref[...])
    gradient = descent_ref[...].T * mask_slope * mask * (1.0 - mask)
    gradient_ref[...] = gradient
    sums_ref[0:1, :] = jnp.broadcast_to(jnp.sum(gradient * gradient), (1, LANES))
    sums_ref[1:2, :] = jnp.broadcast_to(jnp.sum(loss), (1, LANES))
    copy.wait()


def finish_kernel(params_ref, gradient_ref, sums_ref, new_ref, loss_ref, *, count):
    mean = sums_ref[...] * (1.0 / count)
    scale = step_length / jnp.sqrt(mean[0:1] + norm_eps)
    new_ref[...] = params_ref[...] - gradient_ref[...] * scale
    loss_ref[...] = mean[1:2]


def shards(mask_params, target, col_taps, row_taps, kernel_weights):
    rows, cols = target.shape
    kernels, _, taps = col_taps.shape
    wide = 2 * HALF
    tiles = rows // LANES + 1
    long, span = tiles * LANES, cols + wide
    units, back_units = FORWARD_UNROLL, BACKWARD_UNROLL
    if cols != LANES or rows % LANES or taps != wide + 1 or kernels % units or kernels % back_units:
        raise ValueError("block shape")
    smem = pl.BlockSpec(memory_space=pltpu.SMEM)
    vmem = pl.BlockSpec(memory_space=pltpu.VMEM)
    hbm = pl.BlockSpec(memory_space=pltpu.HBM)
    array = jax.ShapeDtypeStruct

    def call(body, name, specs, outs, out_specs=None, scratch=(), grant=4 * 2**20, flops=10**6):
        return pl.pallas_call(
            body,
            in_specs=specs,
            out_shape=outs,
            out_specs=[vmem] * len(outs) if out_specs is None else out_specs,
            scratch_shapes=scratch,
            compiler_params=pltpu.CompilerParams(vmem_limit_bytes=grant),
            cost_estimate=pl.CostEstimate(flops=flops, bytes_accessed=10**6, transcendentals=0),
            name=name,
        )

    plain, edge = array((rows, cols), BF16), array((wide + HALF, cols), BF16)
    full = array((rows, cols), F32)
    params, mask_half, code, to_down, to_up = call(
        prepare_kernel,
        "prepare",
        [hbm, hbm],
        (full, plain, plain, edge, edge),
        scratch=[pltpu.VMEM((rows, cols), target.dtype), pltpu.SemaphoreType.DMA((2,))],
    )(mask_params[0], target)
    from_up = lax.ppermute(to_down, "strip", ring("strip", 1))
    from_down = lax.ppermute(to_up, "strip", ring("strip", -1))
    (tap_rows,) = call(
        taps_kernel, "taps", [smem, vmem, vmem], (array((kernels, 8, 2 * LANES), F32),), flops=10**8
    )(kernel_weights, col_taps, row_taps)

    sides, strips = lax.axis_size("col"), lax.axis_size("strip")
    place, level = lax.axis_index("col"), lax.axis_index("strip")
    ends = jnp.stack([place == 0, place == sides - 1, level == 0, level == strips - 1]).astype(jnp.int32)
    side, turned = array((wide + HALF, long), BF16), array((cols, long), BF16)
    centre, code_turned, *messages = call(
        assemble_kernel,
        "assemble",
        [smem, vmem, vmem, vmem, vmem, pl.BlockSpec(memory_space=pl.ANY)],
        (turned, turned) + (side,) * (1 if sides == 2 else 2),
    )(ends, mask_half, code, from_up, from_down, tap_rows)
    if sides == 2:
        before = after = lax.ppermute(messages[0], "col", ring("col", 1))
    else:
        before = lax.ppermute(messages[0], "col", ring("col", 1))
        after = lax.ppermute(messages[1], "col", ring("col", -1))

    masks = pltpu.VMEM((4, LANES, LANES), BF16)
    plane = (tiles, span, LANES)
    field, intensity = call(
        forward_kernel,
        "forward",
        [smem] + [vmem] * 4,
        (array((kernels, tiles, span, 2 * LANES), BF16), array(plane, F32)),
        scratch=[
            pltpu.VMEM((LANES, (cols // wide + 1) * long), BF16),
            pltpu.VMEM((tiles, span, 2 * LANES), F32),
            masks,
            pltpu.VMEM((units * 2 * wide, LANES), BF16),
            pltpu.VMEM((units, tiles * span, 2 * LANES), BF16),
        ],
        grant=VMEM,
    )(ends, centre, before, after, tap_rows)

    other = lax.ppermute(intensity, "expo", [(0, 1), (1, 0)])

    gradient, resist, sums = call(
        backward_kernel,
        "backward",
        [smem] + [vmem] * 8,
        (full, full, array((2, LANES), F32)),
        out_specs=[vmem, hbm, vmem],
        scratch=[
            pltpu.VMEM((tiles, span, 2 * LANES), BF16),
            pltpu.VMEM((cols, rows), F32),
            pltpu.VMEM((rows, cols), F32),
            masks,
            pltpu.VMEM((cols, back_units * 2 * span), BF16),
            pltpu.VMEM((back_units * 2 * span, rows), BF16),
            pltpu.SemaphoreType.DMA,
        ],
        grant=VMEM,
    )(ends, intensity, other, code_turned, before, after, params, field, tap_rows)

    sums = sums + lax.ppermute(sums, "expo", [(0, 1), (1, 0)])
    for axis in ("col", "strip"):
        sums = total_over(sums, axis)
    count = 2 * rows * cols * strips * sides
    new_params, loss = call(
        functools.partial(finish_kernel, count=count), "finish", [vmem] * 3, (full, array((1, LANES), F32))
    )(params, gradient, sums)
    return (new_params[None], resist, loss[0, 0:1])


def solution(mesh):
    if mesh.shape["expo"] != 2:
        raise ValueError("two exposures")
    return jax.shard_map(
        shards,
        mesh=mesh,
        in_specs=(
            P("expo", ("tiles", "strip"), "col"),
            P(("tiles", "strip"), "col"),
            P(),
            P(),
            P(),
        ),
        out_specs=(P("expo", ("tiles", "strip"), "col"), P(("tiles", "strip"), "col"), P("tiles")),
        check_vma=False,
    )
```

```python
import functools
import jax
import jax.numpy as jnp
from jax import lax
from jax.experimental import pallas as pl
from jax.experimental.pallas import tpu as pltpu
from jax.sharding import PartitionSpec as P

HALF = 32
LANES = 128
FORWARD_UNROLL = 24
BACKWARD_UNROLL = 12
CHUNK = 4
VMEM = 24 * 2**20

mask_slope = 4.0
resist_steep = 4.0
resist_level = 3.0
step_length = 0.5
norm_eps = 1e-06

BF16 = jnp.bfloat16
F32 = jnp.float32


def stay(array):
    return pltpu.with_memory_space_constraint(array, pltpu.HBM)


def ring(axis, step):
    peers = lax.axis_size(axis)
    return [(i, (i + step) % peers) for i in range(peers)]


def snake(step):
    tiles, strips = lax.axis_size("tiles"), lax.axis_size("strip")
    order = []
    for tile in range(tiles):
        levels = range(strips) if tile % 2 == 0 else reversed(range(strips))
        order += [tile * strips + level for level in levels]
    return [(device, order[(i + step) % len(order)]) for i, device in enumerate(order)]


def partners(peers, other):
    return [(2 * i + core, 2 * other(i) + 1 - core) for i in range(peers) for core in range(2)]


def total_over(value, axis):
    peers = lax.axis_size(axis)
    if peers & (peers - 1):
        return lax.psum(value, axis)
    both = (axis, "expo")
    if peers == 4:
        one, two, three = (
            lax.ppermute(value, both, partners(peers, lambda i, d=d: i ^ d)) for d in (1, 2, 3)
        )
        return (value + two) + (one + three)
    reach = 1
    while reach < peers:
        value = value + lax.ppermute(value, both, partners(peers, lambda i, r=reach: i ^ r))
        reach *= 2
    return value


def circulant(row, shift):
    spread = jnp.broadcast_to(row, (LANES, LANES))
    return pltpu.roll(spread, shift, 1, stride=1, stride_axis=0).astype(BF16)


def index_pair(shape):
    return lax.broadcasted_iota(jnp.int32, shape, 0), lax.broadcasted_iota(jnp.int32, shape, 1)


def write_masks(masks_ref):
    a, b = index_pair((LANES, LANES))
    one, zero = jnp.ones((LANES, LANES), F32), jnp.zeros((LANES, LANES), F32)
    for slot, keep in enumerate((b >= a, b < a, a >= b, a < b)):
        masks_ref[slot] = jnp.where(keep, one, zero).astype(BF16)


def taps_kernel(weights_hbm, col_hbm, row_hbm, out_ref, weights_ref, col_ref, row_ref, flat_ref, sems):
    kernels, _, taps = col_ref.shape
    copies = [
        pltpu.make_async_copy(source, target, sems.at[slot])
        for slot, (source, target) in enumerate(
            ((weights_hbm, weights_ref), (col_hbm, col_ref), (row_hbm, row_ref))
        )
    ]
    for copy in copies:
        copy.start()
    t, l = index_pair((taps, 2 * LANES))
    pick = jnp.where((l == t) | (l == LANES + taps - 1 - t), 1.0, 0.0).astype(BF16)
    for copy in copies:
        copy.wait()
    for k in range(kernels):
        flat_ref[4 * k : 4 * k + 2] = col_ref[k].astype(F32)
        flat_ref[4 * k + 2 : 4 * k + 4] = row_ref[k].astype(F32)
    rows = jnp.dot(flat_ref[...].astype(BF16), pick, preferred_element_type=F32)
    for k in range(kernels):
        out_ref[k, 0:4] = rows[4 * k : 4 * k + 4]
        out_ref[k, 4:8] = jnp.full((4, 2 * LANES), weights_ref[k], F32)


def prepare_kernel(
    ends_ref, params_hbm, target_hbm, params_ref, mask_ref, code_ref, ahead_ref, behind_ref, target_ref, sems
):
    rows = params_ref.shape[0]
    wide = 2 * HALF
    copies = [
        pltpu.make_async_copy(params_hbm, params_ref, sems.at[0]),
        pltpu.make_async_copy(target_hbm, target_ref, sems.at[1]),
    ]
    for copy in copies:
        copy.start()
    for copy in copies:
        copy.wait()
    mask = jax.nn.sigmoid(mask_slope * params_ref[...]).astype(BF16)
    code = (target_ref[...] + 1).astype(F32).astype(BF16)
    mask_ref[...] = mask
    code_ref[...] = code

    def edges(down_ref, up_ref):
        down_ref[0:wide, :] = mask[rows - wide :]
        down_ref[wide:, :] = code[rows - HALF :]
        up_ref[0:wide, :] = mask[0:wide]
        up_ref[wide:, :] = code[0:HALF]

    pl.when(ends_ref[4] == 0)(lambda: edges(ahead_ref, behind_ref))
    pl.when(ends_ref[4] == 1)(lambda: edges(behind_ref, ahead_ref))


def unless(end, values):
    return jnp.where(end == 1, 0.0, values.astype(F32))


def assemble_kernel(
    ends_ref, mask_ref, code_ref, behind_ref, ahead_ref, _, centre_ref, code_out_ref, *side_refs
):
    rows, cols = mask_ref.shape
    wide = 2 * HALF
    turn = ends_ref[4] == 1
    behind, ahead = behind_ref[...].astype(F32), ahead_ref[...].astype(F32)
    above = unless(ends_ref[2], jnp.where(turn, ahead, behind))
    below = unless(ends_ref[3], jnp.where(turn, behind, ahead))
    tall = jnp.concatenate([above[0:wide], mask_ref[...].astype(F32), below[0:wide]], axis=0)
    turned = tall.T.astype(BF16)
    code = jnp.concatenate(
        [above[wide:], code_ref[...].astype(F32), below[wide:], jnp.zeros((wide, cols), F32)], axis=0
    )
    code = code.T.astype(BF16)
    centre_ref[...] = turned
    code_out_ref[...] = code

    def right(ref):
        ref[0:wide, :] = turned[cols - wide :, :]
        ref[wide:, :] = code[cols - HALF :, :]

    def left(ref):
        ref[0:wide, :] = turned[0:wide, :]
        ref[wide:, :] = code[0:HALF, :]

    if len(side_refs) == 2:
        right(side_refs[0])
        left(side_refs[1])
    else:
        pl.when(ends_ref[0] == 1)(lambda: right(side_refs[0]))
        pl.when(ends_ref[0] == 0)(lambda: left(side_refs[0]))


def forward_kernel(
    ends_ref,
    centre_ref,
    before_ref,
    after_ref,
    taps_ref,
    field_ref,
    intensity_ref,
    mask_ref,
    total_ref,
    masks_ref,
    table_ref,
    columns_ref,
):
    kernels = taps_ref.shape[0]
    units = columns_ref.shape[0]
    cols = centre_ref.shape[0]
    wide = 2 * HALF
    long = centre_ref.shape[1]
    tiles = long // LANES
    blocks = cols // wide + 1
    span = cols + wide

    mask = jnp.concatenate(
        [
            unless(ends_ref[0], before_ref[0:wide, :]).astype(BF16),
            centre_ref[...],
            unless(ends_ref[1], after_ref[0:wide, :]).astype(BF16),
        ],
        axis=0,
    )
    for block in range(blocks):
        mask_ref[:, block * long : (block + 1) * long] = mask[block * wide : block * wide + LANES]
    total_ref[...] = jnp.zeros_like(total_ref)
    write_masks(masks_ref)

    def group(step, carry):
        for unit in range(units):
            for part in range(2):
                row = taps_ref[step * units + unit, part : part + 1, 0:LANES]
                base = circulant(row, 0)[0:wide]
                at = (unit * 2 + part) * wide
                table_ref[at : at + wide, :] = base * masks_ref[0, 0:wide]
        columns = jnp.dot(table_ref[...], mask_ref[...], preferred_element_type=F32).astype(BF16)
        for unit in range(units):
            for part in range(2):
                at = (unit * 2 + part) * wide
                for block in range(blocks):
                    for t in range(tiles):
                        lane = block * long + t * LANES
                        to = t * span + block * wide
                        columns_ref[unit, to : to + wide, part * LANES : (part + 1) * LANES] = columns[
                            at : at + wide, lane : lane + LANES
                        ]
        for unit in range(units):
            kernel = step * units + unit
            near, far = [], []
            for part in range(2):
                base = circulant(taps_ref[kernel, 2 + part : 3 + part, LANES:], LANES // 2)
                near.append(base * masks_ref[2])
                far.append(base * masks_ref[3])
            near = [
                jnp.concatenate([near[0], near[1]], axis=1),
                jnp.concatenate([-near[1], near[0]], axis=1),
            ]
            far = [
                jnp.concatenate([far[0], far[1]], axis=1),
                jnp.concatenate([-far[1], far[0]], axis=1),
            ]
            weight = taps_ref[kernel, 4:5, :]
            edge = (tiles - 1) * span
            window = jnp.concatenate([columns_ref[unit, 0:edge], columns_ref[unit, span:]], axis=1)
            inner = jnp.dot(window, jnp.concatenate(near + far, axis=0), preferred_element_type=F32)
            outer = jnp.dot(
                columns_ref[unit, edge:], jnp.concatenate(near, axis=0), preferred_element_type=F32
            )
            for t in range(tiles):
                part = inner[t * span : (t + 1) * span] if t + 1 < tiles else outer
                scaled = weight * part
                field_ref[kernel, t] = scaled.astype(field_ref.dtype)
                total_ref[t] += scaled * part
        return carry

    lax.fori_loop(0, kernels // units, group, 0)
    for t in range(tiles):
        intensity_ref[t] = total_ref[t, :, 0:LANES] + total_ref[t, :, LANES:]


def backward_kernel(
    ends_ref,
    own_ref,
    other_ref,
    code_ref,
    code_before_ref,
    code_after_ref,
    params_ref,
    field_ref,
    taps_ref,
    gradient_ref,
    resist_hbm,
    sums_ref,
    slope_ref,
    descent_ref,
    resist_ref,
    masks_ref,
    table_ref,
    source_ref,
    sem,
):
    kernels = taps_ref.shape[0]
    cols = code_ref.shape[0]
    wide = 2 * HALF
    tiles = own_ref.shape[0]
    span = cols + wide
    rows = (tiles - 1) * LANES
    units = table_ref.shape[1] // (2 * span)

    resists, loss = [], 0.0
    for t in range(tiles):
        lanes = slice(t * LANES, (t + 1) * LANES)
        code = jnp.concatenate(
            [
                unless(ends_ref[0], code_before_ref[wide:, lanes]),
                code_ref[:, lanes].astype(F32),
                unless(ends_ref[1], code_after_ref[wide:, lanes]),
            ],
            axis=0,
        )
        summed = own_ref[t] + other_ref[t]
        resist = jax.nn.sigmoid(resist_steep * (summed - resist_level))
        mismatch = resist - (code - 1.0)
        slope = 4.0 * mismatch * resist_steep * resist * (1.0 - resist)
        slope = jnp.where(code > 0.5, slope, 0.0).astype(BF16)
        slope_ref[t] = jnp.concatenate([slope, slope], axis=1)
        resists.append(resist[HALF : HALF + cols])
        mine = mismatch[HALF : HALF + cols]
        _, lane = index_pair(mine.shape)
        lane = lane + t * LANES
        mine = jnp.where((lane >= HALF) & (lane < HALF + rows), mine, 0.0)
        loss = loss + mine * mine
    resist_ref[...] = jnp.concatenate(resists, axis=1).T[HALF : HALF + rows]
    copy = pltpu.make_async_copy(resist_ref, resist_hbm, sem)
    copy.start()
    descent_ref[...] = jnp.zeros_like(descent_ref)
    write_masks(masks_ref)

    def group(step, carry):
        a, b = index_pair((LANES, LANES))
        inside = jnp.where(b < wide, b, b - wide) < a
        for unit in range(units):
            kernel = step * units + unit
            near, far = [], []
            for part in range(2):
                base = circulant(taps_ref[kernel, 2 + part : 3 + part, 0:LANES], LANES // 2)
                near.append(base * masks_ref[2])
                far.append(base * masks_ref[3])
            table = jnp.concatenate(
                [
                    jnp.concatenate([near[0], -near[1]], axis=1),
                    jnp.concatenate([near[1], near[0]], axis=1),
                    jnp.concatenate([far[0], -far[1]], axis=1),
                    jnp.concatenate([far[1], far[0]], axis=1),
                ],
                axis=0,
            )
            products = [slope_ref[t] * field_ref[kernel, t] for t in range(tiles)]
            window = jnp.concatenate(
                [jnp.concatenate(products[:-1], axis=0), jnp.concatenate(products[1:], axis=0)], axis=1
            )
            returned = jnp.dot(window, table, preferred_element_type=F32).astype(BF16)
            at = unit * 2 * span
            for t in range(tiles - 1):
                to = slice(t * LANES, (t + 1) * LANES)
                for part in range(2):
                    piece = returned[t * span : (t + 1) * span, part * LANES : (part + 1) * LANES]
                    source_ref[at + part * cols : at + (part + 1) * cols, to] = piece[0:cols]
                    tail = at + 2 * cols + part * wide
                    source_ref[tail : tail + wide, to] = piece[cols:]
            turned = []
            for part in range(2):
                row = taps_ref[kernel, part : part + 1, LANES:]
                table_ref[:, at + part * LANES : at + (part + 1) * LANES] = circulant(row, 0) * masks_ref[0]
                spread = jnp.broadcast_to(row, (LANES, LANES))
                turned.append(pltpu.roll(spread, part * wide, 1, stride=1, stride_axis=0))
            both = jnp.where(b < wide, turned[0], turned[1])
            table_ref[:, at + 2 * LANES : at + 3 * LANES] = jnp.where(inside, both, 0.0).astype(BF16)
            if unit % CHUNK == CHUNK - 1:
                chunk = slice((unit + 1 - CHUNK) * 2 * span, (unit + 1) * 2 * span)
                descent_ref[...] += jnp.dot(
                    table_ref[:, chunk], source_ref[chunk, :], preferred_element_type=F32
                )
        return carry

    lax.fori_loop(0, kernels // units, group, 0)
    mask = jax.nn.sigmoid(mask_slope * params_ref[...])
    gradient = descent_ref[...].T * mask_slope * mask * (1.0 - mask)
    gradient_ref[...] = gradient
    sums_ref[0:1, :] = jnp.broadcast_to(jnp.sum(gradient * gradient), (1, LANES))
    sums_ref[1:2, :] = jnp.broadcast_to(jnp.sum(loss), (1, LANES))
    copy.wait()


def finish_kernel(params_ref, gradient_ref, sums_ref, new_ref, loss_ref, *, count):
    mean = sums_ref[...] * (1.0 / count)
    scale = step_length / jnp.sqrt(mean[0:1] + norm_eps)
    new_ref[...] = params_ref[...] - gradient_ref[...] * scale
    loss_ref[...] = mean[1:2]


def shards(mask_params, target, col_taps, row_taps, kernel_weights):
    rows, cols = target.shape
    kernels, _, taps = col_taps.shape
    wide = 2 * HALF
    tiles = rows // LANES + 1
    long, span = tiles * LANES, cols + wide
    units, back_units = FORWARD_UNROLL, BACKWARD_UNROLL
    if cols != LANES or rows % LANES or taps != wide + 1 or kernels % units or kernels % back_units:
        raise ValueError("block shape")
    smem = pl.BlockSpec(memory_space=pltpu.SMEM)
    vmem = pl.BlockSpec(memory_space=pltpu.VMEM)
    hbm = pl.BlockSpec(memory_space=pltpu.HBM)
    array = jax.ShapeDtypeStruct

    def call(body, name, specs, outs, out_specs=None, scratch=(), grant=4 * 2**20, flops=10**6):
        return pl.pallas_call(
            body,
            in_specs=specs,
            out_shape=outs,
            out_specs=[vmem] * len(outs) if out_specs is None else out_specs,
            scratch_shapes=scratch,
            compiler_params=pltpu.CompilerParams(vmem_limit_bytes=grant),
            cost_estimate=pl.CostEstimate(flops=flops, bytes_accessed=10**6, transcendentals=0),
            name=name,
        )

    plain, edge = array((rows, cols), BF16), array((wide + HALF, cols), BF16)
    full = array((rows, cols), F32)
    sides, strips = lax.axis_size("col"), lax.axis_size("strip")
    place, level, turn = lax.axis_index("col"), lax.axis_index("strip"), lax.axis_index("tiles") % 2
    ends = jnp.stack([place == 0, place == sides - 1, level == 0, level == strips - 1, turn == 1]).astype(jnp.int32)
    params, mask_half, code, ahead, behind = call(
        prepare_kernel,
        "prepare",
        [smem, hbm, hbm],
        (full, plain, plain, edge, edge),
        scratch=[pltpu.VMEM((rows, cols), target.dtype), pltpu.SemaphoreType.DMA((2,))],
    )(ends, stay(mask_params[0]), stay(target))
    from_behind = lax.ppermute(ahead, ("tiles", "strip"), snake(1))
    from_ahead = lax.ppermute(behind, ("tiles", "strip"), snake(-1))
    (tap_rows,) = call(
        taps_kernel,
        "taps",
        [hbm] * 3,
        (array((kernels, 8, 2 * LANES), F32),),
        scratch=[
            pltpu.SMEM(kernel_weights.shape, F32),
            pltpu.VMEM(col_taps.shape, BF16),
            pltpu.VMEM(row_taps.shape, BF16),
            pltpu.VMEM((4 * kernels, taps), F32),
            pltpu.SemaphoreType.DMA((3,)),
        ],
        flops=10**8,
    )(stay(kernel_weights), stay(col_taps), stay(row_taps))

    side, turned = array((wide + HALF, long), BF16), array((cols, long), BF16)
    centre, code_turned, *messages = call(
        assemble_kernel,
        "assemble",
        [smem, vmem, vmem, vmem, vmem, pl.BlockSpec(memory_space=pl.ANY)],
        (turned, turned) + (side,) * (1 if sides == 2 else 2),
    )(ends, mask_half, code, from_behind, from_ahead, tap_rows)
    if sides == 2:
        before = after = lax.ppermute(messages[0], "col", ring("col", 1))
    else:
        before = lax.ppermute(messages[0], "col", ring("col", 1))
        after = lax.ppermute(messages[1], "col", ring("col", -1))

    masks = pltpu.VMEM((4, LANES, LANES), BF16)
    plane = (tiles, span, LANES)
    field, intensity = call(
        forward_kernel,
        "forward",
        [smem] + [vmem] * 4,
        (array((kernels, tiles, span, 2 * LANES), BF16), array(plane, F32)),
        scratch=[
            pltpu.VMEM((LANES, (cols // wide + 1) * long), BF16),
            pltpu.VMEM((tiles, span, 2 * LANES), F32),
            masks,
            pltpu.VMEM((units * 2 * wide, LANES), BF16),
            pltpu.VMEM((units, tiles * span, 2 * LANES), BF16),
        ],
        grant=VMEM,
    )(ends, centre, before, after, tap_rows)

    other = lax.ppermute(intensity, "expo", [(0, 1), (1, 0)])

    gradient, resist, sums = call(
        backward_kernel,
        "backward",
        [smem] + [vmem] * 8,
        (full, full, array((2, LANES), F32)),
        out_specs=[vmem, hbm, vmem],
        scratch=[
            pltpu.VMEM((tiles, span, 2 * LANES), BF16),
            pltpu.VMEM((cols, rows), F32),
            pltpu.VMEM((rows, cols), F32),
            masks,
            pltpu.VMEM((cols, back_units * 2 * span), BF16),
            pltpu.VMEM((back_units * 2 * span, rows), BF16),
            pltpu.SemaphoreType.DMA,
        ],
        grant=VMEM,
    )(ends, intensity, other, code_turned, before, after, params, field, tap_rows)

    sums = sums + lax.ppermute(sums, "expo", [(0, 1), (1, 0)])
    for axis in ("col", "strip"):
        sums = total_over(sums, axis)
    count = 2 * rows * cols * strips * sides
    new_params, loss = call(
        functools.partial(finish_kernel, count=count), "finish", [vmem] * 3, (full, array((1, LANES), F32))
    )(params, gradient, sums)
    return (new_params[None], resist, loss[0, 0:1])


def solution(mesh):
    if mesh.shape["expo"] != 2:
        raise ValueError("two exposures")
    return jax.shard_map(
        shards,
        mesh=mesh,
        in_specs=(
            P("expo", ("tiles", "strip"), "col"),
            P(("tiles", "strip"), "col"),
            P(),
            P(),
            P(),
        ),
        out_specs=(P("expo", ("tiles", "strip"), "col"), P(("tiles", "strip"), "col"), P("tiles")),
        check_vma=False,
    )
```

```python
import functools
import jax
import jax.numpy as jnp
from jax import lax
from jax.experimental import pallas as pl
from jax.experimental.pallas import tpu as pltpu
from jax.sharding import PartitionSpec as P

HALF = 32
LANES = 128
FORWARD_UNROLL = 24
BACKWARD_UNROLL = 12
CHUNK = 4
VMEM = 24 * 2**20

mask_slope = 4.0
resist_steep = 4.0
resist_level = 3.0
step_length = 0.5
norm_eps = 1e-06

BF16 = jnp.bfloat16
F32 = jnp.float32


def stay(array):
    return pltpu.with_memory_space_constraint(array, pltpu.HBM)


def ring(axis, step):
    peers = lax.axis_size(axis)
    return [(i, (i + step) % peers) for i in range(peers)]


def snake(step):
    tiles, strips = lax.axis_size("tiles"), lax.axis_size("strip")
    order = []
    for tile in range(tiles):
        levels = range(strips) if tile % 2 == 0 else reversed(range(strips))
        order += [tile * strips + level for level in levels]
    return [(device, order[(i + step) % len(order)]) for i, device in enumerate(order)]


def partners(peers, other):
    return [(2 * i + core, 2 * other(i) + 1 - core) for i in range(peers) for core in range(2)]


def total_over(value, axis):
    peers = lax.axis_size(axis)
    if peers & (peers - 1):
        return lax.psum(value, axis)
    both = (axis, "expo")
    if peers == 4:
        one, two, three = (
            lax.ppermute(value, both, partners(peers, lambda i, d=d: i ^ d)) for d in (1, 2, 3)
        )
        return (value + two) + (one + three)
    reach = 1
    while reach < peers:
        value = value + lax.ppermute(value, both, partners(peers, lambda i, r=reach: i ^ r))
        reach *= 2
    return value


def circulant(row, shift):
    spread = jnp.broadcast_to(row, (LANES, LANES))
    return pltpu.roll(spread, shift, 1, stride=1, stride_axis=0).astype(BF16)


def index_pair(shape):
    return lax.broadcasted_iota(jnp.int32, shape, 0), lax.broadcasted_iota(jnp.int32, shape, 1)


def write_masks(masks_ref):
    a, b = index_pair((LANES, LANES))
    one, zero = jnp.ones((LANES, LANES), F32), jnp.zeros((LANES, LANES), F32)
    for slot, keep in enumerate((b >= a, b < a, a >= b, a < b)):
        masks_ref[slot] = jnp.where(keep, one, zero).astype(BF16)


def taps_kernel(weights_hbm, col_hbm, row_hbm, out_ref, weights_ref, col_ref, row_ref, flat_ref, sems):
    kernels, _, taps = col_ref.shape
    copies = [
        pltpu.make_async_copy(source, target, sems.at[slot])
        for slot, (source, target) in enumerate(
            ((weights_hbm, weights_ref), (col_hbm, col_ref), (row_hbm, row_ref))
        )
    ]
    for copy in copies:
        copy.start()
    t, l = index_pair((taps, 2 * LANES))
    pick = jnp.where((l == t) | (l == LANES + taps - 1 - t), 1.0, 0.0).astype(BF16)
    for copy in copies:
        copy.wait()
    for k in range(kernels):
        flat_ref[4 * k : 4 * k + 2] = col_ref[k].astype(F32)
        flat_ref[4 * k + 2 : 4 * k + 4] = row_ref[k].astype(F32)
    rows = jnp.dot(flat_ref[...].astype(BF16), pick, preferred_element_type=F32)
    for k in range(kernels):
        out_ref[k, 0:4] = rows[4 * k : 4 * k + 4]
        out_ref[k, 4:8] = jnp.full((4, 2 * LANES), weights_ref[k], F32)


def prepare_kernel(
    params_hbm, target_hbm, params_ref, mask_ref, code_ref, ahead_ref, behind_ref, target_ref, sems
):
    rows = params_ref.shape[0]
    wide = 2 * HALF
    copies = [
        pltpu.make_async_copy(params_hbm, params_ref, sems.at[0]),
        pltpu.make_async_copy(target_hbm, target_ref, sems.at[1]),
    ]
    for copy in copies:
        copy.start()
    for copy in copies:
        copy.wait()
    mask = jax.nn.sigmoid(mask_slope * params_ref[...]).astype(BF16)
    code = (target_ref[...] + 1).astype(F32).astype(BF16)
    mask_ref[...] = mask
    code_ref[...] = code

    def edges(down_ref, up_ref):
        down_ref[0:wide, :] = mask[rows - wide :]
        down_ref[wide:, :] = code[rows - HALF :]
        up_ref[0:wide, :] = mask[0:wide]
        up_ref[wide:, :] = code[0:HALF]

    pl.when(jnp.logical_not(turned_tile()))(lambda: edges(ahead_ref, behind_ref))
    pl.when(turned_tile())(lambda: edges(behind_ref, ahead_ref))


def unless(end, values):
    return jnp.where(end, 0.0, values.astype(F32))


def at_start(axis):
    return lax.axis_index(axis) == 0


def at_end(axis):
    return lax.axis_index(axis) == lax.axis_size(axis) - 1


def turned_tile():
    return lax.axis_index("tiles") % 2 == 1


def assemble_kernel(
    mask_ref, code_ref, behind_ref, ahead_ref, _, centre_ref, code_out_ref, *side_refs
):
    rows, cols = mask_ref.shape
    wide = 2 * HALF
    turn = turned_tile()
    behind, ahead = behind_ref[...].astype(F32), ahead_ref[...].astype(F32)
    above = unless(at_start("strip"), jnp.where(turn, ahead, behind))
    below = unless(at_end("strip"), jnp.where(turn, behind, ahead))
    tall = jnp.concatenate([above[0:wide], mask_ref[...].astype(F32), below[0:wide]], axis=0)
    turned = tall.T.astype(BF16)
    code = jnp.concatenate(
        [above[wide:], code_ref[...].astype(F32), below[wide:], jnp.zeros((wide, cols), F32)], axis=0
    )
    code = code.T.astype(BF16)
    centre_ref[...] = turned
    code_out_ref[...] = code

    def right(ref):
        ref[0:wide, :] = turned[cols - wide :, :]
        ref[wide:, :] = code[cols - HALF :, :]

    def left(ref):
        ref[0:wide, :] = turned[0:wide, :]
        ref[wide:, :] = code[0:HALF, :]

    if len(side_refs) == 2:
        right(side_refs[0])
        left(side_refs[1])
    else:
        pl.when(at_start("col"))(lambda: right(side_refs[0]))
        pl.when(at_end("col"))(lambda: left(side_refs[0]))


def forward_kernel(
    centre_ref,
    before_ref,
    after_ref,
    taps_ref,
    field_ref,
    intensity_ref,
    mask_ref,
    total_ref,
    masks_ref,
    table_ref,
    columns_ref,
):
    kernels = taps_ref.shape[0]
    units = columns_ref.shape[0]
    cols = centre_ref.shape[0]
    wide = 2 * HALF
    long = centre_ref.shape[1]
    tiles = long // LANES
    blocks = cols // wide + 1
    span = cols + wide

    mask = jnp.concatenate(
        [
            unless(at_start("col"), before_ref[0:wide, :]).astype(BF16),
            centre_ref[...],
            unless(at_end("col"), after_ref[0:wide, :]).astype(BF16),
        ],
        axis=0,
    )
    for block in range(blocks):
        mask_ref[:, block * long : (block + 1) * long] = mask[block * wide : block * wide + LANES]
    total_ref[...] = jnp.zeros_like(total_ref)
    write_masks(masks_ref)

    def group(step, carry):
        for unit in range(units):
            for part in range(2):
                row = taps_ref[step * units + unit, part : part + 1, 0:LANES]
                base = circulant(row, 0)[0:wide]
                at = (unit * 2 + part) * wide
                table_ref[at : at + wide, :] = base * masks_ref[0, 0:wide]
        columns = jnp.dot(table_ref[...], mask_ref[...], preferred_element_type=F32).astype(BF16)
        for unit in range(units):
            for part in range(2):
                at = (unit * 2 + part) * wide
                for block in range(blocks):
                    for t in range(tiles):
                        lane = block * long + t * LANES
                        to = t * span + block * wide
                        columns_ref[unit, to : to + wide, part * LANES : (part + 1) * LANES] = columns[
                            at : at + wide, lane : lane + LANES
                        ]
        for unit in range(units):
            kernel = step * units + unit
            near, far = [], []
            for part in range(2):
                base = circulant(taps_ref[kernel, 2 + part : 3 + part, LANES:], LANES // 2)
                near.append(base * masks_ref[2])
                far.append(base * masks_ref[3])
            near = [
                jnp.concatenate([near[0], near[1]], axis=1),
                jnp.concatenate([-near[1], near[0]], axis=1),
            ]
            far = [
                jnp.concatenate([far[0], far[1]], axis=1),
                jnp.concatenate([-far[1], far[0]], axis=1),
            ]
            weight = taps_ref[kernel, 4:5, :]
            edge = (tiles - 1) * span
            window = jnp.concatenate([columns_ref[unit, 0:edge], columns_ref[unit, span:]], axis=1)
            inner = jnp.dot(window, jnp.concatenate(near + far, axis=0), preferred_element_type=F32)
            outer = jnp.dot(
                columns_ref[unit, edge:], jnp.concatenate(near, axis=0), preferred_element_type=F32
            )
            for t in range(tiles):
                part = inner[t * span : (t + 1) * span] if t + 1 < tiles else outer
                scaled = weight * part
                field_ref[kernel, t] = scaled.astype(field_ref.dtype)
                total_ref[t] += scaled * part
        return carry

    lax.fori_loop(0, kernels // units, group, 0)
    for t in range(tiles):
        intensity_ref[t] = total_ref[t, :, 0:LANES] + total_ref[t, :, LANES:]


def backward_kernel(
    own_ref,
    other_ref,
    code_ref,
    code_before_ref,
    code_after_ref,
    params_ref,
    field_ref,
    taps_ref,
    gradient_ref,
    resist_hbm,
    sums_ref,
    slope_ref,
    descent_ref,
    resist_ref,
    masks_ref,
    table_ref,
    source_ref,
    sem,
):
    kernels = taps_ref.shape[0]
    cols = code_ref.shape[0]
    wide = 2 * HALF
    tiles = own_ref.shape[0]
    span = cols + wide
    rows = (tiles - 1) * LANES
    units = table_ref.shape[1] // (2 * span)

    resists, loss = [], 0.0
    for t in range(tiles):
        lanes = slice(t * LANES, (t + 1) * LANES)
        code = jnp.concatenate(
            [
                unless(at_start("col"), code_before_ref[wide:, lanes]),
                code_ref[:, lanes].astype(F32),
                unless(at_end("col"), code_after_ref[wide:, lanes]),
            ],
            axis=0,
        )
        summed = own_ref[t] + other_ref[t]
        resist = jax.nn.sigmoid(resist_steep * (summed - resist_level))
        mismatch = resist - (code - 1.0)
        slope = 4.0 * mismatch * resist_steep * resist * (1.0 - resist)
        slope = jnp.where(code > 0.5, slope, 0.0).astype(BF16)
        slope_ref[t] = jnp.concatenate([slope, slope], axis=1)
        resists.append(resist[HALF : HALF + cols])
        mine = mismatch[HALF : HALF + cols]
        _, lane = index_pair(mine.shape)
        lane = lane + t * LANES
        mine = jnp.where((lane >= HALF) & (lane < HALF + rows), mine, 0.0)
        loss = loss + mine * mine
    resist_ref[...] = jnp.concatenate(resists, axis=1).T[HALF : HALF + rows]
    copy = pltpu.make_async_copy(resist_ref, resist_hbm, sem)
    copy.start()
    descent_ref[...] = jnp.zeros_like(descent_ref)
    write_masks(masks_ref)

    def group(step, carry):
        a, b = index_pair((LANES, LANES))
        inside = jnp.where(b < wide, b, b - wide) < a
        for unit in range(units):
            kernel = step * units + unit
            near, far = [], []
            for part in range(2):
                base = circulant(taps_ref[kernel, 2 + part : 3 + part, 0:LANES], LANES // 2)
                near.append(base * masks_ref[2])
                far.append(base * masks_ref[3])
            table = jnp.concatenate(
                [
                    jnp.concatenate([near[0], -near[1]], axis=1),
                    jnp.concatenate([near[1], near[0]], axis=1),
                    jnp.concatenate([far[0], -far[1]], axis=1),
                    jnp.concatenate([far[1], far[0]], axis=1),
                ],
                axis=0,
            )
            products = [slope_ref[t] * field_ref[kernel, t] for t in range(tiles)]
            window = jnp.concatenate(
                [jnp.concatenate(products[:-1], axis=0), jnp.concatenate(products[1:], axis=0)], axis=1
            )
            returned = jnp.dot(window, table, preferred_element_type=F32).astype(BF16)
            at = unit * 2 * span
            for t in range(tiles - 1):
                to = slice(t * LANES, (t + 1) * LANES)
                for part in range(2):
                    piece = returned[t * span : (t + 1) * span, part * LANES : (part + 1) * LANES]
                    source_ref[at + part * cols : at + (part + 1) * cols, to] = piece[0:cols]
                    tail = at + 2 * cols + part * wide
                    source_ref[tail : tail + wide, to] = piece[cols:]
            turned = []
            for part in range(2):
                row = taps_ref[kernel, part : part + 1, LANES:]
                table_ref[:, at + part * LANES : at + (part + 1) * LANES] = circulant(row, 0) * masks_ref[0]
                spread = jnp.broadcast_to(row, (LANES, LANES))
                turned.append(pltpu.roll(spread, part * wide, 1, stride=1, stride_axis=0))
            both = jnp.where(b < wide, turned[0], turned[1])
            table_ref[:, at + 2 * LANES : at + 3 * LANES] = jnp.where(inside, both, 0.0).astype(BF16)
            if unit % CHUNK == CHUNK - 1:
                chunk = slice((unit + 1 - CHUNK) * 2 * span, (unit + 1) * 2 * span)
                descent_ref[...] += jnp.dot(
                    table_ref[:, chunk], source_ref[chunk, :], preferred_element_type=F32
                )
        return carry

    lax.fori_loop(0, kernels // units, group, 0)
    mask = jax.nn.sigmoid(mask_slope * params_ref[...])
    gradient = descent_ref[...].T * mask_slope * mask * (1.0 - mask)
    gradient_ref[...] = gradient
    sums_ref[0:1, :] = jnp.broadcast_to(jnp.sum(gradient * gradient), (1, LANES))
    sums_ref[1:2, :] = jnp.broadcast_to(jnp.sum(loss), (1, LANES))
    copy.wait()


def finish_kernel(params_ref, gradient_ref, sums_ref, new_ref, loss_ref, *, count):
    mean = sums_ref[...] * (1.0 / count)
    scale = step_length / jnp.sqrt(mean[0:1] + norm_eps)
    new_ref[...] = params_ref[...] - gradient_ref[...] * scale
    loss_ref[...] = mean[1:2]


def shards(mask_params, target, col_taps, row_taps, kernel_weights):
    rows, cols = target.shape
    kernels, _, taps = col_taps.shape
    wide = 2 * HALF
    tiles = rows // LANES + 1
    long, span = tiles * LANES, cols + wide
    units, back_units = FORWARD_UNROLL, BACKWARD_UNROLL
    if cols != LANES or rows % LANES or taps != wide + 1 or kernels % units or kernels % back_units:
        raise ValueError("block shape")
    vmem = pl.BlockSpec(memory_space=pltpu.VMEM)
    hbm = pl.BlockSpec(memory_space=pltpu.HBM)
    array = jax.ShapeDtypeStruct

    def call(body, name, specs, outs, out_specs=None, scratch=(), grant=4 * 2**20, flops=10**6):
        return pl.pallas_call(
            body,
            in_specs=specs,
            out_shape=outs,
            out_specs=[vmem] * len(outs) if out_specs is None else out_specs,
            scratch_shapes=scratch,
            compiler_params=pltpu.CompilerParams(vmem_limit_bytes=grant),
            cost_estimate=pl.CostEstimate(flops=flops, bytes_accessed=10**6, transcendentals=0),
            name=name,
        )

    plain, edge = array((rows, cols), BF16), array((wide + HALF, cols), BF16)
    full = array((rows, cols), F32)
    sides, strips = lax.axis_size("col"), lax.axis_size("strip")
    params, mask_half, code, ahead, behind = call(
        prepare_kernel,
        "prepare",
        [hbm, hbm],
        (full, plain, plain, edge, edge),
        scratch=[pltpu.VMEM((rows, cols), target.dtype), pltpu.SemaphoreType.DMA((2,))],
    )(stay(mask_params[0]), stay(target))
    from_behind = lax.ppermute(ahead, ("tiles", "strip"), snake(1))
    from_ahead = lax.ppermute(behind, ("tiles", "strip"), snake(-1))
    (tap_rows,) = call(
        taps_kernel,
        "taps",
        [hbm] * 3,
        (array((kernels, 8, 2 * LANES), F32),),
        scratch=[
            pltpu.SMEM(kernel_weights.shape, F32),
            pltpu.VMEM(col_taps.shape, BF16),
            pltpu.VMEM(row_taps.shape, BF16),
            pltpu.VMEM((4 * kernels, taps), F32),
            pltpu.SemaphoreType.DMA((3,)),
        ],
        flops=10**8,
    )(stay(kernel_weights), stay(col_taps), stay(row_taps))

    side, turned = array((wide + HALF, long), BF16), array((cols, long), BF16)
    centre, code_turned, *messages = call(
        assemble_kernel,
        "assemble",
        [vmem] * 4 + [pl.BlockSpec(memory_space=pl.ANY)],
        (turned, turned) + (side,) * (1 if sides == 2 else 2),
    )(mask_half, code, from_behind, from_ahead, tap_rows)
    if sides == 2:
        before = after = lax.ppermute(messages[0], "col", ring("col", 1))
    else:
        before = lax.ppermute(messages[0], "col", ring("col", 1))
        after = lax.ppermute(messages[1], "col", ring("col", -1))

    masks = pltpu.VMEM((4, LANES, LANES), BF16)
    plane = (tiles, span, LANES)
    field, intensity = call(
        forward_kernel,
        "forward",
        [vmem] * 4,
        (array((kernels, tiles, span, 2 * LANES), BF16), array(plane, F32)),
        scratch=[
            pltpu.VMEM((LANES, (cols // wide + 1) * long), BF16),
            pltpu.VMEM((tiles, span, 2 * LANES), F32),
            masks,
            pltpu.VMEM((units * 2 * wide, LANES), BF16),
            pltpu.VMEM((units, tiles * span, 2 * LANES), BF16),
        ],
        grant=VMEM,
    )(centre, before, after, tap_rows)

    other = lax.ppermute(intensity, "expo", [(0, 1), (1, 0)])

    gradient, resist, sums = call(
        backward_kernel,
        "backward",
        [vmem] * 8,
        (full, full, array((2, LANES), F32)),
        out_specs=[vmem, hbm, vmem],
        scratch=[
            pltpu.VMEM((tiles, span, 2 * LANES), BF16),
            pltpu.VMEM((cols, rows), F32),
            pltpu.VMEM((rows, cols), F32),
            masks,
            pltpu.VMEM((cols, back_units * 2 * span), BF16),
            pltpu.VMEM((back_units * 2 * span, rows), BF16),
            pltpu.SemaphoreType.DMA,
        ],
        grant=VMEM,
    )(intensity, other, code_turned, before, after, params, field, tap_rows)

    sums = sums + lax.ppermute(sums, "expo", [(0, 1), (1, 0)])
    for axis in ("col", "strip"):
        sums = total_over(sums, axis)
    count = 2 * rows * cols * strips * sides
    new_params, loss = call(
        functools.partial(finish_kernel, count=count), "finish", [vmem] * 3, (full, array((1, LANES), F32))
    )(params, gradient, sums)
    return (new_params[None], resist, loss[0, 0:1])


def solution(mesh):
    if mesh.shape["expo"] != 2:
        raise ValueError("two exposures")
    return jax.shard_map(
        shards,
        mesh=mesh,
        in_specs=(
            P("expo", ("tiles", "strip"), "col"),
            P(("tiles", "strip"), "col"),
            P(),
            P(),
            P(),
        ),
        out_specs=(P("expo", ("tiles", "strip"), "col"), P(("tiles", "strip"), "col"), P("tiles")),
        check_vma=False,
    )
```

```python
import functools
import jax
import jax.numpy as jnp
from jax import lax
from jax.experimental import pallas as pl
from jax.experimental.pallas import tpu as pltpu
from jax.sharding import PartitionSpec as P

HALF = 32
LANES = 128
BACKWARD_UNROLL = 12
CHUNK = 4
VMEM = 24 * 2**20

mask_slope = 4.0
resist_steep = 4.0
resist_level = 3.0
step_length = 0.5
norm_eps = 1e-06

BF16 = jnp.bfloat16
F32 = jnp.float32


def stay(array):
    return pltpu.with_memory_space_constraint(array, pltpu.HBM)


def ring(axis, step):
    peers = lax.axis_size(axis)
    return [(i, (i + step) % peers) for i in range(peers)]


def snake(step):
    tiles, strips = lax.axis_size("tiles"), lax.axis_size("strip")
    order = []
    for tile in range(tiles):
        levels = range(strips) if tile % 2 == 0 else reversed(range(strips))
        order += [tile * strips + level for level in levels]
    return [(device, order[(i + step) % len(order)]) for i, device in enumerate(order)]


def partners(peers, other):
    return [(2 * i + core, 2 * other(i) + 1 - core) for i in range(peers) for core in range(2)]


def total_over(value, axis):
    peers = lax.axis_size(axis)
    if peers & (peers - 1):
        return lax.psum(value, axis)
    both = (axis, "expo")
    if peers == 4:
        one, two, three = (
            lax.ppermute(value, both, partners(peers, lambda i, d=d: i ^ d)) for d in (1, 2, 3)
        )
        return (value + two) + (one + three)
    reach = 1
    while reach < peers:
        value = value + lax.ppermute(value, both, partners(peers, lambda i, r=reach: i ^ r))
        reach *= 2
    return value


def circulant(row, shift):
    spread = jnp.broadcast_to(row, (LANES, LANES))
    return pltpu.roll(spread, shift, 1, stride=1, stride_axis=0).astype(BF16)


def index_pair(shape):
    return lax.broadcasted_iota(jnp.int32, shape, 0), lax.broadcasted_iota(jnp.int32, shape, 1)


def write_masks(masks_ref):
    a, b = index_pair((LANES, LANES))
    one, zero = jnp.ones((LANES, LANES), F32), jnp.zeros((LANES, LANES), F32)
    for slot, keep in enumerate((b >= a, b < a, a >= b, a < b)):
        masks_ref[slot] = jnp.where(keep, one, zero).astype(BF16)


def taps_kernel(weights_hbm, col_hbm, row_hbm, out_ref, weights_ref, col_ref, row_ref, flat_ref, sems):
    kernels, _, taps = col_ref.shape
    copies = [
        pltpu.make_async_copy(source, target, sems.at[slot])
        for slot, (source, target) in enumerate(
            ((weights_hbm, weights_ref), (col_hbm, col_ref), (row_hbm, row_ref))
        )
    ]
    for copy in copies:
        copy.start()
    t, l = index_pair((taps, 2 * LANES))
    pick = jnp.where((l == t) | (l == LANES + taps - 1 - t), 1.0, 0.0).astype(BF16)
    for copy in copies:
        copy.wait()
    for k in range(kernels):
        flat_ref[4 * k : 4 * k + 2] = col_ref[k].astype(F32)
        flat_ref[4 * k + 2 : 4 * k + 4] = row_ref[k].astype(F32)
    rows = jnp.dot(flat_ref[...].astype(BF16), pick, preferred_element_type=F32)
    for k in range(kernels):
        out_ref[k, 0:4] = rows[4 * k : 4 * k + 4]
        out_ref[k, 4:8] = jnp.full((4, 2 * LANES), weights_ref[k], F32)


def prepare_kernel(
    params_hbm, target_hbm, params_ref, mask_ref, code_ref, ahead_ref, behind_ref, target_ref, sems
):
    rows = params_ref.shape[0]
    wide = 2 * HALF
    copies = [
        pltpu.make_async_copy(params_hbm, params_ref, sems.at[0]),
        pltpu.make_async_copy(target_hbm, target_ref, sems.at[1]),
    ]
    for copy in copies:
        copy.start()
    for copy in copies:
        copy.wait()
    mask = jax.nn.sigmoid(mask_slope * params_ref[...]).astype(BF16)
    code = (target_ref[...] + 1).astype(F32).astype(BF16)
    mask_ref[...] = mask
    code_ref[...] = code

    def edges(down_ref, up_ref):
        down_ref[0:wide, :] = mask[rows - wide :]
        down_ref[wide:, :] = code[rows - HALF :]
        up_ref[0:wide, :] = mask[0:wide]
        up_ref[wide:, :] = code[0:HALF]

    pl.when(jnp.logical_not(turned_tile()))(lambda: edges(ahead_ref, behind_ref))
    pl.when(turned_tile())(lambda: edges(behind_ref, ahead_ref))


def unless(end, values):
    return jnp.where(end, 0.0, values.astype(F32))


def at_start(axis):
    return lax.axis_index(axis) == 0


def at_end(axis):
    return lax.axis_index(axis) == lax.axis_size(axis) - 1


def turned_tile():
    return lax.axis_index("tiles") % 2 == 1


def assemble_kernel(
    mask_ref, code_ref, behind_ref, ahead_ref, _, centre_ref, code_out_ref, *side_refs
):
    rows, cols = mask_ref.shape
    wide = 2 * HALF
    turn = turned_tile()
    behind, ahead = behind_ref[...].astype(F32), ahead_ref[...].astype(F32)
    above = unless(at_start("strip"), jnp.where(turn, ahead, behind))
    below = unless(at_end("strip"), jnp.where(turn, behind, ahead))
    tall = jnp.concatenate([above[0:wide], mask_ref[...].astype(F32), below[0:wide]], axis=0)
    turned = tall.T.astype(BF16)
    code = jnp.concatenate(
        [above[wide:], code_ref[...].astype(F32), below[wide:], jnp.zeros((wide, cols), F32)], axis=0
    )
    code = code.T.astype(BF16)
    centre_ref[...] = turned
    code_out_ref[...] = code

    def right(ref):
        ref[0:wide, :] = turned[cols - wide :, :]
        ref[wide:, :] = code[cols - HALF :, :]

    def left(ref):
        ref[0:wide, :] = turned[0:wide, :]
        ref[wide:, :] = code[0:HALF, :]

    if len(side_refs) == 2:
        right(side_refs[0])
        left(side_refs[1])
    else:
        pl.when(at_start("col"))(lambda: right(side_refs[0]))
        pl.when(at_end("col"))(lambda: left(side_refs[0]))


def correlate(taps_ref, source_ref, field_ref, total_ref, masks_ref, table_ref, columns_ref):
    kernels = taps_ref.shape[0]
    tiles, span = field_ref.shape[1:3]
    wide = 2 * HALF
    long = tiles * LANES
    total_ref[...] = jnp.zeros_like(total_ref)
    write_masks(masks_ref)
    for kernel in range(kernels):
        for part in range(2):
            base = circulant(taps_ref[kernel, part : part + 1, 0:LANES], 0)[0:wide]
            at = (kernel * 2 + part) * wide
            table_ref[at : at + wide, :] = base * masks_ref[0, 0:wide]
    columns = jnp.dot(table_ref[...], source_ref[...], preferred_element_type=F32).astype(BF16)
    for kernel in range(kernels):
        for part in range(2):
            at = (kernel * 2 + part) * wide
            for block in range(span // wide):
                for t in range(tiles):
                    lane = block * long + t * LANES
                    to = t * span + block * wide
                    columns_ref[kernel, to : to + wide, part * LANES : (part + 1) * LANES] = columns[
                        at : at + wide, lane : lane + LANES
                    ]
    edge = (tiles - 1) * span
    for kernel in range(kernels):
        near, far = [], []
        for part in range(2):
            base = circulant(taps_ref[kernel, 2 + part : 3 + part, LANES:], LANES // 2)
            near.append(base * masks_ref[2])
            far.append(base * masks_ref[3])
        near = [
            jnp.concatenate([near[0], near[1]], axis=1),
            jnp.concatenate([-near[1], near[0]], axis=1),
        ]
        far = [
            jnp.concatenate([far[0], far[1]], axis=1),
            jnp.concatenate([-far[1], far[0]], axis=1),
        ]
        weight = taps_ref[kernel, 4:5, :]
        window = jnp.concatenate([columns_ref[kernel, 0:edge], columns_ref[kernel, span:]], axis=1)
        inner = jnp.dot(window, jnp.concatenate(near + far, axis=0), preferred_element_type=F32)
        outer = jnp.dot(columns_ref[kernel, edge:], jnp.concatenate(near, axis=0), preferred_element_type=F32)
        for t in range(tiles):
            part = inner[t * span : (t + 1) * span] if t + 1 < tiles else outer
            scaled = weight * part
            field_ref[kernel, t] = scaled.astype(field_ref.dtype)
            total_ref[t] += scaled * part


def middle_kernel(centre_ref, taps_ref, field_ref, intensity_ref, total_ref, *scratch):
    correlate(taps_ref, centre_ref, field_ref, total_ref, *scratch)
    for t in range(total_ref.shape[0]):
        intensity_ref[t] = total_ref[t, :, 0:LANES] + total_ref[t, :, LANES:]


def side_kernel(
    centre_ref, before_ref, after_ref, taps_ref, middle_ref, field_ref, intensity_ref, total_ref, source_ref, *scratch
):
    wide = 2 * HALF
    cols, long = centre_ref.shape
    source_ref[0:wide, 0:long] = unless(at_start("col"), before_ref[0:wide, :]).astype(BF16)
    source_ref[wide:, 0:long] = centre_ref[0:wide, :]
    source_ref[0:wide, long:] = centre_ref[cols - wide :, :]
    source_ref[wide:, long:] = unless(at_end("col"), after_ref[0:wide, :]).astype(BF16)
    correlate(taps_ref, source_ref, field_ref, total_ref, *scratch)
    for t in range(total_ref.shape[0]):
        intensity = total_ref[t, :, 0:LANES] + total_ref[t, :, LANES:]
        intensity_ref[t, 0:wide] = intensity[0:wide]
        intensity_ref[t, wide : 2 * wide] = middle_ref[t]
        intensity_ref[t, 2 * wide :] = intensity[wide:]


def backward_kernel(
    own_ref,
    other_ref,
    code_ref,
    code_before_ref,
    code_after_ref,
    params_ref,
    middle_ref,
    side_ref,
    taps_ref,
    gradient_ref,
    resist_hbm,
    sums_ref,
    slope_ref,
    descent_ref,
    resist_ref,
    masks_ref,
    table_ref,
    source_ref,
    sem,
):
    kernels = taps_ref.shape[0]
    cols = code_ref.shape[0]
    wide = 2 * HALF
    tiles = own_ref.shape[0]
    span = cols + wide
    rows = (tiles - 1) * LANES
    units = table_ref.shape[1] // (2 * span)

    resists, loss = [], 0.0
    for t in range(tiles):
        lanes = slice(t * LANES, (t + 1) * LANES)
        code = jnp.concatenate(
            [
                unless(at_start("col"), code_before_ref[wide:, lanes]),
                code_ref[:, lanes].astype(F32),
                unless(at_end("col"), code_after_ref[wide:, lanes]),
            ],
            axis=0,
        )
        summed = own_ref[t] + other_ref[t]
        resist = jax.nn.sigmoid(resist_steep * (summed - resist_level))
        mismatch = resist - (code - 1.0)
        slope = 4.0 * mismatch * resist_steep * resist * (1.0 - resist)
        slope = jnp.where(code > 0.5, slope, 0.0).astype(BF16)
        slope_ref[t] = jnp.concatenate([slope, slope], axis=1)
        resists.append(resist[HALF : HALF + cols])
        mine = mismatch[HALF : HALF + cols]
        _, lane = index_pair(mine.shape)
        lane = lane + t * LANES
        mine = jnp.where((lane >= HALF) & (lane < HALF + rows), mine, 0.0)
        loss = loss + mine * mine
    resist_ref[...] = jnp.concatenate(resists, axis=1).T[HALF : HALF + rows]
    copy = pltpu.make_async_copy(resist_ref, resist_hbm, sem)
    copy.start()
    descent_ref[...] = jnp.zeros_like(descent_ref)
    write_masks(masks_ref)

    def group(step, carry):
        a, b = index_pair((LANES, LANES))
        inside = jnp.where(b < wide, b, b - wide) < a
        for unit in range(units):
            kernel = step * units + unit
            near, far = [], []
            for part in range(2):
                base = circulant(taps_ref[kernel, 2 + part : 3 + part, 0:LANES], LANES // 2)
                near.append(base * masks_ref[2])
                far.append(base * masks_ref[3])
            table = jnp.concatenate(
                [
                    jnp.concatenate([near[0], -near[1]], axis=1),
                    jnp.concatenate([near[1], near[0]], axis=1),
                    jnp.concatenate([far[0], -far[1]], axis=1),
                    jnp.concatenate([far[1], far[0]], axis=1),
                ],
                axis=0,
            )
            products = [
                slope_ref[t]
                * jnp.concatenate(
                    [side_ref[kernel, t, 0:wide], middle_ref[kernel, t], side_ref[kernel, t, wide:]], axis=0
                )
                for t in range(tiles)
            ]
            window = jnp.concatenate(
                [jnp.concatenate(products[:-1], axis=0), jnp.concatenate(products[1:], axis=0)], axis=1
            )
            returned = jnp.dot(window, table, preferred_element_type=F32).astype(BF16)
            at = unit * 2 * span
            for t in range(tiles - 1):
                to = slice(t * LANES, (t + 1) * LANES)
                for part in range(2):
                    piece = returned[t * span : (t + 1) * span, part * LANES : (part + 1) * LANES]
                    source_ref[at + part * cols : at + (part + 1) * cols, to] = piece[0:cols]
                    tail = at + 2 * cols + part * wide
                    source_ref[tail : tail + wide, to] = piece[cols:]
            turned = []
            for part in range(2):
                row = taps_ref[kernel, part : part + 1, LANES:]
                table_ref[:, at + part * LANES : at + (part + 1) * LANES] = circulant(row, 0) * masks_ref[0]
                spread = jnp.broadcast_to(row, (LANES, LANES))
                turned.append(pltpu.roll(spread, part * wide, 1, stride=1, stride_axis=0))
            both = jnp.where(b < wide, turned[0], turned[1])
            table_ref[:, at + 2 * LANES : at + 3 * LANES] = jnp.where(inside, both, 0.0).astype(BF16)
            if unit % CHUNK == CHUNK - 1:
                chunk = slice((unit + 1 - CHUNK) * 2 * span, (unit + 1) * 2 * span)
                descent_ref[...] += jnp.dot(
                    table_ref[:, chunk], source_ref[chunk, :], preferred_element_type=F32
                )
        return carry

    lax.fori_loop(0, kernels // units, group, 0)
    mask = jax.nn.sigmoid(mask_slope * params_ref[...])
    gradient = descent_ref[...].T * mask_slope * mask * (1.0 - mask)
    gradient_ref[...] = gradient
    sums_ref[0:1, :] = jnp.broadcast_to(jnp.sum(gradient * gradient), (1, LANES))
    sums_ref[1:2, :] = jnp.broadcast_to(jnp.sum(loss), (1, LANES))
    copy.wait()


def finish_kernel(params_ref, gradient_ref, sums_ref, new_ref, loss_ref, *, count):
    mean = sums_ref[...] * (1.0 / count)
    scale = step_length / jnp.sqrt(mean[0:1] + norm_eps)
    new_ref[...] = params_ref[...] - gradient_ref[...] * scale
    loss_ref[...] = mean[1:2]


def shards(mask_params, target, col_taps, row_taps, kernel_weights):
    rows, cols = target.shape
    kernels, _, taps = col_taps.shape
    wide = 2 * HALF
    tiles = rows // LANES + 1
    long, span = tiles * LANES, cols + wide
    back_units = BACKWARD_UNROLL
    if cols != LANES or rows % LANES or taps != wide + 1 or kernels % back_units:
        raise ValueError("block shape")
    vmem = pl.BlockSpec(memory_space=pltpu.VMEM)
    hbm = pl.BlockSpec(memory_space=pltpu.HBM)
    array = jax.ShapeDtypeStruct

    def call(body, name, specs, outs, out_specs=None, scratch=(), grant=4 * 2**20, flops=10**6):
        return pl.pallas_call(
            body,
            in_specs=specs,
            out_shape=outs,
            out_specs=[vmem] * len(outs) if out_specs is None else out_specs,
            scratch_shapes=scratch,
            compiler_params=pltpu.CompilerParams(vmem_limit_bytes=grant),
            cost_estimate=pl.CostEstimate(flops=flops, bytes_accessed=10**6, transcendentals=0),
            name=name,
        )

    plain, edge = array((rows, cols), BF16), array((wide + HALF, cols), BF16)
    full = array((rows, cols), F32)
    sides, strips = lax.axis_size("col"), lax.axis_size("strip")
    params, mask_half, code, ahead, behind = call(
        prepare_kernel,
        "prepare",
        [hbm, hbm],
        (full, plain, plain, edge, edge),
        scratch=[pltpu.VMEM((rows, cols), target.dtype), pltpu.SemaphoreType.DMA((2,))],
    )(stay(mask_params[0]), stay(target))
    from_behind = lax.ppermute(ahead, ("tiles", "strip"), snake(1))
    from_ahead = lax.ppermute(behind, ("tiles", "strip"), snake(-1))
    (tap_rows,) = call(
        taps_kernel,
        "taps",
        [hbm] * 3,
        (array((kernels, 8, 2 * LANES), F32),),
        scratch=[
            pltpu.SMEM(kernel_weights.shape, F32),
            pltpu.VMEM(col_taps.shape, BF16),
            pltpu.VMEM(row_taps.shape, BF16),
            pltpu.VMEM((4 * kernels, taps), F32),
            pltpu.SemaphoreType.DMA((3,)),
        ],
        flops=10**8,
    )(stay(kernel_weights), stay(col_taps), stay(row_taps))

    side, turned = array((wide + HALF, long), BF16), array((cols, long), BF16)
    centre, code_turned, *messages = call(
        assemble_kernel,
        "assemble",
        [vmem] * 4 + [pl.BlockSpec(memory_space=pl.ANY)],
        (turned, turned) + (side,) * (1 if sides == 2 else 2),
    )(mask_half, code, from_behind, from_ahead, tap_rows)
    if sides == 2:
        before = after = lax.ppermute(messages[0], "col", ring("col", 1))
    else:
        before = lax.ppermute(messages[0], "col", ring("col", 1))
        after = lax.ppermute(messages[1], "col", ring("col", -1))

    masks = pltpu.VMEM((4, LANES, LANES), BF16)

    def part(width):
        fields = array((kernels, tiles, width, 2 * LANES), BF16)
        scratch = [
            masks,
            pltpu.VMEM((kernels * 2 * wide, LANES), BF16),
            pltpu.VMEM((kernels, tiles * width, 2 * LANES), BF16),
        ]
        return fields, pltpu.VMEM((tiles, width, 2 * LANES), F32), scratch

    fields, total, scratch = part(wide)
    middle, middle_intensity = call(
        middle_kernel,
        "middle",
        [vmem] * 2,
        (fields, array((tiles, wide, LANES), F32)),
        scratch=[total] + scratch,
        grant=VMEM,
        flops=4 * 10**9,
    )(centre, tap_rows)
    plane = (tiles, span, LANES)
    fields, total, scratch = part(2 * wide)
    sides_field, intensity = call(
        side_kernel,
        "side",
        [vmem] * 5,
        (fields, array(plane, F32)),
        scratch=[total, pltpu.VMEM((LANES, 2 * long), BF16)] + scratch,
        grant=VMEM,
    )(centre, before, after, tap_rows, middle_intensity)

    other = lax.ppermute(intensity, "expo", [(0, 1), (1, 0)])

    gradient, resist, sums = call(
        backward_kernel,
        "backward",
        [vmem] * 9,
        (full, full, array((2, LANES), F32)),
        out_specs=[vmem, hbm, vmem],
        scratch=[
            pltpu.VMEM((tiles, span, 2 * LANES), BF16),
            pltpu.VMEM((cols, rows), F32),
            pltpu.VMEM((rows, cols), F32),
            masks,
            pltpu.VMEM((cols, back_units * 2 * span), BF16),
            pltpu.VMEM((back_units * 2 * span, rows), BF16),
            pltpu.SemaphoreType.DMA,
        ],
        grant=VMEM,
    )(intensity, other, code_turned, before, after, params, middle, sides_field, tap_rows)

    sums = sums + lax.ppermute(sums, "expo", [(0, 1), (1, 0)])
    for axis in ("col", "strip"):
        sums = total_over(sums, axis)
    count = 2 * rows * cols * strips * sides
    new_params, loss = call(
        functools.partial(finish_kernel, count=count), "finish", [vmem] * 3, (full, array((1, LANES), F32))
    )(params, gradient, sums)
    return (new_params[None], resist, loss[0, 0:1])


def solution(mesh):
    if mesh.shape["expo"] != 2:
        raise ValueError("two exposures")
    return jax.shard_map(
        shards,
        mesh=mesh,
        in_specs=(
            P("expo", ("tiles", "strip"), "col"),
            P(("tiles", "strip"), "col"),
            P(),
            P(),
            P(),
        ),
        out_specs=(P("expo", ("tiles", "strip"), "col"), P(("tiles", "strip"), "col"), P("tiles")),
        check_vma=False,
    )
```

```python
import functools
import jax
import jax.numpy as jnp
from jax import lax
from jax.experimental import pallas as pl
from jax.experimental.pallas import tpu as pltpu
from jax.sharding import PartitionSpec as P

HALF = 32
LANES = 128
BACKWARD_UNROLL = 12
CHUNK = 6
VMEM = 24 * 2**20

mask_slope = 4.0
resist_steep = 4.0
resist_level = 3.0
step_length = 0.5
norm_eps = 1e-06

BF16 = jnp.bfloat16
F32 = jnp.float32


def stay(array):
    return pltpu.with_memory_space_constraint(array, pltpu.HBM)


def ring(axis, step):
    peers = lax.axis_size(axis)
    return [(i, (i + step) % peers) for i in range(peers)]


def snake(step):
    tiles, strips = lax.axis_size("tiles"), lax.axis_size("strip")
    order = []
    for tile in range(tiles):
        levels = range(strips) if tile % 2 == 0 else reversed(range(strips))
        order += [tile * strips + level for level in levels]
    return [(device, order[(i + step) % len(order)]) for i, device in enumerate(order)]


def partners(peers, other):
    return [(2 * i + core, 2 * other(i) + 1 - core) for i in range(peers) for core in range(2)]


def total_over(value, axis):
    peers = lax.axis_size(axis)
    if peers & (peers - 1):
        return lax.psum(value, axis)
    both = (axis, "expo")
    reach = 1
    while reach < peers:
        value = value + lax.ppermute(value, both, partners(peers, lambda i, r=reach: i ^ r))
        reach *= 2
    return value


def circulant(row, shift):
    spread = jnp.broadcast_to(row, (LANES, LANES))
    return pltpu.roll(spread, shift, 1, stride=1, stride_axis=0).astype(BF16)


def index_pair(shape):
    return lax.broadcasted_iota(jnp.int32, shape, 0), lax.broadcasted_iota(jnp.int32, shape, 1)


def write_masks(masks_ref):
    a, b = index_pair((LANES, LANES))
    one, zero = jnp.ones((LANES, LANES), F32), jnp.zeros((LANES, LANES), F32)
    for slot, keep in enumerate((b >= a, b < a, a >= b, a < b)):
        masks_ref[slot] = jnp.where(keep, one, zero).astype(BF16)


def mask_of(params):
    return jax.nn.sigmoid(mask_slope * params).astype(BF16)


def code_of(target):
    return (target + 1).astype(F32).astype(BF16)


def edges_kernel(params_hbm, target_hbm, ahead_ref, behind_ref, params_ref, target_ref, sems):
    rows = params_hbm.shape[0]
    wide = 2 * HALF
    copies = [
        pltpu.make_async_copy(source.at[pl.ds(start, size)], target.at[slot], sems.at[sem, slot])
        for sem, (source, target, size) in enumerate(
            ((params_hbm, params_ref, wide), (target_hbm, target_ref, HALF))
        )
        for slot, start in enumerate((0, rows - size))
    ]
    for copy in copies:
        copy.start()
    for copy in copies:
        copy.wait()

    def fill(refs):
        for slot, ref in enumerate(refs):
            ref[0:wide, :] = mask_of(params_ref[slot])
            ref[wide:, :] = code_of(target_ref[slot])

    pl.when(jnp.logical_not(turned_tile()))(lambda: fill((behind_ref, ahead_ref)))
    pl.when(turned_tile())(lambda: fill((ahead_ref, behind_ref)))


def load_kernel(
    params_hbm,
    target_hbm,
    weights_hbm,
    col_hbm,
    row_hbm,
    params_ref,
    mask_ref,
    code_ref,
    taps_ref,
    target_ref,
    weights_ref,
    col_ref,
    row_ref,
    flat_ref,
    sems,
):
    kernels, _, taps = col_ref.shape
    copies = [
        pltpu.make_async_copy(source, target, sems.at[slot])
        for slot, (source, target) in enumerate(
            (
                (weights_hbm, weights_ref),
                (col_hbm, col_ref),
                (row_hbm, row_ref),
                (params_hbm, params_ref),
                (target_hbm, target_ref),
            )
        )
    ]
    for copy in copies:
        copy.start()
    t, l = index_pair((taps, 2 * LANES))
    pick = jnp.where((l == t) | (l == LANES + taps - 1 - t), 1.0, 0.0).astype(BF16)
    for copy in copies:
        copy.wait()
    for k in range(kernels):
        flat_ref[4 * k : 4 * k + 2] = col_ref[k].astype(F32)
        flat_ref[4 * k + 2 : 4 * k + 4] = row_ref[k].astype(F32)
    rows = jnp.dot(flat_ref[...].astype(BF16), pick, preferred_element_type=F32)
    for k in range(kernels):
        taps_ref[k, 0:4] = rows[4 * k : 4 * k + 4]
        taps_ref[k, 4:8] = jnp.full((4, 2 * LANES), weights_ref[k], F32)
    mask_ref[...] = mask_of(params_ref[...])
    code_ref[...] = code_of(target_ref[...])


def unless(end, values):
    return jnp.where(end, 0.0, values.astype(F32))


def at_start(axis):
    return lax.axis_index(axis) == 0


def at_end(axis):
    return lax.axis_index(axis) == lax.axis_size(axis) - 1


def turned_tile():
    return lax.axis_index("tiles") % 2 == 1


def assemble_kernel(
    mask_ref, code_ref, behind_ref, ahead_ref, centre_ref, code_out_ref, *side_refs
):
    rows, cols = mask_ref.shape
    wide = 2 * HALF
    turn = turned_tile()
    behind, ahead = behind_ref[...].astype(F32), ahead_ref[...].astype(F32)
    above = unless(at_start("strip"), jnp.where(turn, ahead, behind))
    below = unless(at_end("strip"), jnp.where(turn, behind, ahead))
    tall = jnp.concatenate([above[0:wide], mask_ref[...].astype(F32), below[0:wide]], axis=0)
    turned = tall.T.astype(BF16)
    code = jnp.concatenate(
        [above[wide:], code_ref[...].astype(F32), below[wide:], jnp.zeros((wide, cols), F32)], axis=0
    )
    code = code.T.astype(BF16)
    centre_ref[...] = turned
    code_out_ref[...] = code

    def right(ref):
        ref[0:wide, :] = turned[cols - wide :, :]
        ref[wide:, :] = code[cols - HALF :, :]

    def left(ref):
        ref[0:wide, :] = turned[0:wide, :]
        ref[wide:, :] = code[0:HALF, :]

    if len(side_refs) == 2:
        right(side_refs[0])
        left(side_refs[1])
    else:
        pl.when(at_start("col"))(lambda: right(side_refs[0]))
        pl.when(at_end("col"))(lambda: left(side_refs[0]))


def correlate(taps_ref, source_ref, field_ref, total_ref, masks_ref, table_ref, columns_ref):
    kernels = taps_ref.shape[0]
    tiles, span = field_ref.shape[1:3]
    wide = 2 * HALF
    long = tiles * LANES
    total_ref[...] = jnp.zeros_like(total_ref)
    write_masks(masks_ref)
    for kernel in range(kernels):
        for part in range(2):
            base = circulant(taps_ref[kernel, part : part + 1, 0:LANES], 0)[0:wide]
            at = (kernel * 2 + part) * wide
            table_ref[at : at + wide, :] = base * masks_ref[0, 0:wide]
    columns = jnp.dot(table_ref[...], source_ref[...], preferred_element_type=F32).astype(BF16)
    for kernel in range(kernels):
        for part in range(2):
            at = (kernel * 2 + part) * wide
            for block in range(span // wide):
                for t in range(tiles):
                    lane = block * long + t * LANES
                    to = t * span + block * wide
                    columns_ref[kernel, to : to + wide, part * LANES : (part + 1) * LANES] = columns[
                        at : at + wide, lane : lane + LANES
                    ]
    edge = (tiles - 1) * span
    for kernel in range(kernels):
        near, far = [], []
        for part in range(2):
            base = circulant(taps_ref[kernel, 2 + part : 3 + part, LANES:], LANES // 2)
            near.append(base * masks_ref[2])
            far.append(base * masks_ref[3])
        near = [
            jnp.concatenate([near[0], near[1]], axis=1),
            jnp.concatenate([-near[1], near[0]], axis=1),
        ]
        far = [
            jnp.concatenate([far[0], far[1]], axis=1),
            jnp.concatenate([-far[1], far[0]], axis=1),
        ]
        weight = taps_ref[kernel, 4:5, :]
        window = jnp.concatenate([columns_ref[kernel, 0:edge], columns_ref[kernel, span:]], axis=1)
        inner = jnp.dot(window, jnp.concatenate(near + far, axis=0), preferred_element_type=F32)
        outer = jnp.dot(columns_ref[kernel, edge:], jnp.concatenate(near, axis=0), preferred_element_type=F32)
        for t in range(tiles):
            part = inner[t * span : (t + 1) * span] if t + 1 < tiles else outer
            scaled = weight * part
            field_ref[kernel, t] = scaled.astype(field_ref.dtype)
            total_ref[t] += scaled * part


def middle_kernel(centre_ref, taps_ref, field_ref, intensity_ref, total_ref, *scratch):
    correlate(taps_ref, centre_ref, field_ref, total_ref, *scratch)
    for t in range(total_ref.shape[0]):
        intensity_ref[t] = total_ref[t, :, 0:LANES] + total_ref[t, :, LANES:]


def side_kernel(
    centre_ref, before_ref, after_ref, taps_ref, middle_ref, field_ref, intensity_ref, total_ref, source_ref, *scratch
):
    wide = 2 * HALF
    cols, long = centre_ref.shape
    source_ref[0:wide, 0:long] = unless(at_start("col"), before_ref[0:wide, :]).astype(BF16)
    source_ref[wide:, 0:long] = centre_ref[0:wide, :]
    source_ref[0:wide, long:] = centre_ref[cols - wide :, :]
    source_ref[wide:, long:] = unless(at_end("col"), after_ref[0:wide, :]).astype(BF16)
    correlate(taps_ref, source_ref, field_ref, total_ref, *scratch)
    for t in range(total_ref.shape[0]):
        intensity = total_ref[t, :, 0:LANES] + total_ref[t, :, LANES:]
        intensity_ref[t, 0:wide] = intensity[0:wide]
        intensity_ref[t, wide : 2 * wide] = middle_ref[t]
        intensity_ref[t, 2 * wide :] = intensity[wide:]


def backward_kernel(
    own_ref,
    other_ref,
    code_ref,
    code_before_ref,
    code_after_ref,
    params_ref,
    middle_ref,
    side_ref,
    taps_ref,
    gradient_ref,
    resist_hbm,
    sums_ref,
    slope_ref,
    descent_ref,
    resist_ref,
    masks_ref,
    table_ref,
    source_ref,
    sem,
):
    kernels = taps_ref.shape[0]
    cols = code_ref.shape[0]
    wide = 2 * HALF
    tiles = own_ref.shape[0]
    span = cols + wide
    rows = (tiles - 1) * LANES
    units = table_ref.shape[1] // (2 * span)

    resists, loss = [], 0.0
    for t in range(tiles):
        lanes = slice(t * LANES, (t + 1) * LANES)
        code = jnp.concatenate(
            [
                unless(at_start("col"), code_before_ref[wide:, lanes]),
                code_ref[:, lanes].astype(F32),
                unless(at_end("col"), code_after_ref[wide:, lanes]),
            ],
            axis=0,
        )
        summed = own_ref[t] + other_ref[t]
        resist = jax.nn.sigmoid(resist_steep * (summed - resist_level))
        mismatch = resist - (code - 1.0)
        slope = 4.0 * mismatch * resist_steep * resist * (1.0 - resist)
        slope = jnp.where(code > 0.5, slope, 0.0).astype(BF16)
        slope_ref[t] = jnp.concatenate([slope, slope], axis=1)
        resists.append(resist[HALF : HALF + cols])
        mine = mismatch[HALF : HALF + cols]
        _, lane = index_pair(mine.shape)
        lane = lane + t * LANES
        mine = jnp.where((lane >= HALF) & (lane < HALF + rows), mine, 0.0)
        loss = loss + mine * mine
    resist_ref[...] = jnp.concatenate(resists, axis=1).T[HALF : HALF + rows]
    copy = pltpu.make_async_copy(resist_ref, resist_hbm, sem)
    copy.start()
    descent_ref[...] = jnp.zeros_like(descent_ref)
    write_masks(masks_ref)

    def group(step, carry):
        a, b = index_pair((LANES, LANES))
        inside = jnp.where(b < wide, b, b - wide) < a
        for unit in range(units):
            kernel = step * units + unit
            near, far = [], []
            for part in range(2):
                base = circulant(taps_ref[kernel, 2 + part : 3 + part, 0:LANES], LANES // 2)
                near.append(base * masks_ref[2])
                far.append(base * masks_ref[3])
            table = jnp.concatenate(
                [
                    jnp.concatenate([near[0], -near[1]], axis=1),
                    jnp.concatenate([near[1], near[0]], axis=1),
                    jnp.concatenate([far[0], -far[1]], axis=1),
                    jnp.concatenate([far[1], far[0]], axis=1),
                ],
                axis=0,
            )
            products = [
                slope_ref[t]
                * jnp.concatenate(
                    [side_ref[kernel, t, 0:wide], middle_ref[kernel, t], side_ref[kernel, t, wide:]], axis=0
                )
                for t in range(tiles)
            ]
            window = jnp.concatenate(
                [jnp.concatenate(products[:-1], axis=0), jnp.concatenate(products[1:], axis=0)], axis=1
            )
            returned = jnp.dot(window, table, preferred_element_type=F32).astype(BF16)
            at = unit * 2 * span
            for t in range(tiles - 1):
                to = slice(t * LANES, (t + 1) * LANES)
                for part in range(2):
                    piece = returned[t * span : (t + 1) * span, part * LANES : (part + 1) * LANES]
                    source_ref[at + part * cols : at + (part + 1) * cols, to] = piece[0:cols]
                    tail = at + 2 * cols + part * wide
                    source_ref[tail : tail + wide, to] = piece[cols:]
            turned = []
            for part in range(2):
                row = taps_ref[kernel, part : part + 1, LANES:]
                table_ref[:, at + part * LANES : at + (part + 1) * LANES] = circulant(row, 0) * masks_ref[0]
                spread = jnp.broadcast_to(row, (LANES, LANES))
                turned.append(pltpu.roll(spread, part * wide, 1, stride=1, stride_axis=0))
            both = jnp.where(b < wide, turned[0], turned[1])
            table_ref[:, at + 2 * LANES : at + 3 * LANES] = jnp.where(inside, both, 0.0).astype(BF16)
            if unit % CHUNK == CHUNK - 1:
                chunk = slice((unit + 1 - CHUNK) * 2 * span, (unit + 1) * 2 * span)
                descent_ref[...] += jnp.dot(
                    table_ref[:, chunk], source_ref[chunk, :], preferred_element_type=F32
                )
        return carry

    lax.fori_loop(0, kernels // units, group, 0)
    mask = jax.nn.sigmoid(mask_slope * params_ref[...])
    gradient = descent_ref[...].T * mask_slope * mask * (1.0 - mask)
    gradient_ref[...] = gradient
    sums_ref[0:1, :] = jnp.broadcast_to(jnp.sum(gradient * gradient), (1, LANES))
    sums_ref[1:2, :] = jnp.broadcast_to(jnp.sum(loss), (1, LANES))
    copy.wait()


def finish_kernel(params_ref, gradient_ref, sums_ref, new_ref, loss_ref, *, count):
    mean = sums_ref[...] * (1.0 / count)
    scale = step_length / jnp.sqrt(mean[0:1] + norm_eps)
    new_ref[...] = params_ref[...] - gradient_ref[...] * scale
    loss_ref[...] = mean[1:2]


def shards(mask_params, target, col_taps, row_taps, kernel_weights):
    rows, cols = target.shape
    kernels, _, taps = col_taps.shape
    wide = 2 * HALF
    tiles = rows // LANES + 1
    long, span = tiles * LANES, cols + wide
    back_units = BACKWARD_UNROLL
    if cols != LANES or rows % LANES or taps != wide + 1 or kernels % back_units:
        raise ValueError("block shape")
    vmem = pl.BlockSpec(memory_space=pltpu.VMEM)
    hbm = pl.BlockSpec(memory_space=pltpu.HBM)
    array = jax.ShapeDtypeStruct

    def call(body, name, specs, outs, out_specs=None, scratch=(), grant=4 * 2**20, flops=10**6):
        return pl.pallas_call(
            body,
            in_specs=specs,
            out_shape=outs,
            out_specs=[vmem] * len(outs) if out_specs is None else out_specs,
            scratch_shapes=scratch,
            compiler_params=pltpu.CompilerParams(vmem_limit_bytes=grant),
            cost_estimate=pl.CostEstimate(flops=flops, bytes_accessed=10**6, transcendentals=0),
            name=name,
        )

    plain, edge = array((rows, cols), BF16), array((wide + HALF, cols), BF16)
    full = array((rows, cols), F32)
    sides, strips = lax.axis_size("col"), lax.axis_size("strip")
    mine, goal = stay(mask_params[0]), stay(target)
    ahead, behind = call(
        edges_kernel,
        "edges",
        [hbm, hbm],
        (edge, edge),
        scratch=[
            pltpu.VMEM((2, wide, cols), F32),
            pltpu.VMEM((2, HALF, cols), target.dtype),
            pltpu.SemaphoreType.DMA((2, 2)),
        ],
    )(mine, goal)
    from_behind = lax.ppermute(ahead, ("tiles", "strip"), snake(1))
    from_ahead = lax.ppermute(behind, ("tiles", "strip"), snake(-1))
    params, mask_half, code, tap_rows = call(
        load_kernel,
        "load",
        [hbm] * 5,
        (full, plain, plain, array((kernels, 8, 2 * LANES), F32)),
        scratch=[
            pltpu.VMEM((rows, cols), target.dtype),
            pltpu.SMEM(kernel_weights.shape, F32),
            pltpu.VMEM(col_taps.shape, BF16),
            pltpu.VMEM(row_taps.shape, BF16),
            pltpu.VMEM((4 * kernels, taps), F32),
            pltpu.SemaphoreType.DMA((5,)),
        ],
        flops=10**8,
    )(mine, goal, stay(kernel_weights), stay(col_taps), stay(row_taps))

    side, turned = array((wide + HALF, long), BF16), array((cols, long), BF16)
    centre, code_turned, *messages = call(
        assemble_kernel,
        "assemble",
        [vmem] * 4,
        (turned, turned) + (side,) * (1 if sides == 2 else 2),
    )(mask_half, code, from_behind, from_ahead)
    if sides == 2:
        before = after = lax.ppermute(messages[0], "col", ring("col", 1))
    else:
        before = lax.ppermute(messages[0], "col", ring("col", 1))
        after = lax.ppermute(messages[1], "col", ring("col", -1))

    masks = pltpu.VMEM((4, LANES, LANES), BF16)

    def part(width):
        fields = array((kernels, tiles, width, 2 * LANES), BF16)
        scratch = [
            masks,
            pltpu.VMEM((kernels * 2 * wide, LANES), BF16),
            pltpu.VMEM((kernels, tiles * width, 2 * LANES), BF16),
        ]
        return fields, pltpu.VMEM((tiles, width, 2 * LANES), F32), scratch

    fields, total, scratch = part(wide)
    middle, middle_intensity = call(
        middle_kernel,
        "middle",
        [vmem] * 2,
        (fields, array((tiles, wide, LANES), F32)),
        scratch=[total] + scratch,
        grant=VMEM,
        flops=4 * 10**9,
    )(centre, tap_rows)
    plane = (tiles, span, LANES)
    fields, total, scratch = part(2 * wide)
    sides_field, intensity = call(
        side_kernel,
        "side",
        [vmem] * 5,
        (fields, array(plane, F32)),
        scratch=[total, pltpu.VMEM((LANES, 2 * long), BF16)] + scratch,
        grant=VMEM,
    )(centre, before, after, tap_rows, middle_intensity)

    other = lax.ppermute(intensity, "expo", [(0, 1), (1, 0)])

    gradient, resist, sums = call(
        backward_kernel,
        "backward",
        [vmem] * 9,
        (full, full, array((2, LANES), F32)),
        out_specs=[vmem, hbm, vmem],
        scratch=[
            pltpu.VMEM((tiles, span, 2 * LANES), BF16),
            pltpu.VMEM((cols, rows), F32),
            pltpu.VMEM((rows, cols), F32),
            masks,
            pltpu.VMEM((cols, back_units * 2 * span), BF16),
            pltpu.VMEM((back_units * 2 * span, rows), BF16),
            pltpu.SemaphoreType.DMA,
        ],
        grant=VMEM,
    )(intensity, other, code_turned, before, after, params, middle, sides_field, tap_rows)

    sums = sums + lax.ppermute(sums, "expo", [(0, 1), (1, 0)])
    for axis in ("col", "strip"):
        sums = total_over(sums, axis)
    count = 2 * rows * cols * strips * sides
    new_params, loss = call(
        functools.partial(finish_kernel, count=count), "finish", [vmem] * 3, (full, array((1, LANES), F32))
    )(params, gradient, sums)
    return (new_params[None], resist, loss[0, 0:1])


def solution(mesh):
    if mesh.shape["expo"] != 2:
        raise ValueError("two exposures")
    return jax.shard_map(
        shards,
        mesh=mesh,
        in_specs=(
            P("expo", ("tiles", "strip"), "col"),
            P(("tiles", "strip"), "col"),
            P(),
            P(),
            P(),
        ),
        out_specs=(P("expo", ("tiles", "strip"), "col"), P(("tiles", "strip"), "col"), P("tiles")),
        check_vma=False,
    )
```

```python
import functools
import jax
import jax.numpy as jnp
from jax import lax
from jax.experimental import pallas as pl
from jax.experimental.pallas import tpu as pltpu
from jax.sharding import PartitionSpec as P

HALF = 32
LANES = 128
BACKWARD_UNROLL = 12
CHUNK = 6
VMEM = 24 * 2**20

mask_slope = 4.0
resist_steep = 4.0
resist_level = 3.0
step_length = 0.5
norm_eps = 1e-06

BF16 = jnp.bfloat16
F32 = jnp.float32


def stay(array):
    return pltpu.with_memory_space_constraint(array, pltpu.HBM)


def ring(axis, step):
    peers = lax.axis_size(axis)
    return [(i, (i + step) % peers) for i in range(peers)]


def snake(step):
    tiles, strips = lax.axis_size("tiles"), lax.axis_size("strip")
    order = []
    for tile in range(tiles):
        levels = range(strips) if tile % 2 == 0 else reversed(range(strips))
        order += [tile * strips + level for level in levels]
    return [(device, order[(i + step) % len(order)]) for i, device in enumerate(order)]


def partners(peers, other):
    return [(2 * i + core, 2 * other(i) + 1 - core) for i in range(peers) for core in range(2)]


def total_over(value, axis):
    peers = lax.axis_size(axis)
    if peers & (peers - 1):
        return lax.psum(value, axis)
    both = (axis, "expo")
    reach = 1
    while reach < peers:
        value = value + lax.ppermute(value, both, partners(peers, lambda i, r=reach: i ^ r))
        reach *= 2
    return value


def circulant(row, shift):
    spread = jnp.broadcast_to(row, (LANES, LANES))
    return pltpu.roll(spread, shift, 1, stride=1, stride_axis=0).astype(BF16)


def index_pair(shape):
    return lax.broadcasted_iota(jnp.int32, shape, 0), lax.broadcasted_iota(jnp.int32, shape, 1)


def write_masks(masks_ref):
    a, b = index_pair((LANES, LANES))
    one, zero = jnp.ones((LANES, LANES), F32), jnp.zeros((LANES, LANES), F32)
    for slot, keep in enumerate((b >= a, b < a, a >= b, a < b)):
        masks_ref[slot] = jnp.where(keep, one, zero).astype(BF16)


def mask_of(params):
    return jax.nn.sigmoid(mask_slope * params).astype(BF16)


def code_of(target):
    return (target + 1).astype(F32).astype(BF16)


def edges_kernel(params_hbm, target_hbm, ahead_ref, behind_ref, params_ref, target_ref, sems):
    rows = params_hbm.shape[0]
    wide = 2 * HALF
    copies = [
        pltpu.make_async_copy(source.at[pl.ds(start, size)], target.at[slot], sems.at[sem, slot])
        for sem, (source, target, size) in enumerate(
            ((params_hbm, params_ref, wide), (target_hbm, target_ref, HALF))
        )
        for slot, start in enumerate((0, rows - size))
    ]
    for copy in copies:
        copy.start()
    for copy in copies:
        copy.wait()

    def fill(refs):
        for slot, ref in enumerate(refs):
            ref[0:wide, :] = mask_of(params_ref[slot])
            ref[wide:, :] = code_of(target_ref[slot])

    pl.when(jnp.logical_not(turned_tile()))(lambda: fill((behind_ref, ahead_ref)))
    pl.when(turned_tile())(lambda: fill((ahead_ref, behind_ref)))


def load_kernel(
    params_hbm,
    target_hbm,
    weights_hbm,
    col_hbm,
    row_hbm,
    params_ref,
    mask_ref,
    code_ref,
    taps_ref,
    near_ref,
    row_table_ref,
    target_ref,
    weights_ref,
    col_ref,
    row_ref,
    flat_ref,
    masks_ref,
    sems,
):
    kernels, _, taps = col_ref.shape
    copies = [
        pltpu.make_async_copy(source, target, sems.at[slot])
        for slot, (source, target) in enumerate(
            (
                (weights_hbm, weights_ref),
                (col_hbm, col_ref),
                (row_hbm, row_ref),
                (params_hbm, params_ref),
                (target_hbm, target_ref),
            )
        )
    ]
    for copy in copies:
        copy.start()
    t, l = index_pair((taps, 2 * LANES))
    pick = jnp.where((l == t) | (l == LANES + taps - 1 - t), 1.0, 0.0).astype(BF16)
    for copy in copies:
        copy.wait()
    for k in range(kernels):
        flat_ref[4 * k : 4 * k + 2] = col_ref[k].astype(F32)
        flat_ref[4 * k + 2 : 4 * k + 4] = row_ref[k].astype(F32)
    rows = jnp.dot(flat_ref[...].astype(BF16), pick, preferred_element_type=F32)
    for k in range(kernels):
        taps_ref[k, 0:4] = rows[4 * k : 4 * k + 4]
        taps_ref[k, 4:8] = jnp.full((4, 2 * LANES), weights_ref[k], F32)
    mask_ref[...] = mask_of(params_ref[...])
    code_ref[...] = code_of(target_ref[...])
    write_masks(masks_ref)
    wide = taps - 1
    for k in range(kernels):
        for part in range(2):
            at = (2 * k + part) * wide
            base = circulant(taps_ref[k, part : part + 1, 0:LANES], 0)[0:wide]
            near_ref[at : at + wide, :] = base * masks_ref[0, 0:wide]
        for half in range(2):
            zero, one = (
                circulant(taps_ref[k, 2 + part : 3 + part, LANES:], LANES // 2) * masks_ref[2 + half]
                for part in range(2)
            )
            at = half * 2 * LANES
            row_table_ref[k, at : at + LANES] = jnp.concatenate([zero, one], axis=1)
            row_table_ref[k, at + LANES : at + 2 * LANES] = jnp.concatenate([-one, zero], axis=1)


def unless(end, values):
    return jnp.where(end, 0.0, values.astype(F32))


def at_start(axis):
    return lax.axis_index(axis) == 0


def at_end(axis):
    return lax.axis_index(axis) == lax.axis_size(axis) - 1


def turned_tile():
    return lax.axis_index("tiles") % 2 == 1


def assemble_kernel(
    mask_ref, code_ref, behind_ref, ahead_ref, centre_ref, code_out_ref, *side_refs
):
    rows, cols = mask_ref.shape
    wide = 2 * HALF
    turn = turned_tile()
    behind, ahead = behind_ref[...].astype(F32), ahead_ref[...].astype(F32)
    above = unless(at_start("strip"), jnp.where(turn, ahead, behind))
    below = unless(at_end("strip"), jnp.where(turn, behind, ahead))
    tall = jnp.concatenate([above[0:wide], mask_ref[...].astype(F32), below[0:wide]], axis=0)
    turned = tall.T.astype(BF16)
    code = jnp.concatenate(
        [above[wide:], code_ref[...].astype(F32), below[wide:], jnp.zeros((wide, cols), F32)], axis=0
    )
    code = code.T.astype(BF16)
    centre_ref[...] = turned
    code_out_ref[...] = code

    def right(ref):
        ref[0:wide, :] = turned[cols - wide :, :]
        ref[wide:, :] = code[cols - HALF :, :]

    def left(ref):
        ref[0:wide, :] = turned[0:wide, :]
        ref[wide:, :] = code[0:HALF, :]

    if len(side_refs) == 2:
        right(side_refs[0])
        left(side_refs[1])
    else:
        pl.when(at_start("col"))(lambda: right(side_refs[0]))
        pl.when(at_end("col"))(lambda: left(side_refs[0]))


def correlate(tables, source_ref, field_ref, total_ref, columns_ref):
    taps_ref, near_ref, row_table_ref = tables
    kernels = taps_ref.shape[0]
    tiles, span = field_ref.shape[1:3]
    wide = 2 * HALF
    long = tiles * LANES
    total_ref[...] = jnp.zeros_like(total_ref)
    columns = jnp.dot(near_ref[...], source_ref[...], preferred_element_type=F32).astype(BF16)
    for kernel in range(kernels):
        for part in range(2):
            at = (kernel * 2 + part) * wide
            for block in range(span // wide):
                for t in range(tiles):
                    lane = block * long + t * LANES
                    to = t * span + block * wide
                    columns_ref[kernel, to : to + wide, part * LANES : (part + 1) * LANES] = columns[
                        at : at + wide, lane : lane + LANES
                    ]
    edge = (tiles - 1) * span
    for kernel in range(kernels):
        weight = taps_ref[kernel, 4:5, :]
        window = jnp.concatenate([columns_ref[kernel, 0:edge], columns_ref[kernel, span:]], axis=1)
        inner = jnp.dot(window, row_table_ref[kernel], preferred_element_type=F32)
        outer = jnp.dot(
            columns_ref[kernel, edge:], row_table_ref[kernel, 0 : 2 * LANES], preferred_element_type=F32
        )
        for t in range(tiles):
            part = inner[t * span : (t + 1) * span] if t + 1 < tiles else outer
            scaled = weight * part
            field_ref[kernel, t] = scaled.astype(field_ref.dtype)
            total_ref[t] += scaled * part


def back_tables_kernel(taps_ref, _, row_table_ref, col_table_ref, masks_ref):
    kernels = taps_ref.shape[0]
    wide = 2 * HALF
    each = 3 * LANES
    write_masks(masks_ref)
    a, b = index_pair((LANES, LANES))
    inside = jnp.where(b < wide, b, b - wide) < a
    for kernel in range(kernels):
        for half in range(2):
            zero, one = (
                circulant(taps_ref[kernel, 2 + part : 3 + part, 0:LANES], LANES // 2) * masks_ref[2 + half]
                for part in range(2)
            )
            at = half * 2 * LANES
            row_table_ref[kernel, at : at + LANES] = jnp.concatenate([zero, -one], axis=1)
            row_table_ref[kernel, at + LANES : at + 2 * LANES] = jnp.concatenate([one, zero], axis=1)
        turned = []
        group, at = kernel // CHUNK, kernel % CHUNK * each
        for part in range(2):
            row = taps_ref[kernel, part : part + 1, LANES:]
            to = slice(at + part * LANES, at + (part + 1) * LANES)
            col_table_ref[group, :, to] = circulant(row, 0) * masks_ref[0]
            spread = jnp.broadcast_to(row, (LANES, LANES))
            turned.append(pltpu.roll(spread, part * wide, 1, stride=1, stride_axis=0))
        both = jnp.where(b < wide, turned[0], turned[1])
        col_table_ref[group, :, at + 2 * LANES : at + each] = jnp.where(inside, both, 0.0).astype(BF16)


def middle_kernel(
    centre_ref, taps_ref, near_ref, row_table_ref, field_ref, intensity_ref, total_ref, columns_ref
):
    correlate((taps_ref, near_ref, row_table_ref), centre_ref, field_ref, total_ref, columns_ref)
    for t in range(total_ref.shape[0]):
        intensity_ref[t] = total_ref[t, :, 0:LANES] + total_ref[t, :, LANES:]


def side_kernel(
    centre_ref,
    before_ref,
    after_ref,
    middle_ref,
    taps_ref,
    near_ref,
    row_table_ref,
    field_ref,
    intensity_ref,
    total_ref,
    source_ref,
    columns_ref,
):
    wide = 2 * HALF
    cols, long = centre_ref.shape
    source_ref[0:wide, 0:long] = unless(at_start("col"), before_ref[0:wide, :]).astype(BF16)
    source_ref[wide:, 0:long] = centre_ref[0:wide, :]
    source_ref[0:wide, long:] = centre_ref[cols - wide :, :]
    source_ref[wide:, long:] = unless(at_end("col"), after_ref[0:wide, :]).astype(BF16)
    correlate((taps_ref, near_ref, row_table_ref), source_ref, field_ref, total_ref, columns_ref)
    for t in range(total_ref.shape[0]):
        intensity = total_ref[t, :, 0:LANES] + total_ref[t, :, LANES:]
        intensity_ref[t, 0:wide] = intensity[0:wide]
        intensity_ref[t, wide : 2 * wide] = middle_ref[t]
        intensity_ref[t, 2 * wide :] = intensity[wide:]


def backward_kernel(
    own_ref,
    other_ref,
    code_ref,
    code_before_ref,
    code_after_ref,
    params_ref,
    middle_ref,
    side_ref,
    row_table_ref,
    col_table_ref,
    gradient_ref,
    resist_hbm,
    sums_ref,
    slope_ref,
    descent_ref,
    resist_ref,
    source_ref,
    sem,
):
    kernels = row_table_ref.shape[0]
    cols = code_ref.shape[0]
    wide = 2 * HALF
    tiles = own_ref.shape[0]
    span = cols + wide
    rows = (tiles - 1) * LANES
    units = source_ref.shape[0] // (2 * span)

    resists, loss = [], 0.0
    for t in range(tiles):
        lanes = slice(t * LANES, (t + 1) * LANES)
        code = jnp.concatenate(
            [
                unless(at_start("col"), code_before_ref[wide:, lanes]),
                code_ref[:, lanes].astype(F32),
                unless(at_end("col"), code_after_ref[wide:, lanes]),
            ],
            axis=0,
        )
        summed = own_ref[t] + other_ref[t]
        resist = jax.nn.sigmoid(resist_steep * (summed - resist_level))
        mismatch = resist - (code - 1.0)
        slope = 4.0 * mismatch * resist_steep * resist * (1.0 - resist)
        slope = jnp.where(code > 0.5, slope, 0.0).astype(BF16)
        slope_ref[t] = jnp.concatenate([slope, slope], axis=1)
        resists.append(resist[HALF : HALF + cols])
        mine = mismatch[HALF : HALF + cols]
        _, lane = index_pair(mine.shape)
        lane = lane + t * LANES
        mine = jnp.where((lane >= HALF) & (lane < HALF + rows), mine, 0.0)
        loss = loss + mine * mine
    resist_ref[...] = jnp.concatenate(resists, axis=1).T[HALF : HALF + rows]
    copy = pltpu.make_async_copy(resist_ref, resist_hbm, sem)
    copy.start()
    descent_ref[...] = jnp.zeros_like(descent_ref)

    def group(step, carry):
        for unit in range(units):
            kernel = step * units + unit
            products = [
                slope_ref[t]
                * jnp.concatenate(
                    [side_ref[kernel, t, 0:wide], middle_ref[kernel, t], side_ref[kernel, t, wide:]], axis=0
                )
                for t in range(tiles)
            ]
            window = jnp.concatenate(
                [jnp.concatenate(products[:-1], axis=0), jnp.concatenate(products[1:], axis=0)], axis=1
            )
            returned = jnp.dot(window, row_table_ref[kernel], preferred_element_type=F32).astype(BF16)
            at = unit * 2 * span
            for t in range(tiles - 1):
                to = slice(t * LANES, (t + 1) * LANES)
                for part in range(2):
                    piece = returned[t * span : (t + 1) * span, part * LANES : (part + 1) * LANES]
                    source_ref[at + part * cols : at + (part + 1) * cols, to] = piece[0:cols]
                    tail = at + 2 * cols + part * wide
                    source_ref[tail : tail + wide, to] = piece[cols:]
            if unit % CHUNK == CHUNK - 1:
                chunk = slice((unit + 1 - CHUNK) * 2 * span, (unit + 1) * 2 * span)
                descent_ref[...] += jnp.dot(
                    col_table_ref[step * (units // CHUNK) + unit // CHUNK], source_ref[chunk, :], preferred_element_type=F32
                )
        return carry

    lax.fori_loop(0, kernels // units, group, 0)
    mask = jax.nn.sigmoid(mask_slope * params_ref[...])
    gradient = descent_ref[...].T * mask_slope * mask * (1.0 - mask)
    gradient_ref[...] = gradient
    sums_ref[0:1, :] = jnp.broadcast_to(jnp.sum(gradient * gradient), (1, LANES))
    sums_ref[1:2, :] = jnp.broadcast_to(jnp.sum(loss), (1, LANES))
    copy.wait()


def finish_kernel(params_ref, gradient_ref, sums_ref, new_ref, loss_ref, *, count):
    mean = sums_ref[...] * (1.0 / count)
    scale = step_length / jnp.sqrt(mean[0:1] + norm_eps)
    new_ref[...] = params_ref[...] - gradient_ref[...] * scale
    loss_ref[...] = mean[1:2]


def shards(mask_params, target, col_taps, row_taps, kernel_weights):
    rows, cols = target.shape
    kernels, _, taps = col_taps.shape
    wide = 2 * HALF
    tiles = rows // LANES + 1
    long, span = tiles * LANES, cols + wide
    back_units = BACKWARD_UNROLL
    if cols != LANES or rows % LANES or taps != wide + 1 or kernels % back_units:
        raise ValueError("block shape")
    vmem = pl.BlockSpec(memory_space=pltpu.VMEM)
    hbm = pl.BlockSpec(memory_space=pltpu.HBM)
    array = jax.ShapeDtypeStruct

    def call(body, name, specs, outs, out_specs=None, scratch=(), grant=4 * 2**20, flops=10**6):
        return pl.pallas_call(
            body,
            in_specs=specs,
            out_shape=outs,
            out_specs=[vmem] * len(outs) if out_specs is None else out_specs,
            scratch_shapes=scratch,
            compiler_params=pltpu.CompilerParams(vmem_limit_bytes=grant),
            cost_estimate=pl.CostEstimate(flops=flops, bytes_accessed=10**6, transcendentals=0),
            name=name,
        )

    plain, edge = array((rows, cols), BF16), array((wide + HALF, cols), BF16)
    full = array((rows, cols), F32)
    sides, strips = lax.axis_size("col"), lax.axis_size("strip")
    mine, goal = stay(mask_params[0]), stay(target)
    ahead, behind = call(
        edges_kernel,
        "edges",
        [hbm, hbm],
        (edge, edge),
        scratch=[
            pltpu.VMEM((2, wide, cols), F32),
            pltpu.VMEM((2, HALF, cols), target.dtype),
            pltpu.SemaphoreType.DMA((2, 2)),
        ],
    )(mine, goal)
    from_behind = lax.ppermute(ahead, ("tiles", "strip"), snake(1))
    from_ahead = lax.ppermute(behind, ("tiles", "strip"), snake(-1))
    masks = pltpu.VMEM((4, LANES, LANES), BF16)
    row_tables = array((kernels, 4 * LANES, 2 * LANES), BF16)
    params, mask_half, code, *tables = call(
        load_kernel,
        "load",
        [hbm] * 5,
        (full, plain, plain, array((kernels, 8, 2 * LANES), F32), array((kernels * 2 * wide, LANES), BF16), row_tables),
        scratch=[
            pltpu.VMEM((rows, cols), target.dtype),
            pltpu.SMEM(kernel_weights.shape, F32),
            pltpu.VMEM(col_taps.shape, BF16),
            pltpu.VMEM(row_taps.shape, BF16),
            pltpu.VMEM((4 * kernels, taps), F32),
            masks,
            pltpu.SemaphoreType.DMA((5,)),
        ],
        flops=10**8,
    )(mine, goal, stay(kernel_weights), stay(col_taps), stay(row_taps))

    side, turned = array((wide + HALF, long), BF16), array((cols, long), BF16)
    centre, code_turned, *messages = call(
        assemble_kernel,
        "assemble",
        [vmem] * 4,
        (turned, turned) + (side,) * (1 if sides == 2 else 2),
    )(mask_half, code, from_behind, from_ahead)
    if sides == 2:
        before = after = lax.ppermute(messages[0], "col", ring("col", 1))
    else:
        before = lax.ppermute(messages[0], "col", ring("col", 1))
        after = lax.ppermute(messages[1], "col", ring("col", -1))

    def part(width):
        fields = array((kernels, tiles, width, 2 * LANES), BF16)
        columns = pltpu.VMEM((kernels, tiles * width, 2 * LANES), BF16)
        return fields, pltpu.VMEM((tiles, width, 2 * LANES), F32), columns

    fields, total, columns = part(wide)
    middle, middle_intensity = call(
        middle_kernel,
        "middle",
        [vmem] * 4,
        (fields, array((tiles, wide, LANES), F32)),
        scratch=[total, columns],
        grant=VMEM,
        flops=4 * 10**9,
    )(centre, *tables)
    plane = (tiles, span, LANES)
    fields, total, columns = part(2 * wide)
    sides_field, intensity = call(
        side_kernel,
        "side",
        [vmem] * 7,
        (fields, array(plane, F32)),
        scratch=[total, pltpu.VMEM((LANES, 2 * long), BF16), columns],
        grant=VMEM,
    )(centre, before, after, middle_intensity, *tables)

    other = lax.ppermute(intensity, "expo", [(0, 1), (1, 0)])
    back_tables = call(
        back_tables_kernel,
        "back_tables",
        [vmem, pl.BlockSpec(memory_space=pl.ANY)],
        (row_tables, array((kernels // CHUNK, cols, CHUNK * 2 * span), BF16)),
        scratch=[masks],
        flops=10**9,
    )(tables[0], intensity)

    gradient, resist, sums = call(
        backward_kernel,
        "backward",
        [vmem] * 10,
        (full, full, array((2, LANES), F32)),
        out_specs=[vmem, hbm, vmem],
        scratch=[
            pltpu.VMEM((tiles, span, 2 * LANES), BF16),
            pltpu.VMEM((cols, rows), F32),
            pltpu.VMEM((rows, cols), F32),
            pltpu.VMEM((back_units * 2 * span, rows), BF16),
            pltpu.SemaphoreType.DMA,
        ],
        grant=VMEM,
    )(intensity, other, code_turned, before, after, params, middle, sides_field, *back_tables)

    sums = sums + lax.ppermute(sums, "expo", [(0, 1), (1, 0)])
    for axis in ("col", "strip"):
        sums = total_over(sums, axis)
    count = 2 * rows * cols * strips * sides
    new_params, loss = call(
        functools.partial(finish_kernel, count=count), "finish", [vmem] * 3, (full, array((1, LANES), F32))
    )(params, gradient, sums)
    return (new_params[None], resist, loss[0, 0:1])


def solution(mesh):
    if mesh.shape["expo"] != 2:
        raise ValueError("two exposures")
    return jax.shard_map(
        shards,
        mesh=mesh,
        in_specs=(
            P("expo", ("tiles", "strip"), "col"),
            P(("tiles", "strip"), "col"),
            P(),
            P(),
            P(),
        ),
        out_specs=(P("expo", ("tiles", "strip"), "col"), P(("tiles", "strip"), "col"), P("tiles")),
        check_vma=False,
    )
```

```python
import functools
import jax
import jax.numpy as jnp
from jax import lax
from jax.experimental import pallas as pl
from jax.experimental.pallas import tpu as pltpu
from jax.sharding import PartitionSpec as P

HALF = 32
LANES = 128
BACKWARD_UNROLL = 12
CHUNK = 6
VMEM = 24 * 2**20

mask_slope = 4.0
resist_steep = 4.0
resist_level = 3.0
step_length = 0.5
norm_eps = 1e-06

BF16 = jnp.bfloat16
F32 = jnp.float32


def stay(array):
    return pltpu.with_memory_space_constraint(array, pltpu.HBM)


def ring(axis, step):
    peers = lax.axis_size(axis)
    return [(i, (i + step) % peers) for i in range(peers)]


def snake(step):
    tiles, strips = lax.axis_size("tiles"), lax.axis_size("strip")
    order = []
    for tile in range(tiles):
        levels = range(strips) if tile % 2 == 0 else reversed(range(strips))
        order += [tile * strips + level for level in levels]
    return [(device, order[(i + step) % len(order)]) for i, device in enumerate(order)]


def partners(peers, other):
    return [(2 * i + core, 2 * other(i) + 1 - core) for i in range(peers) for core in range(2)]


def total_over(value, axis):
    peers = lax.axis_size(axis)
    if peers & (peers - 1):
        return lax.psum(value, axis)
    both = (axis, "expo")
    reach = 1
    while reach < peers:
        value = value + lax.ppermute(value, both, partners(peers, lambda i, r=reach: i ^ r))
        reach *= 2
    return value


def circulant(row, shift):
    spread = jnp.broadcast_to(row, (LANES, LANES))
    return pltpu.roll(spread, shift, 1, stride=1, stride_axis=0).astype(BF16)


def index_pair(shape):
    return lax.broadcasted_iota(jnp.int32, shape, 0), lax.broadcasted_iota(jnp.int32, shape, 1)


def write_masks(masks_ref):
    a, b = index_pair((LANES, LANES))
    one, zero = jnp.ones((LANES, LANES), F32), jnp.zeros((LANES, LANES), F32)
    for slot, keep in enumerate((b >= a, b < a, a >= b, a < b)):
        masks_ref[slot] = jnp.where(keep, one, zero).astype(BF16)


def mask_of(params):
    return jax.nn.sigmoid(mask_slope * params).astype(BF16)


def code_of(target):
    return (target + 1).astype(F32).astype(BF16)


def edges_kernel(params_hbm, target_hbm, ahead_ref, behind_ref, params_ref, target_ref, sems):
    rows = params_hbm.shape[0]
    wide = 2 * HALF
    copies = [
        pltpu.make_async_copy(source.at[pl.ds(start, size)], target.at[slot], sems.at[sem, slot])
        for sem, (source, target, size) in enumerate(
            ((params_hbm, params_ref, wide), (target_hbm, target_ref, HALF))
        )
        for slot, start in enumerate((0, rows - size))
    ]
    for copy in copies:
        copy.start()
    for copy in copies:
        copy.wait()

    def fill(refs):
        for slot, ref in enumerate(refs):
            ref[0:wide, :] = mask_of(params_ref[slot])
            ref[wide:, :] = code_of(target_ref[slot])

    pl.when(jnp.logical_not(turned_tile()))(lambda: fill((behind_ref, ahead_ref)))
    pl.when(turned_tile())(lambda: fill((ahead_ref, behind_ref)))


def load_kernel(
    params_hbm,
    target_hbm,
    weights_hbm,
    col_hbm,
    row_hbm,
    params_ref,
    mask_ref,
    code_ref,
    taps_ref,
    near_ref,
    row_table_ref,
    target_ref,
    weights_ref,
    col_ref,
    row_ref,
    flat_ref,
    masks_ref,
    sems,
):
    kernels, _, taps = col_ref.shape
    copies = [
        pltpu.make_async_copy(source, target, sems.at[slot])
        for slot, (source, target) in enumerate(
            (
                (weights_hbm, weights_ref),
                (col_hbm, col_ref),
                (row_hbm, row_ref),
                (params_hbm, params_ref),
                (target_hbm, target_ref),
            )
        )
    ]
    for copy in copies:
        copy.start()
    t, l = index_pair((taps, 2 * LANES))
    pick = jnp.where((l == t) | (l == LANES + taps - 1 - t), 1.0, 0.0).astype(BF16)
    for copy in copies:
        copy.wait()
    for k in range(kernels):
        flat_ref[4 * k : 4 * k + 2] = col_ref[k].astype(F32)
        flat_ref[4 * k + 2 : 4 * k + 4] = row_ref[k].astype(F32)
    rows = jnp.dot(flat_ref[...].astype(BF16), pick, preferred_element_type=F32)
    for k in range(kernels):
        taps_ref[k, 0:4] = rows[4 * k : 4 * k + 4]
        taps_ref[k, 4:8] = jnp.full((4, 2 * LANES), weights_ref[k], F32)
    mask_ref[...] = mask_of(params_ref[...])
    code_ref[...] = code_of(target_ref[...])
    write_masks(masks_ref)
    wide = taps - 1
    for k in range(kernels):
        for part in range(2):
            at = (2 * k + part) * wide
            base = circulant(taps_ref[k, part : part + 1, 0:LANES], 0)[0:wide]
            near_ref[at : at + wide, :] = base * masks_ref[0, 0:wide]
        for half in range(2):
            zero, one = (
                circulant(taps_ref[k, 2 + part : 3 + part, LANES:], LANES // 2) * masks_ref[2 + half]
                for part in range(2)
            )
            at = half * 2 * LANES
            row_table_ref[k, at : at + LANES] = jnp.concatenate([zero, one], axis=1)
            row_table_ref[k, at + LANES : at + 2 * LANES] = jnp.concatenate([-one, zero], axis=1)


def unless(end, values):
    return jnp.where(end, 0.0, values.astype(F32))


def at_start(axis):
    return lax.axis_index(axis) == 0


def at_end(axis):
    return lax.axis_index(axis) == lax.axis_size(axis) - 1


def turned_tile():
    return lax.axis_index("tiles") % 2 == 1


def assemble_kernel(
    mask_ref, code_ref, behind_ref, ahead_ref, centre_ref, code_out_ref, *side_refs
):
    rows, cols = mask_ref.shape
    wide = 2 * HALF
    turn = turned_tile()
    behind, ahead = behind_ref[...].astype(F32), ahead_ref[...].astype(F32)
    above = unless(at_start("strip"), jnp.where(turn, ahead, behind))
    below = unless(at_end("strip"), jnp.where(turn, behind, ahead))
    tall = jnp.concatenate([above[0:wide], mask_ref[...].astype(F32), below[0:wide]], axis=0)
    turned = tall.T.astype(BF16)
    code = jnp.concatenate(
        [above[wide:], code_ref[...].astype(F32), below[wide:], jnp.zeros((wide, cols), F32)], axis=0
    )
    code = code.T.astype(BF16)
    centre_ref[...] = turned
    code_out_ref[...] = code

    def right(ref):
        ref[0:wide, :] = turned[cols - wide :, :]
        ref[wide:, :] = code[cols - HALF :, :]

    def left(ref):
        ref[0:wide, :] = turned[0:wide, :]
        ref[wide:, :] = code[0:HALF, :]

    if len(side_refs) == 2:
        right(side_refs[0])
        left(side_refs[1])
    else:
        pl.when(at_start("col"))(lambda: right(side_refs[0]))
        pl.when(at_end("col"))(lambda: left(side_refs[0]))


def correlate(tables, source_ref, field_ref, total_ref, columns_ref):
    taps_ref, near_ref, row_table_ref = tables
    kernels = taps_ref.shape[0]
    tiles, span = field_ref.shape[1:3]
    wide = 2 * HALF
    long = tiles * LANES
    total_ref[...] = jnp.zeros_like(total_ref)
    columns = jnp.dot(near_ref[...], source_ref[...], preferred_element_type=F32).astype(BF16)
    for kernel in range(kernels):
        for part in range(2):
            at = (kernel * 2 + part) * wide
            for block in range(span // wide):
                for t in range(tiles):
                    lane = block * long + t * LANES
                    to = t * span + block * wide
                    columns_ref[kernel, to : to + wide, part * LANES : (part + 1) * LANES] = columns[
                        at : at + wide, lane : lane + LANES
                    ]
    edge = (tiles - 1) * span
    for kernel in range(kernels):
        weight = taps_ref[kernel, 4:5, :]
        window = jnp.concatenate([columns_ref[kernel, 0:edge], columns_ref[kernel, span:]], axis=1)
        inner = jnp.dot(window, row_table_ref[kernel], preferred_element_type=F32)
        outer = jnp.dot(
            columns_ref[kernel, edge:], row_table_ref[kernel, 0 : 2 * LANES], preferred_element_type=F32
        )
        for t in range(tiles):
            part = inner[t * span : (t + 1) * span] if t + 1 < tiles else outer
            scaled = weight * part
            field_ref[kernel, t] = scaled.astype(field_ref.dtype)
            total_ref[t] += scaled * part


def back_tables_kernel(
    taps_ref, code_ref, code_before_ref, code_after_ref, _, row_table_ref, col_table_ref, goal_ref, factor_ref, masks_ref
):
    kernels = taps_ref.shape[0]
    for t in range(goal_ref.shape[0]):
        lanes = slice(t * LANES, (t + 1) * LANES)
        code = jnp.concatenate(
            [
                unless(at_start("col"), code_before_ref[2 * HALF :, lanes]),
                code_ref[:, lanes].astype(F32),
                unless(at_end("col"), code_after_ref[2 * HALF :, lanes]),
            ],
            axis=0,
        )
        goal_ref[t] = code - 1.0
        factor_ref[t] = jnp.where(code > 0.5, 4.0 * resist_steep, 0.0)
    wide = 2 * HALF
    each = 3 * LANES
    write_masks(masks_ref)
    a, b = index_pair((LANES, LANES))
    inside = jnp.where(b < wide, b, b - wide) < a
    for kernel in range(kernels):
        for half in range(2):
            zero, one = (
                circulant(taps_ref[kernel, 2 + part : 3 + part, 0:LANES], LANES // 2) * masks_ref[2 + half]
                for part in range(2)
            )
            at = half * 2 * LANES
            row_table_ref[kernel, at : at + LANES] = jnp.concatenate([zero, -one], axis=1)
            row_table_ref[kernel, at + LANES : at + 2 * LANES] = jnp.concatenate([one, zero], axis=1)
        turned = []
        group, at = kernel // CHUNK, kernel % CHUNK * each
        for part in range(2):
            row = taps_ref[kernel, part : part + 1, LANES:]
            to = slice(at + part * LANES, at + (part + 1) * LANES)
            col_table_ref[group, :, to] = circulant(row, 0) * masks_ref[0]
            spread = jnp.broadcast_to(row, (LANES, LANES))
            turned.append(pltpu.roll(spread, part * wide, 1, stride=1, stride_axis=0))
        both = jnp.where(b < wide, turned[0], turned[1])
        col_table_ref[group, :, at + 2 * LANES : at + each] = jnp.where(inside, both, 0.0).astype(BF16)


def middle_kernel(
    centre_ref, taps_ref, near_ref, row_table_ref, field_ref, intensity_ref, total_ref, columns_ref
):
    correlate((taps_ref, near_ref, row_table_ref), centre_ref, field_ref, total_ref, columns_ref)
    for t in range(total_ref.shape[0]):
        intensity_ref[t] = total_ref[t, :, 0:LANES] + total_ref[t, :, LANES:]


def side_kernel(
    centre_ref,
    before_ref,
    after_ref,
    middle_ref,
    taps_ref,
    near_ref,
    row_table_ref,
    field_ref,
    intensity_ref,
    total_ref,
    source_ref,
    columns_ref,
):
    wide = 2 * HALF
    cols, long = centre_ref.shape
    source_ref[0:wide, 0:long] = unless(at_start("col"), before_ref[0:wide, :]).astype(BF16)
    source_ref[wide:, 0:long] = centre_ref[0:wide, :]
    source_ref[0:wide, long:] = centre_ref[cols - wide :, :]
    source_ref[wide:, long:] = unless(at_end("col"), after_ref[0:wide, :]).astype(BF16)
    correlate((taps_ref, near_ref, row_table_ref), source_ref, field_ref, total_ref, columns_ref)
    for t in range(total_ref.shape[0]):
        intensity = total_ref[t, :, 0:LANES] + total_ref[t, :, LANES:]
        intensity_ref[t, 0:wide] = intensity[0:wide]
        intensity_ref[t, wide : 2 * wide] = middle_ref[t]
        intensity_ref[t, 2 * wide :] = intensity[wide:]


def backward_kernel(
    own_ref,
    other_ref,
    goal_ref,
    factor_ref,
    params_ref,
    middle_ref,
    side_ref,
    row_table_ref,
    col_table_ref,
    gradient_ref,
    resist_hbm,
    sums_ref,
    slope_ref,
    descent_ref,
    resist_ref,
    source_ref,
    sem,
):
    kernels = row_table_ref.shape[0]
    cols = gradient_ref.shape[1]
    wide = 2 * HALF
    tiles = own_ref.shape[0]
    span = cols + wide
    rows = (tiles - 1) * LANES
    units = source_ref.shape[0] // (2 * span)

    resists, loss = [], 0.0
    for t in range(tiles):
        summed = own_ref[t] + other_ref[t]
        resist = jax.nn.sigmoid(resist_steep * (summed - resist_level))
        mismatch = resist - goal_ref[t]
        slope = (mismatch * resist * (1.0 - resist) * factor_ref[t]).astype(BF16)
        slope_ref[t] = jnp.concatenate([slope, slope], axis=1)
        resists.append(resist[HALF : HALF + cols])
        mine = mismatch[HALF : HALF + cols]
        _, lane = index_pair(mine.shape)
        lane = lane + t * LANES
        mine = jnp.where((lane >= HALF) & (lane < HALF + rows), mine, 0.0)
        loss = loss + mine * mine
    resist_ref[...] = jnp.concatenate(resists, axis=1).T[HALF : HALF + rows]
    copy = pltpu.make_async_copy(resist_ref, resist_hbm, sem)
    copy.start()
    descent_ref[...] = jnp.zeros_like(descent_ref)

    def group(step, carry):
        for unit in range(units):
            kernel = step * units + unit
            products = [
                slope_ref[t]
                * jnp.concatenate(
                    [side_ref[kernel, t, 0:wide], middle_ref[kernel, t], side_ref[kernel, t, wide:]], axis=0
                )
                for t in range(tiles)
            ]
            window = jnp.concatenate(
                [jnp.concatenate(products[:-1], axis=0), jnp.concatenate(products[1:], axis=0)], axis=1
            )
            returned = jnp.dot(window, row_table_ref[kernel], preferred_element_type=F32).astype(BF16)
            at = unit * 2 * span
            for t in range(tiles - 1):
                to = slice(t * LANES, (t + 1) * LANES)
                for part in range(2):
                    piece = returned[t * span : (t + 1) * span, part * LANES : (part + 1) * LANES]
                    source_ref[at + part * cols : at + (part + 1) * cols, to] = piece[0:cols]
                    tail = at + 2 * cols + part * wide
                    source_ref[tail : tail + wide, to] = piece[cols:]
            if unit % CHUNK == CHUNK - 1:
                chunk = slice((unit + 1 - CHUNK) * 2 * span, (unit + 1) * 2 * span)
                descent_ref[...] += jnp.dot(
                    col_table_ref[step * (units // CHUNK) + unit // CHUNK], source_ref[chunk, :], preferred_element_type=F32
                )
        return carry

    lax.fori_loop(0, kernels // units, group, 0)
    mask = jax.nn.sigmoid(mask_slope * params_ref[...])
    gradient = descent_ref[...].T * mask_slope * mask * (1.0 - mask)
    gradient_ref[...] = gradient
    sums_ref[0:1, :] = jnp.broadcast_to(jnp.sum(gradient * gradient), (1, LANES))
    sums_ref[1:2, :] = jnp.broadcast_to(jnp.sum(loss), (1, LANES))
    copy.wait()


def finish_kernel(params_ref, gradient_ref, sums_ref, new_ref, loss_ref, *, count):
    mean = sums_ref[...] * (1.0 / count)
    scale = step_length / jnp.sqrt(mean[0:1] + norm_eps)
    new_ref[...] = params_ref[...] - gradient_ref[...] * scale
    loss_ref[...] = mean[1:2]


def shards(mask_params, target, col_taps, row_taps, kernel_weights):
    rows, cols = target.shape
    kernels, _, taps = col_taps.shape
    wide = 2 * HALF
    tiles = rows // LANES + 1
    long, span = tiles * LANES, cols + wide
    back_units = BACKWARD_UNROLL
    if cols != LANES or rows % LANES or taps != wide + 1 or kernels % back_units:
        raise ValueError("block shape")
    vmem = pl.BlockSpec(memory_space=pltpu.VMEM)
    hbm = pl.BlockSpec(memory_space=pltpu.HBM)
    array = jax.ShapeDtypeStruct

    def call(body, name, specs, outs, out_specs=None, scratch=(), grant=4 * 2**20, flops=10**6):
        return pl.pallas_call(
            body,
            in_specs=specs,
            out_shape=outs,
            out_specs=[vmem] * len(outs) if out_specs is None else out_specs,
            scratch_shapes=scratch,
            compiler_params=pltpu.CompilerParams(vmem_limit_bytes=grant),
            cost_estimate=pl.CostEstimate(flops=flops, bytes_accessed=10**6, transcendentals=0),
            name=name,
        )

    plain, edge = array((rows, cols), BF16), array((wide + HALF, cols), BF16)
    full = array((rows, cols), F32)
    sides, strips = lax.axis_size("col"), lax.axis_size("strip")
    mine, goal = stay(mask_params[0]), stay(target)
    ahead, behind = call(
        edges_kernel,
        "edges",
        [hbm, hbm],
        (edge, edge),
        scratch=[
            pltpu.VMEM((2, wide, cols), F32),
            pltpu.VMEM((2, HALF, cols), target.dtype),
            pltpu.SemaphoreType.DMA((2, 2)),
        ],
    )(mine, goal)
    from_behind = lax.ppermute(ahead, ("tiles", "strip"), snake(1))
    from_ahead = lax.ppermute(behind, ("tiles", "strip"), snake(-1))
    masks = pltpu.VMEM((4, LANES, LANES), BF16)
    row_tables = array((kernels, 4 * LANES, 2 * LANES), BF16)
    params, mask_half, code, *tables = call(
        load_kernel,
        "load",
        [hbm] * 5,
        (full, plain, plain, array((kernels, 8, 2 * LANES), F32), array((kernels * 2 * wide, LANES), BF16), row_tables),
        scratch=[
            pltpu.VMEM((rows, cols), target.dtype),
            pltpu.SMEM(kernel_weights.shape, F32),
            pltpu.VMEM(col_taps.shape, BF16),
            pltpu.VMEM(row_taps.shape, BF16),
            pltpu.VMEM((4 * kernels, taps), F32),
            masks,
            pltpu.SemaphoreType.DMA((5,)),
        ],
        flops=10**8,
    )(mine, goal, stay(kernel_weights), stay(col_taps), stay(row_taps))

    side, turned = array((wide + HALF, long), BF16), array((cols, long), BF16)
    centre, code_turned, *messages = call(
        assemble_kernel,
        "assemble",
        [vmem] * 4,
        (turned, turned) + (side,) * (1 if sides == 2 else 2),
    )(mask_half, code, from_behind, from_ahead)
    if sides == 2:
        before = after = lax.ppermute(messages[0], "col", ring("col", 1))
    else:
        before = lax.ppermute(messages[0], "col", ring("col", 1))
        after = lax.ppermute(messages[1], "col", ring("col", -1))

    def part(width):
        fields = array((kernels, tiles, width, 2 * LANES), BF16)
        columns = pltpu.VMEM((kernels, tiles * width, 2 * LANES), BF16)
        return fields, pltpu.VMEM((tiles, width, 2 * LANES), F32), columns

    fields, total, columns = part(wide)
    middle, middle_intensity = call(
        middle_kernel,
        "middle",
        [vmem] * 4,
        (fields, array((tiles, wide, LANES), F32)),
        scratch=[total, columns],
        grant=VMEM,
        flops=4 * 10**9,
    )(centre, *tables)
    plane = (tiles, span, LANES)
    fields, total, columns = part(2 * wide)
    sides_field, intensity = call(
        side_kernel,
        "side",
        [vmem] * 7,
        (fields, array(plane, F32)),
        scratch=[total, pltpu.VMEM((LANES, 2 * long), BF16), columns],
        grant=VMEM,
    )(centre, before, after, middle_intensity, *tables)

    other = lax.ppermute(intensity, "expo", [(0, 1), (1, 0)])
    row_table, col_table, goal, factor = call(
        back_tables_kernel,
        "back_tables",
        [vmem] * 4 + [pl.BlockSpec(memory_space=pl.ANY)],
        (
            row_tables,
            array((kernels // CHUNK, cols, CHUNK * 2 * span), BF16),
            array(plane, F32),
            array(plane, F32),
        ),
        scratch=[masks],
        flops=10**9,
    )(tables[0], code_turned, before, after, intensity)

    gradient, resist, sums = call(
        backward_kernel,
        "backward",
        [vmem] * 9,
        (full, full, array((2, LANES), F32)),
        out_specs=[vmem, hbm, vmem],
        scratch=[
            pltpu.VMEM((tiles, span, 2 * LANES), BF16),
            pltpu.VMEM((cols, rows), F32),
            pltpu.VMEM((rows, cols), F32),
            pltpu.VMEM((back_units * 2 * span, rows), BF16),
            pltpu.SemaphoreType.DMA,
        ],
        grant=VMEM,
    )(intensity, other, goal, factor, params, middle, sides_field, row_table, col_table)

    sums = sums + lax.ppermute(sums, "expo", [(0, 1), (1, 0)])
    for axis in ("col", "strip"):
        sums = total_over(sums, axis)
    count = 2 * rows * cols * strips * sides
    new_params, loss = call(
        functools.partial(finish_kernel, count=count), "finish", [vmem] * 3, (full, array((1, LANES), F32))
    )(params, gradient, sums)
    return (new_params[None], resist, loss[0, 0:1])


def solution(mesh):
    if mesh.shape["expo"] != 2:
        raise ValueError("two exposures")
    return jax.shard_map(
        shards,
        mesh=mesh,
        in_specs=(
            P("expo", ("tiles", "strip"), "col"),
            P(("tiles", "strip"), "col"),
            P(),
            P(),
            P(),
        ),
        out_specs=(P("expo", ("tiles", "strip"), "col"), P(("tiles", "strip"), "col"), P("tiles")),
        check_vma=False,
    )
```

```python
import functools
import jax
import jax.numpy as jnp
from jax import lax
from jax.experimental import pallas as pl
from jax.experimental.pallas import tpu as pltpu
from jax.sharding import PartitionSpec as P

HALF = 32
LANES = 128
BACKWARD_UNROLL = 12
GROUPS = 2
CHUNK = 12
VMEM = 24 * 2**20

mask_slope = 4.0
resist_steep = 4.0
resist_level = 3.0
step_length = 0.5
norm_eps = 1e-06

BF16 = jnp.bfloat16
F32 = jnp.float32


def stay(array):
    return pltpu.with_memory_space_constraint(array, pltpu.HBM)


def ring(axis, step):
    peers = lax.axis_size(axis)
    return [(i, (i + step) % peers) for i in range(peers)]


def snake(step):
    tiles, strips = lax.axis_size("tiles"), lax.axis_size("strip")
    order = []
    for tile in range(tiles):
        levels = range(strips) if tile % 2 == 0 else reversed(range(strips))
        order += [tile * strips + level for level in levels]
    return [(device, order[(i + step) % len(order)]) for i, device in enumerate(order)]


def partners(peers, other):
    return [(2 * i + core, 2 * other(i) + 1 - core) for i in range(peers) for core in range(2)]


def total_over(value, axis):
    peers = lax.axis_size(axis)
    if peers & (peers - 1):
        return lax.psum(value, axis)
    both = (axis, "expo")
    reach = 1
    while reach < peers:
        value = value + lax.ppermute(value, both, partners(peers, lambda i, r=reach: i ^ r))
        reach *= 2
    return value


def circulant(row, shift):
    spread = jnp.broadcast_to(row, (LANES, LANES))
    return pltpu.roll(spread, shift, 1, stride=1, stride_axis=0).astype(BF16)


def index_pair(shape):
    return lax.broadcasted_iota(jnp.int32, shape, 0), lax.broadcasted_iota(jnp.int32, shape, 1)


def write_masks(masks_ref):
    a, b = index_pair((LANES, LANES))
    one, zero = jnp.ones((LANES, LANES), F32), jnp.zeros((LANES, LANES), F32)
    for slot, keep in enumerate((b >= a, b < a, a >= b, a < b)):
        masks_ref[slot] = jnp.where(keep, one, zero).astype(BF16)


def mask_of(params):
    return jax.nn.sigmoid(mask_slope * params).astype(BF16)


def code_of(target):
    return (target + 1).astype(F32).astype(BF16)


def edges_kernel(params_hbm, target_hbm, ahead_ref, behind_ref, params_ref, target_ref, sems):
    rows = params_hbm.shape[0]
    wide = 2 * HALF
    copies = [
        pltpu.make_async_copy(source.at[pl.ds(start, size)], target.at[slot], sems.at[sem, slot])
        for sem, (source, target, size) in enumerate(
            ((params_hbm, params_ref, wide), (target_hbm, target_ref, HALF))
        )
        for slot, start in enumerate((0, rows - size))
    ]
    for copy in copies:
        copy.start()
    for copy in copies:
        copy.wait()

    def fill(refs):
        for slot, ref in enumerate(refs):
            ref[0:wide, :] = mask_of(params_ref[slot])
            ref[wide:, :] = code_of(target_ref[slot])

    pl.when(jnp.logical_not(turned_tile()))(lambda: fill((behind_ref, ahead_ref)))
    pl.when(turned_tile())(lambda: fill((ahead_ref, behind_ref)))


def load_kernel(
    params_hbm,
    target_hbm,
    weights_hbm,
    col_hbm,
    row_hbm,
    params_ref,
    mask_ref,
    code_ref,
    taps_ref,
    near_ref,
    row_table_ref,
    target_ref,
    weights_ref,
    col_ref,
    row_ref,
    flat_ref,
    masks_ref,
    sems,
):
    kernels, _, taps = col_ref.shape
    copies = [
        pltpu.make_async_copy(source, target, sems.at[slot])
        for slot, (source, target) in enumerate(
            (
                (weights_hbm, weights_ref),
                (col_hbm, col_ref),
                (row_hbm, row_ref),
                (params_hbm, params_ref),
                (target_hbm, target_ref),
            )
        )
    ]
    for copy in copies:
        copy.start()
    t, l = index_pair((taps, 2 * LANES))
    pick = jnp.where((l == t) | (l == LANES + taps - 1 - t), 1.0, 0.0).astype(BF16)
    for copy in copies:
        copy.wait()
    for k in range(kernels):
        flat_ref[4 * k : 4 * k + 2] = col_ref[k].astype(F32)
        flat_ref[4 * k + 2 : 4 * k + 4] = row_ref[k].astype(F32)
    rows = jnp.dot(flat_ref[...].astype(BF16), pick, preferred_element_type=F32)
    for k in range(kernels):
        taps_ref[k, 0:4] = rows[4 * k : 4 * k + 4]
        taps_ref[k, 4:8] = jnp.full((4, 2 * LANES), weights_ref[k], F32)
    mask_ref[...] = mask_of(params_ref[...])
    code_ref[...] = code_of(target_ref[...])
    write_masks(masks_ref)
    wide = taps - 1
    for k in range(kernels):
        for part in range(2):
            at = (2 * k + part) * wide
            base = circulant(taps_ref[k, part : part + 1, 0:LANES], 0)[0:wide]
            near_ref[at : at + wide, :] = base * masks_ref[0, 0:wide]
        for half in range(2):
            zero, one = (
                circulant(taps_ref[k, 2 + part : 3 + part, LANES:], LANES // 2) * masks_ref[2 + half]
                for part in range(2)
            )
            at = half * 2 * LANES
            row_table_ref[k, at : at + LANES] = jnp.concatenate([zero, one], axis=1)
            row_table_ref[k, at + LANES : at + 2 * LANES] = jnp.concatenate([-one, zero], axis=1)


def unless(end, values):
    return jnp.where(end, 0.0, values.astype(F32))


def at_start(axis):
    return lax.axis_index(axis) == 0


def at_end(axis):
    return lax.axis_index(axis) == lax.axis_size(axis) - 1


def turned_tile():
    return lax.axis_index("tiles") % 2 == 1


def assemble_kernel(
    mask_ref, code_ref, behind_ref, ahead_ref, centre_ref, code_out_ref, *side_refs
):
    rows, cols = mask_ref.shape
    wide = 2 * HALF
    turn = turned_tile()
    behind, ahead = behind_ref[...].astype(F32), ahead_ref[...].astype(F32)
    above = unless(at_start("strip"), jnp.where(turn, ahead, behind))
    below = unless(at_end("strip"), jnp.where(turn, behind, ahead))
    tall = jnp.concatenate([above[0:wide], mask_ref[...].astype(F32), below[0:wide]], axis=0)
    turned = tall.T.astype(BF16)
    code = jnp.concatenate(
        [above[wide:], code_ref[...].astype(F32), below[wide:], jnp.zeros((wide, cols), F32)], axis=0
    )
    code = code.T.astype(BF16)
    centre_ref[...] = turned
    code_out_ref[...] = code

    def right(ref):
        ref[0:wide, :] = turned[cols - wide :, :]
        ref[wide:, :] = code[cols - HALF :, :]

    def left(ref):
        ref[0:wide, :] = turned[0:wide, :]
        ref[wide:, :] = code[0:HALF, :]

    if len(side_refs) == 2:
        right(side_refs[0])
        left(side_refs[1])
    else:
        pl.when(at_start("col"))(lambda: right(side_refs[0]))
        pl.when(at_end("col"))(lambda: left(side_refs[0]))


def correlate(tables, source_ref, field_ref, total_ref, columns_ref):
    taps_ref, near_ref, row_table_ref = tables
    kernels = taps_ref.shape[0]
    tiles, span = field_ref.shape[1:3]
    wide = 2 * HALF
    long = tiles * LANES
    total_ref[...] = jnp.zeros_like(total_ref)
    edge = (tiles - 1) * span
    each = kernels // GROUPS
    for group in range(GROUPS):
        first = group * each
        lines = slice(first * 2 * wide, (first + each) * 2 * wide)
        columns = jnp.dot(near_ref[lines, :], source_ref[...], preferred_element_type=F32).astype(BF16)
        for kernel in range(first, first + each):
            for part in range(2):
                at = ((kernel - first) * 2 + part) * wide
                for block in range(span // wide):
                    for t in range(tiles):
                        lane = block * long + t * LANES
                        to = t * span + block * wide
                        columns_ref[kernel, to : to + wide, part * LANES : (part + 1) * LANES] = columns[
                            at : at + wide, lane : lane + LANES
                        ]
        for kernel in range(first, first + each):
            weight = taps_ref[kernel, 4:5, :]
            window = jnp.concatenate([columns_ref[kernel, 0:edge], columns_ref[kernel, span:]], axis=1)
            inner = jnp.dot(window, row_table_ref[kernel], preferred_element_type=F32)
            outer = jnp.dot(
                columns_ref[kernel, edge:], row_table_ref[kernel, 0 : 2 * LANES], preferred_element_type=F32
            )
            for t in range(tiles):
                part = inner[t * span : (t + 1) * span] if t + 1 < tiles else outer
                scaled = weight * part
                field_ref[kernel, t] = scaled.astype(field_ref.dtype)
                total_ref[t] += scaled * part


def back_tables_kernel(
    taps_ref, code_ref, code_before_ref, code_after_ref, _, row_table_ref, col_table_ref, goal_ref, factor_ref, masks_ref
):
    kernels = taps_ref.shape[0]
    for t in range(goal_ref.shape[0]):
        lanes = slice(t * LANES, (t + 1) * LANES)
        code = jnp.concatenate(
            [
                unless(at_start("col"), code_before_ref[2 * HALF :, lanes]),
                code_ref[:, lanes].astype(F32),
                unless(at_end("col"), code_after_ref[2 * HALF :, lanes]),
            ],
            axis=0,
        )
        goal_ref[t] = code - 1.0
        factor_ref[t] = jnp.where(code > 0.5, 4.0 * resist_steep, 0.0)
    wide = 2 * HALF
    each = 3 * LANES
    write_masks(masks_ref)
    a, b = index_pair((LANES, LANES))
    inside = jnp.where(b < wide, b, b - wide) < a
    for kernel in range(kernels):
        for half in range(2):
            zero, one = (
                circulant(taps_ref[kernel, 2 + part : 3 + part, 0:LANES], LANES // 2) * masks_ref[2 + half]
                for part in range(2)
            )
            at = half * 2 * LANES
            row_table_ref[kernel, at : at + LANES] = jnp.concatenate([zero, -one], axis=1)
            row_table_ref[kernel, at + LANES : at + 2 * LANES] = jnp.concatenate([one, zero], axis=1)
        turned = []
        group, at = kernel // CHUNK, kernel % CHUNK * each
        for part in range(2):
            row = taps_ref[kernel, part : part + 1, LANES:]
            to = slice(at + part * LANES, at + (part + 1) * LANES)
            col_table_ref[group, :, to] = circulant(row, 0) * masks_ref[0]
            spread = jnp.broadcast_to(row, (LANES, LANES))
            turned.append(pltpu.roll(spread, part * wide, 1, stride=1, stride_axis=0))
        both = jnp.where(b < wide, turned[0], turned[1])
        col_table_ref[group, :, at + 2 * LANES : at + each] = jnp.where(inside, both, 0.0).astype(BF16)


def middle_kernel(
    centre_ref, taps_ref, near_ref, row_table_ref, field_ref, intensity_ref, total_ref, columns_ref
):
    correlate((taps_ref, near_ref, row_table_ref), centre_ref, field_ref, total_ref, columns_ref)
    for t in range(total_ref.shape[0]):
        intensity_ref[t] = total_ref[t, :, 0:LANES] + total_ref[t, :, LANES:]


def side_kernel(
    centre_ref,
    before_ref,
    after_ref,
    middle_ref,
    taps_ref,
    near_ref,
    row_table_ref,
    field_ref,
    intensity_ref,
    total_ref,
    source_ref,
    columns_ref,
):
    wide = 2 * HALF
    cols, long = centre_ref.shape
    source_ref[0:wide, 0:long] = unless(at_start("col"), before_ref[0:wide, :]).astype(BF16)
    source_ref[wide:, 0:long] = centre_ref[0:wide, :]
    source_ref[0:wide, long:] = centre_ref[cols - wide :, :]
    source_ref[wide:, long:] = unless(at_end("col"), after_ref[0:wide, :]).astype(BF16)
    correlate((taps_ref, near_ref, row_table_ref), source_ref, field_ref, total_ref, columns_ref)
    for t in range(total_ref.shape[0]):
        intensity = total_ref[t, :, 0:LANES] + total_ref[t, :, LANES:]
        intensity_ref[t, 0:wide] = intensity[0:wide]
        intensity_ref[t, wide : 2 * wide] = middle_ref[t]
        intensity_ref[t, 2 * wide :] = intensity[wide:]


def backward_kernel(
    own_ref,
    other_ref,
    goal_ref,
    factor_ref,
    params_ref,
    middle_ref,
    side_ref,
    row_table_ref,
    col_table_ref,
    gradient_ref,
    resist_hbm,
    sums_ref,
    slope_ref,
    descent_ref,
    resist_ref,
    source_ref,
    sem,
):
    kernels = row_table_ref.shape[0]
    cols = gradient_ref.shape[1]
    wide = 2 * HALF
    tiles = own_ref.shape[0]
    span = cols + wide
    rows = (tiles - 1) * LANES
    units = source_ref.shape[0] // (2 * span)

    resists, loss = [], 0.0
    for t in range(tiles):
        summed = own_ref[t] + other_ref[t]
        resist = jax.nn.sigmoid(resist_steep * (summed - resist_level))
        mismatch = resist - goal_ref[t]
        slope = (mismatch * resist * (1.0 - resist) * factor_ref[t]).astype(BF16)
        slope_ref[t] = jnp.concatenate([slope, slope], axis=1)
        resists.append(resist[HALF : HALF + cols])
        mine = mismatch[HALF : HALF + cols]
        _, lane = index_pair(mine.shape)
        lane = lane + t * LANES
        mine = jnp.where((lane >= HALF) & (lane < HALF + rows), mine, 0.0)
        loss = loss + mine * mine
    resist_ref[...] = jnp.concatenate(resists, axis=1).T[HALF : HALF + rows]
    copy = pltpu.make_async_copy(resist_ref, resist_hbm, sem)
    copy.start()
    descent_ref[...] = jnp.zeros_like(descent_ref)

    def group(step, carry):
        for unit in range(units):
            kernel = step * units + unit
            products = [
                slope_ref[t]
                * jnp.concatenate(
                    [side_ref[kernel, t, 0:wide], middle_ref[kernel, t], side_ref[kernel, t, wide:]], axis=0
                )
                for t in range(tiles)
            ]
            window = jnp.concatenate(
                [jnp.concatenate(products[:-1], axis=0), jnp.concatenate(products[1:], axis=0)], axis=1
            )
            returned = jnp.dot(window, row_table_ref[kernel], preferred_element_type=F32).astype(BF16)
            at = unit * 2 * span
            for t in range(tiles - 1):
                to = slice(t * LANES, (t + 1) * LANES)
                for part in range(2):
                    piece = returned[t * span : (t + 1) * span, part * LANES : (part + 1) * LANES]
                    source_ref[at + part * cols : at + (part + 1) * cols, to] = piece[0:cols]
                    tail = at + 2 * cols + part * wide
                    source_ref[tail : tail + wide, to] = piece[cols:]
            if unit % CHUNK == CHUNK - 1:
                chunk = slice((unit + 1 - CHUNK) * 2 * span, (unit + 1) * 2 * span)
                descent_ref[...] += jnp.dot(
                    col_table_ref[step * (units // CHUNK) + unit // CHUNK], source_ref[chunk, :], preferred_element_type=F32
                )
        return carry

    lax.fori_loop(0, kernels // units, group, 0)
    mask = jax.nn.sigmoid(mask_slope * params_ref[...])
    gradient = descent_ref[...].T * mask_slope * mask * (1.0 - mask)
    gradient_ref[...] = gradient
    sums_ref[0:1, :] = jnp.broadcast_to(jnp.sum(gradient * gradient), (1, LANES))
    sums_ref[1:2, :] = jnp.broadcast_to(jnp.sum(loss), (1, LANES))
    copy.wait()


def finish_kernel(params_ref, gradient_ref, sums_ref, new_ref, loss_ref, *, count):
    mean = sums_ref[...] * (1.0 / count)
    scale = step_length / jnp.sqrt(mean[0:1] + norm_eps)
    new_ref[...] = params_ref[...] - gradient_ref[...] * scale
    loss_ref[...] = mean[1:2]


def shards(mask_params, target, col_taps, row_taps, kernel_weights):
    rows, cols = target.shape
    kernels, _, taps = col_taps.shape
    wide = 2 * HALF
    tiles = rows // LANES + 1
    long, span = tiles * LANES, cols + wide
    back_units = BACKWARD_UNROLL
    if cols != LANES or rows % LANES or taps != wide + 1 or kernels % back_units:
        raise ValueError("block shape")
    vmem = pl.BlockSpec(memory_space=pltpu.VMEM)
    hbm = pl.BlockSpec(memory_space=pltpu.HBM)
    array = jax.ShapeDtypeStruct

    def call(body, name, specs, outs, out_specs=None, scratch=(), grant=4 * 2**20, flops=10**6):
        return pl.pallas_call(
            body,
            in_specs=specs,
            out_shape=outs,
            out_specs=[vmem] * len(outs) if out_specs is None else out_specs,
            scratch_shapes=scratch,
            compiler_params=pltpu.CompilerParams(vmem_limit_bytes=grant),
            cost_estimate=pl.CostEstimate(flops=flops, bytes_accessed=10**6, transcendentals=0),
            name=name,
        )

    plain, edge = array((rows, cols), BF16), array((wide + HALF, cols), BF16)
    full = array((rows, cols), F32)
    sides, strips = lax.axis_size("col"), lax.axis_size("strip")
    mine, goal = stay(mask_params[0]), stay(target)
    ahead, behind = call(
        edges_kernel,
        "edges",
        [hbm, hbm],
        (edge, edge),
        scratch=[
            pltpu.VMEM((2, wide, cols), F32),
            pltpu.VMEM((2, HALF, cols), target.dtype),
            pltpu.SemaphoreType.DMA((2, 2)),
        ],
    )(mine, goal)
    from_behind = lax.ppermute(ahead, ("tiles", "strip"), snake(1))
    from_ahead = lax.ppermute(behind, ("tiles", "strip"), snake(-1))
    masks = pltpu.VMEM((4, LANES, LANES), BF16)
    row_tables = array((kernels, 4 * LANES, 2 * LANES), BF16)
    params, mask_half, code, *tables = call(
        load_kernel,
        "load",
        [hbm] * 5,
        (full, plain, plain, array((kernels, 8, 2 * LANES), F32), array((kernels * 2 * wide, LANES), BF16), row_tables),
        scratch=[
            pltpu.VMEM((rows, cols), target.dtype),
            pltpu.SMEM(kernel_weights.shape, F32),
            pltpu.VMEM(col_taps.shape, BF16),
            pltpu.VMEM(row_taps.shape, BF16),
            pltpu.VMEM((4 * kernels, taps), F32),
            masks,
            pltpu.SemaphoreType.DMA((5,)),
        ],
        flops=10**8,
    )(mine, goal, stay(kernel_weights), stay(col_taps), stay(row_taps))

    side, turned = array((wide + HALF, long), BF16), array((cols, long), BF16)
    centre, code_turned, *messages = call(
        assemble_kernel,
        "assemble",
        [vmem] * 4,
        (turned, turned) + (side,) * (1 if sides == 2 else 2),
    )(mask_half, code, from_behind, from_ahead)
    if sides == 2:
        before = after = lax.ppermute(messages[0], "col", ring("col", 1))
    else:
        before = lax.ppermute(messages[0], "col", ring("col", 1))
        after = lax.ppermute(messages[1], "col", ring("col", -1))

    def part(width):
        fields = array((kernels, tiles, width, 2 * LANES), BF16)
        columns = pltpu.VMEM((kernels, tiles * width, 2 * LANES), BF16)
        return fields, pltpu.VMEM((tiles, width, 2 * LANES), F32), columns

    fields, total, columns = part(wide)
    middle, middle_intensity = call(
        middle_kernel,
        "middle",
        [vmem] * 4,
        (fields, array((tiles, wide, LANES), F32)),
        scratch=[total, columns],
        grant=VMEM,
        flops=4 * 10**9,
    )(centre, *tables)
    plane = (tiles, span, LANES)
    fields, total, columns = part(2 * wide)
    sides_field, intensity = call(
        side_kernel,
        "side",
        [vmem] * 7,
        (fields, array(plane, F32)),
        scratch=[total, pltpu.VMEM((LANES, 2 * long), BF16), columns],
        grant=VMEM,
    )(centre, before, after, middle_intensity, *tables)

    other = lax.ppermute(intensity, "expo", [(0, 1), (1, 0)])
    row_table, col_table, goal, factor = call(
        back_tables_kernel,
        "back_tables",
        [vmem] * 4 + [pl.BlockSpec(memory_space=pl.ANY)],
        (
            row_tables,
            array((kernels // CHUNK, cols, CHUNK * 2 * span), BF16),
            array(plane, F32),
            array(plane, F32),
        ),
        scratch=[masks],
        flops=10**9,
    )(tables[0], code_turned, before, after, intensity)

    gradient, resist, sums = call(
        backward_kernel,
        "backward",
        [vmem] * 9,
        (full, full, array((2, LANES), F32)),
        out_specs=[vmem, hbm, vmem],
        scratch=[
            pltpu.VMEM((tiles, span, 2 * LANES), BF16),
            pltpu.VMEM((cols, rows), F32),
            pltpu.VMEM((rows, cols), F32),
            pltpu.VMEM((back_units * 2 * span, rows), BF16),
            pltpu.SemaphoreType.DMA,
        ],
        grant=VMEM,
    )(intensity, other, goal, factor, params, middle, sides_field, row_table, col_table)

    sums = sums + lax.ppermute(sums, "expo", [(0, 1), (1, 0)])
    for axis in ("col", "strip"):
        sums = total_over(sums, axis)
    count = 2 * rows * cols * strips * sides
    new_params, loss = call(
        functools.partial(finish_kernel, count=count), "finish", [vmem] * 3, (full, array((1, LANES), F32))
    )(params, gradient, sums)
    return (new_params[None], resist, loss[0, 0:1])


def solution(mesh):
    if mesh.shape["expo"] != 2:
        raise ValueError("two exposures")
    return jax.shard_map(
        shards,
        mesh=mesh,
        in_specs=(
            P("expo", ("tiles", "strip"), "col"),
            P(("tiles", "strip"), "col"),
            P(),
            P(),
            P(),
        ),
        out_specs=(P("expo", ("tiles", "strip"), "col"), P(("tiles", "strip"), "col"), P("tiles")),
        check_vma=False,
    )
```

```python
import functools
import jax
import jax.numpy as jnp
from jax import lax
from jax.experimental import pallas as pl
from jax.experimental.pallas import tpu as pltpu
from jax.sharding import PartitionSpec as P

HALF = 32
LANES = 128
BACKWARD_UNROLL = 12
CHUNK = 12
VMEM = 24 * 2**20

mask_slope = 4.0
resist_steep = 4.0
resist_level = 3.0
step_length = 0.5
norm_eps = 1e-06

BF16 = jnp.bfloat16
F32 = jnp.float32


def stay(array):
    return pltpu.with_memory_space_constraint(array, pltpu.HBM)


def ring(axis, step):
    peers = lax.axis_size(axis)
    return [(i, (i + step) % peers) for i in range(peers)]


def snake(step):
    tiles, strips = lax.axis_size("tiles"), lax.axis_size("strip")
    order = []
    for tile in range(tiles):
        levels = range(strips) if tile % 2 == 0 else reversed(range(strips))
        order += [tile * strips + level for level in levels]
    return [(device, order[(i + step) % len(order)]) for i, device in enumerate(order)]


def partners(peers, other):
    return [(2 * i + core, 2 * other(i) + 1 - core) for i in range(peers) for core in range(2)]


def total_over(value, axis):
    peers = lax.axis_size(axis)
    if peers & (peers - 1):
        return lax.psum(value, axis)
    both = (axis, "expo")
    reach = 1
    while reach < peers:
        value = value + lax.ppermute(value, both, partners(peers, lambda i, r=reach: i ^ r))
        reach *= 2
    return value


def circulant(row, shift):
    spread = jnp.broadcast_to(row, (LANES, LANES))
    return pltpu.roll(spread, shift, 1, stride=1, stride_axis=0).astype(BF16)


def index_pair(shape):
    return lax.broadcasted_iota(jnp.int32, shape, 0), lax.broadcasted_iota(jnp.int32, shape, 1)


def write_masks(masks_ref):
    a, b = index_pair((LANES, LANES))
    one, zero = jnp.ones((LANES, LANES), F32), jnp.zeros((LANES, LANES), F32)
    for slot, keep in enumerate((b >= a, b < a, a >= b, a < b)):
        masks_ref[slot] = jnp.where(keep, one, zero).astype(BF16)


def mask_of(params):
    return jax.nn.sigmoid(mask_slope * params).astype(BF16)


def code_of(target):
    return (target + 1).astype(F32).astype(BF16)


def edges_kernel(params_hbm, target_hbm, ahead_ref, behind_ref, params_ref, target_ref, sems):
    rows = params_hbm.shape[0]
    wide = 2 * HALF
    copies = [
        pltpu.make_async_copy(source.at[pl.ds(start, size)], target.at[slot], sems.at[sem, slot])
        for sem, (source, target, size) in enumerate(
            ((params_hbm, params_ref, wide), (target_hbm, target_ref, HALF))
        )
        for slot, start in enumerate((0, rows - size))
    ]
    for copy in copies:
        copy.start()
    for copy in copies:
        copy.wait()

    def fill(refs):
        for slot, ref in enumerate(refs):
            ref[0:wide, :] = mask_of(params_ref[slot])
            ref[wide:, :] = code_of(target_ref[slot])

    pl.when(jnp.logical_not(turned_tile()))(lambda: fill((behind_ref, ahead_ref)))
    pl.when(turned_tile())(lambda: fill((ahead_ref, behind_ref)))


def load_kernel(
    params_hbm,
    target_hbm,
    weights_hbm,
    col_hbm,
    row_hbm,
    params_ref,
    mask_ref,
    code_ref,
    taps_ref,
    near_ref,
    row_table_ref,
    target_ref,
    weights_ref,
    col_ref,
    row_ref,
    flat_ref,
    masks_ref,
    sems,
):
    kernels, _, taps = col_ref.shape
    copies = [
        pltpu.make_async_copy(source, target, sems.at[slot])
        for slot, (source, target) in enumerate(
            (
                (weights_hbm, weights_ref),
                (col_hbm, col_ref),
                (row_hbm, row_ref),
                (params_hbm, params_ref),
                (target_hbm, target_ref),
            )
        )
    ]
    for copy in copies:
        copy.start()
    t, l = index_pair((taps, 2 * LANES))
    pick = jnp.where((l == t) | (l == LANES + taps - 1 - t), 1.0, 0.0).astype(BF16)
    for copy in copies:
        copy.wait()
    for k in range(kernels):
        flat_ref[4 * k : 4 * k + 2] = col_ref[k].astype(F32)
        flat_ref[4 * k + 2 : 4 * k + 4] = row_ref[k].astype(F32)
    rows = jnp.dot(flat_ref[...].astype(BF16), pick, preferred_element_type=F32)
    for k in range(kernels):
        taps_ref[k, 0:4] = rows[4 * k : 4 * k + 4]
        taps_ref[k, 4:8] = jnp.full((4, 2 * LANES), weights_ref[k], F32)
    mask_ref[...] = mask_of(params_ref[...])
    code_ref[...] = code_of(target_ref[...])
    write_masks(masks_ref)
    wide = taps - 1
    for k in range(kernels):
        for part in range(2):
            at = (2 * k + part) * wide
            base = circulant(taps_ref[k, part : part + 1, 0:LANES], 0)[0:wide]
            near_ref[at : at + wide, :] = base * masks_ref[0, 0:wide]
        for half in range(2):
            zero, one = (
                circulant(taps_ref[k, 2 + part : 3 + part, LANES:], LANES // 2) * masks_ref[2 + half]
                for part in range(2)
            )
            at = half * 2 * LANES
            row_table_ref[k, at : at + LANES] = jnp.concatenate([zero, one], axis=1)
            row_table_ref[k, at + LANES : at + 2 * LANES] = jnp.concatenate([-one, zero], axis=1)


def unless(end, values):
    return jnp.where(end, 0.0, values.astype(F32))


def at_start(axis):
    return lax.axis_index(axis) == 0


def at_end(axis):
    return lax.axis_index(axis) == lax.axis_size(axis) - 1


def turned_tile():
    return lax.axis_index("tiles") % 2 == 1


def assemble_kernel(
    mask_ref, code_ref, behind_ref, ahead_ref, centre_ref, code_out_ref, *side_refs
):
    rows, cols = mask_ref.shape
    wide = 2 * HALF
    turn = turned_tile()
    behind, ahead = behind_ref[...].astype(F32), ahead_ref[...].astype(F32)
    above = unless(at_start("strip"), jnp.where(turn, ahead, behind))
    below = unless(at_end("strip"), jnp.where(turn, behind, ahead))
    tall = jnp.concatenate([above[0:wide], mask_ref[...].astype(F32), below[0:wide]], axis=0)
    turned = tall.T.astype(BF16)
    code = jnp.concatenate(
        [above[wide:], code_ref[...].astype(F32), below[wide:], jnp.zeros((wide, cols), F32)], axis=0
    )
    code = code.T.astype(BF16)
    centre_ref[...] = turned
    code_out_ref[...] = code

    def right(ref):
        ref[0:wide, :] = turned[cols - wide :, :]
        ref[wide:, :] = code[cols - HALF :, :]

    def left(ref):
        ref[0:wide, :] = turned[0:wide, :]
        ref[wide:, :] = code[0:HALF, :]

    if len(side_refs) == 2:
        right(side_refs[0])
        left(side_refs[1])
    else:
        pl.when(at_start("col"))(lambda: right(side_refs[0]))
        pl.when(at_end("col"))(lambda: left(side_refs[0]))


def correlate(tables, source_ref, field_ref, total_ref, columns_ref):
    taps_ref, near_ref, row_table_ref = tables
    kernels = taps_ref.shape[0]
    tiles, span = field_ref.shape[1:3]
    wide = 2 * HALF
    long = tiles * LANES
    total_ref[...] = jnp.zeros_like(total_ref)
    columns = jnp.dot(near_ref[...], source_ref[...], preferred_element_type=F32).astype(BF16)
    for kernel in range(kernels):
        for part in range(2):
            at = (kernel * 2 + part) * wide
            for block in range(span // wide):
                for t in range(tiles):
                    lane = block * long + t * LANES
                    to = t * span + block * wide
                    columns_ref[kernel, to : to + wide, part * LANES : (part + 1) * LANES] = columns[
                        at : at + wide, lane : lane + LANES
                    ]
    edge = (tiles - 1) * span
    for kernel in range(kernels):
        weight = taps_ref[kernel, 4:5, :]
        window = jnp.concatenate([columns_ref[kernel, 0:edge], columns_ref[kernel, span:]], axis=1)
        inner = jnp.dot(window, row_table_ref[kernel], preferred_element_type=F32)
        outer = jnp.dot(
            columns_ref[kernel, edge:], row_table_ref[kernel, 0 : 2 * LANES], preferred_element_type=F32
        )
        for t in range(tiles):
            part = inner[t * span : (t + 1) * span] if t + 1 < tiles else outer
            scaled = weight * part
            field_ref[kernel, t] = scaled.astype(field_ref.dtype)
            total_ref[t] += scaled * part


def back_tables_kernel(
    taps_ref, code_ref, code_before_ref, code_after_ref, _, row_table_ref, col_table_ref, goal_ref, factor_ref, masks_ref
):
    kernels = taps_ref.shape[0]
    for t in range(goal_ref.shape[0]):
        lanes = slice(t * LANES, (t + 1) * LANES)
        code = jnp.concatenate(
            [
                unless(at_start("col"), code_before_ref[2 * HALF :, lanes]),
                code_ref[:, lanes].astype(F32),
                unless(at_end("col"), code_after_ref[2 * HALF :, lanes]),
            ],
            axis=0,
        )
        goal_ref[t] = code - 1.0
        factor_ref[t] = jnp.where(code > 0.5, 4.0 * resist_steep, 0.0)
    wide = 2 * HALF
    each = 3 * LANES
    write_masks(masks_ref)
    a, b = index_pair((LANES, LANES))
    inside = jnp.where(b < wide, b, b - wide) < a
    for kernel in range(kernels):
        for half in range(2):
            zero, one = (
                circulant(taps_ref[kernel, 2 + part : 3 + part, 0:LANES], LANES // 2) * masks_ref[2 + half]
                for part in range(2)
            )
            at = half * 2 * LANES
            row_table_ref[kernel, at : at + LANES] = jnp.concatenate([zero, -one], axis=1)
            row_table_ref[kernel, at + LANES : at + 2 * LANES] = jnp.concatenate([one, zero], axis=1)
        turned = []
        group, at = kernel // CHUNK, kernel % CHUNK * each
        for part in range(2):
            row = taps_ref[kernel, part : part + 1, LANES:]
            to = slice(at + part * LANES, at + (part + 1) * LANES)
            col_table_ref[group, :, to] = circulant(row, 0) * masks_ref[0]
            spread = jnp.broadcast_to(row, (LANES, LANES))
            turned.append(pltpu.roll(spread, part * wide, 1, stride=1, stride_axis=0))
        both = jnp.where(b < wide, turned[0], turned[1])
        col_table_ref[group, :, at + 2 * LANES : at + each] = jnp.where(inside, both, 0.0).astype(BF16)


def middle_kernel(
    centre_ref, taps_ref, near_ref, row_table_ref, field_ref, intensity_ref, total_ref, columns_ref
):
    correlate((taps_ref, near_ref, row_table_ref), centre_ref, field_ref, total_ref, columns_ref)
    for t in range(total_ref.shape[0]):
        intensity_ref[t] = total_ref[t, :, 0:LANES] + total_ref[t, :, LANES:]


def side_kernel(
    centre_ref,
    before_ref,
    after_ref,
    middle_ref,
    taps_ref,
    near_ref,
    row_table_ref,
    field_ref,
    intensity_ref,
    total_ref,
    source_ref,
    columns_ref,
):
    wide = 2 * HALF
    cols, long = centre_ref.shape
    source_ref[0:wide, 0:long] = unless(at_start("col"), before_ref[0:wide, :]).astype(BF16)
    source_ref[wide:, 0:long] = centre_ref[0:wide, :]
    source_ref[0:wide, long:] = centre_ref[cols - wide :, :]
    source_ref[wide:, long:] = unless(at_end("col"), after_ref[0:wide, :]).astype(BF16)
    correlate((taps_ref, near_ref, row_table_ref), source_ref, field_ref, total_ref, columns_ref)
    for t in range(total_ref.shape[0]):
        intensity = total_ref[t, :, 0:LANES] + total_ref[t, :, LANES:]
        intensity_ref[t, 0:wide] = intensity[0:wide]
        intensity_ref[t, wide : 2 * wide] = middle_ref[t]
        intensity_ref[t, 2 * wide :] = intensity[wide:]


def backward_kernel(
    own_ref,
    other_ref,
    goal_ref,
    factor_ref,
    params_ref,
    middle_ref,
    side_ref,
    row_table_ref,
    col_table_ref,
    gradient_ref,
    resist_hbm,
    sums_ref,
    slope_ref,
    descent_ref,
    resist_ref,
    source_ref,
    sem,
):
    kernels = row_table_ref.shape[0]
    cols = gradient_ref.shape[1]
    wide = 2 * HALF
    tiles = own_ref.shape[0]
    span = cols + wide
    rows = (tiles - 1) * LANES
    units = source_ref.shape[0] // (2 * span)

    resists, loss = [], 0.0
    for t in range(tiles):
        summed = own_ref[t] + other_ref[t]
        resist = jax.nn.sigmoid(resist_steep * (summed - resist_level))
        mismatch = resist - goal_ref[t]
        slope = (mismatch * resist * (1.0 - resist) * factor_ref[t]).astype(BF16)
        slope_ref[t] = jnp.concatenate([slope, slope], axis=1)
        resists.append(resist[HALF : HALF + cols])
        mine = mismatch[HALF : HALF + cols]
        _, lane = index_pair(mine.shape)
        lane = lane + t * LANES
        mine = jnp.where((lane >= HALF) & (lane < HALF + rows), mine, 0.0)
        loss = loss + mine * mine
    resist_ref[...] = jnp.concatenate(resists, axis=1).T[HALF : HALF + rows]
    copy = pltpu.make_async_copy(resist_ref, resist_hbm, sem)
    copy.start()
    descent_ref[...] = jnp.zeros_like(descent_ref)

    def group(step, carry):
        for unit in range(units):
            kernel = step * units + unit
            products = [
                slope_ref[t]
                * jnp.concatenate(
                    [side_ref[kernel, t, 0:wide], middle_ref[kernel, t], side_ref[kernel, t, wide:]], axis=0
                )
                for t in range(tiles)
            ]
            window = jnp.concatenate(
                [jnp.concatenate(products[:-1], axis=0), jnp.concatenate(products[1:], axis=0)], axis=1
            )
            returned = jnp.dot(window, row_table_ref[kernel], preferred_element_type=F32).astype(BF16)
            at = unit * 2 * span
            for t in range(tiles - 1):
                to = slice(t * LANES, (t + 1) * LANES)
                for part in range(2):
                    piece = returned[t * span : (t + 1) * span, part * LANES : (part + 1) * LANES]
                    source_ref[at + part * cols : at + (part + 1) * cols, to] = piece[0:cols]
                    tail = at + 2 * cols + part * wide
                    source_ref[tail : tail + wide, to] = piece[cols:]
            if unit % CHUNK == CHUNK - 1:
                chunk = slice((unit + 1 - CHUNK) * 2 * span, (unit + 1) * 2 * span)
                descent_ref[...] += jnp.dot(
                    col_table_ref[step * (units // CHUNK) + unit // CHUNK], source_ref[chunk, :], preferred_element_type=F32
                )
        return carry

    lax.fori_loop(0, kernels // units, group, 0)
    mask = jax.nn.sigmoid(mask_slope * params_ref[...])
    gradient = descent_ref[...].T * mask_slope * mask * (1.0 - mask)
    gradient_ref[...] = gradient
    sums_ref[0:1, :] = jnp.broadcast_to(jnp.sum(gradient * gradient), (1, LANES))
    sums_ref[1:2, :] = jnp.broadcast_to(jnp.sum(loss), (1, LANES))
    copy.wait()


def finish_kernel(params_ref, gradient_ref, sums_ref, new_ref, loss_ref, *, count):
    mean = sums_ref[...] * (1.0 / count)
    scale = step_length / jnp.sqrt(mean[0:1] + norm_eps)
    new_ref[...] = params_ref[...] - gradient_ref[...] * scale
    loss_ref[...] = mean[1:2]


def shards(mask_params, target, col_taps, row_taps, kernel_weights):
    rows, cols = target.shape
    kernels, _, taps = col_taps.shape
    wide = 2 * HALF
    tiles = rows // LANES + 1
    long, span = tiles * LANES, cols + wide
    back_units = BACKWARD_UNROLL
    if cols != LANES or rows % LANES or taps != wide + 1 or kernels % back_units:
        raise ValueError("block shape")
    vmem = pl.BlockSpec(memory_space=pltpu.VMEM)
    hbm = pl.BlockSpec(memory_space=pltpu.HBM)
    array = jax.ShapeDtypeStruct

    def call(body, name, specs, outs, out_specs=None, scratch=(), grant=4 * 2**20, flops=10**6):
        return pl.pallas_call(
            body,
            in_specs=specs,
            out_shape=outs,
            out_specs=[vmem] * len(outs) if out_specs is None else out_specs,
            scratch_shapes=scratch,
            compiler_params=pltpu.CompilerParams(vmem_limit_bytes=grant),
            cost_estimate=pl.CostEstimate(flops=flops, bytes_accessed=10**6, transcendentals=0),
            name=name,
        )

    plain, edge = array((rows, cols), BF16), array((wide + HALF, cols), BF16)
    full = array((rows, cols), F32)
    sides, strips = lax.axis_size("col"), lax.axis_size("strip")
    mine, goal = stay(mask_params[0]), stay(target)
    ahead, behind = call(
        edges_kernel,
        "edges",
        [hbm, hbm],
        (edge, edge),
        scratch=[
            pltpu.VMEM((2, wide, cols), F32),
            pltpu.VMEM((2, HALF, cols), target.dtype),
            pltpu.SemaphoreType.DMA((2, 2)),
        ],
    )(mine, goal)
    from_behind = lax.ppermute(ahead, ("tiles", "strip"), snake(1))
    from_ahead = lax.ppermute(behind, ("tiles", "strip"), snake(-1))
    masks = pltpu.VMEM((4, LANES, LANES), BF16)
    row_tables = array((kernels, 4 * LANES, 2 * LANES), BF16)
    params, mask_half, code, *tables = call(
        load_kernel,
        "load",
        [hbm] * 5,
        (full, plain, plain, array((kernels, 8, 2 * LANES), F32), array((kernels * 2 * wide, LANES), BF16), row_tables),
        scratch=[
            pltpu.VMEM((rows, cols), target.dtype),
            pltpu.SMEM(kernel_weights.shape, F32),
            pltpu.VMEM(col_taps.shape, BF16),
            pltpu.VMEM(row_taps.shape, BF16),
            pltpu.VMEM((4 * kernels, taps), F32),
            masks,
            pltpu.SemaphoreType.DMA((5,)),
        ],
        flops=10**8,
    )(mine, goal, stay(kernel_weights), stay(col_taps), stay(row_taps))

    side, turned = array((wide + HALF, long), BF16), array((cols, long), BF16)
    centre, code_turned, *messages = call(
        assemble_kernel,
        "assemble",
        [vmem] * 4,
        (turned, turned) + (side,) * (1 if sides == 2 else 2),
    )(mask_half, code, from_behind, from_ahead)
    if sides == 2:
        before = after = lax.ppermute(messages[0], "col", ring("col", 1))
    else:
        before = lax.ppermute(messages[0], "col", ring("col", 1))
        after = lax.ppermute(messages[1], "col", ring("col", -1))

    def part(width):
        fields = array((kernels, tiles, width, 2 * LANES), BF16)
        columns = pltpu.VMEM((kernels, tiles * width, 2 * LANES), BF16)
        return fields, pltpu.VMEM((tiles, width, 2 * LANES), F32), columns

    fields, total, columns = part(wide)
    middle, middle_intensity = call(
        middle_kernel,
        "middle",
        [vmem] * 4,
        (fields, array((tiles, wide, LANES), F32)),
        scratch=[total, columns],
        grant=VMEM,
        flops=4 * 10**9,
    )(centre, *tables)
    plane = (tiles, span, LANES)
    fields, total, columns = part(2 * wide)
    sides_field, intensity = call(
        side_kernel,
        "side",
        [vmem] * 7,
        (fields, array(plane, F32)),
        scratch=[total, pltpu.VMEM((LANES, 2 * long), BF16), columns],
        grant=VMEM,
    )(centre, before, after, middle_intensity, *tables)

    other = lax.ppermute(intensity, "expo", [(0, 1), (1, 0)])
    row_table, col_table, goal, factor = call(
        back_tables_kernel,
        "back_tables",
        [vmem] * 4 + [pl.BlockSpec(memory_space=pl.ANY)],
        (
            row_tables,
            array((kernels // CHUNK, cols, CHUNK * 2 * span), BF16),
            array(plane, F32),
            array(plane, F32),
        ),
        scratch=[masks],
        flops=10**9,
    )(tables[0], code_turned, before, after, intensity)

    gradient, resist, sums = call(
        backward_kernel,
        "backward",
        [vmem] * 9,
        (full, full, array((2, LANES), F32)),
        out_specs=[vmem, hbm, vmem],
        scratch=[
            pltpu.VMEM((tiles, span, 2 * LANES), BF16),
            pltpu.VMEM((cols, rows), F32),
            pltpu.VMEM((rows, cols), F32),
            pltpu.VMEM((back_units * 2 * span, rows), BF16),
            pltpu.SemaphoreType.DMA,
        ],
        grant=VMEM,
    )(intensity, other, goal, factor, params, middle, sides_field, row_table, col_table)

    sums = sums + lax.ppermute(sums, "expo", [(0, 1), (1, 0)])
    for axis in ("col", "strip"):
        sums = total_over(sums, axis)
    count = 2 * rows * cols * strips * sides
    new_params, loss = call(
        functools.partial(finish_kernel, count=count), "finish", [vmem] * 3, (full, array((1, LANES), F32))
    )(params, gradient, sums)
    return (new_params[None], resist, loss[0, 0:1])


def solution(mesh):
    if mesh.shape["expo"] != 2:
        raise ValueError("two exposures")
    return jax.shard_map(
        shards,
        mesh=mesh,
        in_specs=(
            P("expo", ("tiles", "strip"), "col"),
            P(("tiles", "strip"), "col"),
            P(),
            P(),
            P(),
        ),
        out_specs=(P("expo", ("tiles", "strip"), "col"), P(("tiles", "strip"), "col"), P("tiles")),
        check_vma=False,
    )
```
